32 devices in a mesh: groups: 2 (over y), row: 8 (over z, x), col: 2 (over core).
Axes of the slice: x: 2, y: 2, z: 4, core: 2. Of those that a mesh axis runs over, the one named last changes fastest.
Arguments:
- embeddings: bfloat16 [128, 16, 1280], P(('groups', 'row'), 'col'), parts along dimension 0, may hold values from -6 to 52
- pos_embed: bfloat16 [256, 1280], replicated, may hold values from -3 to 3
- ln_gain: float32 [1280], replicated, may hold values from 0.6 to 9
- ln_bias: float32 [1280], replicated, may hold values from -1.5 to 1.5
- w_qkv: bfloat16 [1280, 1920], P(('row', 'col')), may hold values from -0.25155765 to 0.25155765
- b_qkv: float32 [1920], replicated, may hold values from -1.5 to 1.5
- w_out: bfloat16 [1280, 640], P(('row', 'col')), may hold values from -0.25 to 0.25
- b_out: float32 [1280], replicated, may hold values from -1.5 to 1.5
- valid: int32 [16, 2, 256], P(('groups', 'row'), 'col'), parts along dimension 0, may hold values from 0 to 196
Outputs:
- merged: bfloat16 [128, 16, 1280], P(('groups', 'row'), 'col'), parts along dimension 0
The draws below stay inside these ranges and needn't reach their ends.
There are 2 independent parts, one for each index of `groups`. The reference program is written for one: setup_inputs(seed, part) draws one part's arguments, and reference() takes and returns one part's arrays. A program takes and returns all parts, laid end to end along the dimension named above; an argument that names none is the same for every part. Nothing has to cross between parts.
All inputs are finite; a program needn't handle non-finite values.
Results may differ from the reference program's by a relative error of at most 0.0098.
Values may be sent and summed in bfloat16 or wider, within the bound.
A program may use at most 64 MiB of HBM per device.

```python
import jax
import jax.numpy as jnp
from jax import lax

D = 1280
HEADS = 8
HEAD_DIM = 80
TILE = 8
HD = 640
QKV = 1920
WIN = 16
RIM = 4
TOK = 256
TROWS = 8
NPR = 64
NPC = 16
N_COL = 2


def draw_embeddings(key, part):
    first = jax.random.fold_in(key, 0)
    values = jnp.clip(jax.random.normal(first, (NPR, NPC, D), jnp.float32), -6.0, 6.0)
    return values.astype(jnp.bfloat16)


def draw_ln_gain(key, part):
    first = jax.random.fold_in(key, 0)
    base = jax.random.uniform(first, (D,), jnp.float32, 0.6, 1.4)
    return base


def draw_w_qkv(key, part):
    full = jnp.clip(jax.random.normal(key, (D, QKV), jnp.float32), -6.0, 6.0) * D ** (-0.5)
    return full.astype(jnp.bfloat16)


def plant(entries, stream_key, low, high):
    spot = [jax.random.randint(jax.random.fold_in(stream_key, axis), (), 0, length) for axis, length in enumerate(entries.shape)]
    widest = entries.shape.index(max(entries.shape))
    beside = spot[:widest] + [(spot[widest] + 1) % entries.shape[widest]] + spot[widest + 1:]
    return entries.at[tuple(spot)].set(low).at[tuple(beside)].set(high)


def level_of(stream_key, shape, cuts, least, top_value):
    loudness, own = 1.0, jax.random.fold_in(stream_key, 6)
    for axis_at, parts in cuts:
        heights = jnp.exp(jax.random.uniform(jax.random.fold_in(own, axis_at), (parts,), jnp.float32, least / len(cuts), top_value / len(cuts)))
        loudness = loudness * jnp.repeat(heights, shape[axis_at] // parts).reshape([-1 if axis == axis_at else 1 for axis in range(len(shape))])
    return loudness


def bell_draw(key, extent, spread, limit, cuts=(), held_as=jnp.bfloat16):
    entries = spread * jax.random.normal(key, extent, jnp.float32)
    if cuts:
        entries = entries * level_of(key, extent, cuts, -0.22, 0.18)
    return jnp.clip(entries, -limit, limit).astype(held_as)


def setup_inputs(seed: int = 0, part: int = 0) -> dict:
    key_list = jax.random.split(jax.random.key(seed), 10)
    own_keys = jax.random.split(jax.random.fold_in(key_list[9], part), 10)
    embeddings = draw_embeddings(jax.random.fold_in(jax.random.fold_in(key_list[9], part), 71), part)
    pos_embed = bell_draw(key_list[1], (TOK, D), 0.5, 3.0)
    ln_gain = draw_ln_gain(jax.random.fold_in(key_list[9], 71), part)
    ln_bias = bell_draw(key_list[3], (D,), 0.3, 1.5, (), jnp.float32)
    w_qkv = draw_w_qkv(jax.random.fold_in(key_list[9], 71), part)
    b_qkv = bell_draw(key_list[5], (QKV,), 0.3, 1.5, (), jnp.float32)
    w_out = bell_draw(key_list[6], (D, HD), HD ** -0.5, 0.25, ((0, 16),))
    b_out = bell_draw(key_list[7], (D,), 0.3, 1.5, (), jnp.float32)
    valid = plant(jax.random.randint(own_keys[8], (TROWS, N_COL, TOK), 0, 197), jax.random.fold_in(own_keys[8], 1), 0, 196).astype(jnp.int32)
    return dict(embeddings=embeddings, pos_embed=pos_embed, ln_gain=ln_gain, ln_bias=ln_bias, w_qkv=w_qkv, b_qkv=b_qkv, w_out=w_out, b_out=b_out, valid=valid)


EPSILON = 1e-06
SPREAD = 4.0
FLOOR = 0.25

def layer_norm(inputs, ln_gain, ln_bias):
    centred = inputs - lax.optimization_barrier(jnp.mean(inputs, axis=-1, keepdims=True))
    variance = lax.optimization_barrier(jnp.mean(centred * centred, axis=-1, keepdims=True))
    return centred * lax.rsqrt(variance + EPSILON) * ln_gain + ln_bias

def gauss_table(win):
    offsets = jnp.arange(win, dtype=jnp.float32) - (win - 1) / 2.0
    squared = offsets[:, None] * offsets[:, None] + offsets[None, :] * offsets[None, :]
    return jnp.exp(-squared / (2.0 * SPREAD * SPREAD))

def attend(projected):
    rows_count = projected.shape[0]
    queries = projected[:, :HD].reshape(rows_count, HEADS, HEAD_DIM).astype(jnp.float32)
    keys = projected[:, HD:2 * HD].reshape(rows_count, HEADS, HEAD_DIM).astype(jnp.float32)
    values = projected[:, 2 * HD:].reshape(rows_count, HEADS, HEAD_DIM).astype(jnp.float32)
    scores = jnp.einsum('qhd,khd->hqk', queries, keys) * HEAD_DIM ** (-0.5)
    highest = lax.optimization_barrier(jnp.max(scores, axis=-1, keepdims=True))
    expon = jnp.exp(scores - highest)
    probs = (expon / lax.optimization_barrier(jnp.sum(expon, axis=-1, keepdims=True))).astype(jnp.bfloat16)
    mixed = jnp.einsum('hqk,khd->qhd', probs.astype(jnp.float32), values)
    return mixed.astype(jnp.bfloat16).reshape(rows_count, HD)

def reference(embeddings, pos_embed, ln_gain, ln_bias, w_qkv, b_qkv, w_out, b_out, valid):
    padded = jnp.pad(embeddings, ((RIM, RIM), (RIM, RIM), (0, 0)))
    gauss = gauss_table(WIN).reshape(TOK)
    zero_index = jnp.zeros((), jnp.int32)

    def one_window(carry, index):
        numer, denom = carry
        row_at = (index // N_COL).astype(jnp.int32)
        col_at = (index % N_COL).astype(jnp.int32)
        patch = lax.dynamic_slice(padded, (row_at * TILE, col_at * TILE, zero_index), (WIN, WIN, D))
        inputs = patch.reshape(TOK, D).astype(jnp.float32) + pos_embed.astype(jnp.float32)
        normed = layer_norm(inputs, ln_gain, ln_bias).astype(jnp.bfloat16)
        projected = (jnp.dot(normed, w_qkv, preferred_element_type=jnp.float32) + b_qkv).astype(jnp.bfloat16)
        attended = attend(projected)
        hidden = inputs + jnp.dot(attended, w_out.T, preferred_element_type=jnp.float32) + b_out
        counts = lax.dynamic_slice(valid, (row_at, col_at, zero_index), (1, 1, TOK)).reshape(TOK)
        weight = gauss * counts.astype(jnp.float32) / 196.0
        add_numer = (weight[:, None] * hidden).reshape(WIN, WIN, D)
        add_denom = weight.reshape(WIN, WIN)
        start = (row_at * TILE, col_at * TILE, zero_index)
        numer = lax.dynamic_update_slice(numer, lax.dynamic_slice(numer, start, (WIN, WIN, D)) + add_numer, start)
        dstart = (row_at * TILE, col_at * TILE)
        denom = lax.dynamic_update_slice(denom, lax.dynamic_slice(denom, dstart, (WIN, WIN)) + add_denom, dstart)
        return ((numer, denom), None)
    init = (jnp.zeros((NPR + 2 * RIM, NPC + 2 * RIM, D), jnp.float32), jnp.zeros((NPR + 2 * RIM, NPC + 2 * RIM), jnp.float32))
    (numer, denom), _ = lax.scan(one_window, init, jnp.arange(TROWS * N_COL, dtype=jnp.int32))
    numer = numer[RIM:RIM + NPR, RIM:RIM + NPC]
    denom = denom[RIM:RIM + NPR, RIM:RIM + NPC]
    return (numer / jnp.maximum(denom, FLOOR)[:, :, None]).astype(jnp.bfloat16)
```

```python
import functools

import jax
import jax.numpy as jnp
from jax import lax
from jax.experimental import pallas as pl
from jax.experimental.pallas import tpu as pltpu
from jax.sharding import PartitionSpec as P

HEADS = 8
EPSILON = 1e-06
SPREAD = 4.0
FLOOR = 0.25
LANES = 128
MESH = pl.DeviceIdType.MESH


def kernel(
    rows,
    emb_ref, pos_hbm, gain_hbm, bias_hbm, wq_ref, bq_hbm, wo_ref, bo_hbm, valid_ref,
    out_ref, pos_ref, gain_ref, bias_ref, bq_ref, bo_ref, wq_own,
    eb, vb, pack, wq_all, wo_all, nrm, posr, base, wcol, tiles_out, tiles_in,
    rims_out, rims_in, send_sems, recv_sems, local_sems,
):
    g, r, c = lax.axis_index("groups"), lax.axis_index("row"), lax.axis_index("col")
    tile, _, width = emb_ref.shape
    rim = tile // 2
    win = 2 * tile
    tok = win * win
    shard, qkv = wq_ref.shape
    hd = wo_ref.shape[1]
    head = hd // HEADS
    team = 4
    part = hd // team
    packed = pack.shape[2]
    x, z = r % 2, r // 2
    planes = rows // 2
    away = {1: z + 1 - 2 * (z % 2), 2: (z + 2) % planes, 3: planes - 1 - z}
    inner = jnp.logical_and(z > 0, z < planes - 1)
    rx, other = r + 1 - 2 * x, 1 - c
    q = 2 * x + c
    above, below = lax.rem(r + rows - 1, rows), lax.rem(r + 1, rows)
    has_above, has_below = r > 0, r < rows - 1
    has_up, has_down = z > 0, z < planes - 1
    outside = jnp.logical_and(has_above, has_below)
    facing = jnp.where(x == 0, above, below)
    to_core, to_y = (g, r, other), (1 - g, r, c)
    core = {0: c, 1: other}

    names = {}
    pending = []
    fold_base, rim_base = 0, team

    def copy(name, src, dst, device, recv=None):
        at = names.setdefault(name, len(names) + 2 * team)
        return pltpu.make_async_remote_copy(
            src_ref=src, dst_ref=dst, send_sem=send_sems.at[at],
            recv_sem=recv_sems.at[at if recv is None else recv],
            device_id=device, device_id_type=MESH,
        )

    def start(name, src, dst, device, when=None, recv=None):
        item = copy(name, src, dst, device, recv)
        pending.append((when, item))
        if when is None:
            item.start()
        else:
            pl.when(when)(item.start)

    def arrived(name, dst, when=None, recv=None):
        item = copy(name, dst, dst, to_core, recv)
        if when is None:
            item.wait_recv()
        else:
            pl.when(when)(item.wait_recv)

    own_rows, mate_rows = pl.ds(rim + tile * x, tile), pl.ds(rim + tile * (1 - x), tile)
    top_rows, low_rows = pl.ds(0, rim), pl.ds(rim + 2 * tile, rim)
    locals_ = []
    for src, dst in (
        (wq_ref, wq_own), (pos_hbm, pos_ref), (gain_hbm, gain_ref), (bias_hbm, bias_ref),
        (emb_ref, eb.at[c, own_rows]), (valid_ref, vb.at[1]), (bo_hbm, bo_ref), (bq_hbm, bq_ref),
        (wo_ref, wo_all.at[r, c]),
    ):
        item = pltpu.make_async_copy(src, dst, local_sems.at[len(locals_)])
        item.start()
        locals_.append(item)

    barrier = pltpu.get_barrier_semaphore()

    def greet(*device):
        pl.semaphore_signal(barrier, inc=1, device_id=device, device_id_type=MESH)

    for k in (2, 1):
        greet(g, 2 * away[k] + x, c)
        greet(g, 2 * away[k] + x, other)

    @pl.when(inner)
    def _():
        greet(g, 2 * away[3] + x, c)
        greet(g, 2 * away[3] + x, other)

    @pl.when(outside)
    def _():
        greet(g, facing, c)
        greet(g, facing, other)

    greet(1 - g, rx, c)
    greet(1 - g, r, c)
    greet(g, rx, c)
    greet(g, rx, other)
    greet(g, r, other)

    locals_[0].wait()
    own = wq_own[...].astype(jnp.float32)
    for k in range(team):
        cut = [own[:, t * hd + k * part:t * hd + (k + 1) * part] for t in range(3)]
        for t in range(3):
            pack[k, :, t * LANES:(t + 1) * LANES] = cut[t][:, :LANES].astype(jnp.bfloat16)
        rest = part - LANES
        pieces = [item[:, LANES:] for item in cut] + [jnp.zeros((shard, LANES - 3 * rest), jnp.float32)]
        pack[k, :, 3 * LANES:] = jnp.concatenate(pieces, axis=1).astype(jnp.bfloat16)

    pl.semaphore_wait(
        barrier, 9 + 2 * inner.astype(jnp.int32) + 2 * outside.astype(jnp.int32)
    )

    half_w = packed // 2
    mine = pl.ds(pl.multiple_of(g * half_w, LANES), half_w)
    theirs = pl.ds(pl.multiple_of((1 - g) * half_w, LANES), half_w)

    def wq_at(row, core_at, cols):
        return wq_all.at[row, core_at, :, cols]

    def reach(k):
        return None if k < 3 else inner

    for a in (0, 1):
        start(f"xm{a}", pack.at[2 * (1 - x) + core[a], :, mine], wq_at(r, c, mine), (g, rx, core[a]))
    for k in (1, 2, 3):
        for a in (0, 1):
            start(f"A{k}{a}", pack.at[2 * x + core[a], :, mine], wq_at(r, c, mine),
                  (g, 2 * away[k] + x, core[a]), reach(k))
    start("ec", emb_ref, eb.at[c, own_rows], to_core)
    start("ex", emb_ref, eb.at[c, own_rows], (g, rx, c))
    start("wc", pack.at[2 * x + other], wq_all.at[r, c], to_core)

    count_down = [copy("v0", valid_ref, vb.at[0], (g, below, c)), copy("v3", valid_ref, vb.at[3], (g, below, other))]
    count_up = [copy("v2", valid_ref, vb.at[2], (g, above, c)), copy("v5", valid_ref, vb.at[5], (g, above, other))]

    @pl.when(has_below)
    def _():
        for item in count_down:
            item.start()

    @pl.when(has_above)
    def _():
        for item in count_up:
            item.start()

    start("v4", valid_ref, vb.at[4], to_core)
    gives_down = jnp.logical_and(x == 1, has_down)
    gives_up = jnp.logical_and(x == 0, has_up)
    for name, row in (("ht", lax.rem(r + 2, rows)), ("hto", below)):
        start(name, emb_ref.at[pl.ds(tile - rim, rim)], eb.at[c, top_rows], (g, row, c), gives_down,
              names.setdefault("ht", len(names) + 2 * team))
    for name, row in (("hb", lax.rem(r + rows - 2, rows)), ("hbo", above)):
        start(name, emb_ref.at[pl.ds(0, rim)], eb.at[c, low_rows], (g, row, c), gives_up,
              names.setdefault("hb", len(names) + 2 * team))
    own_weights = pltpu.make_async_copy(pack.at[q], wq_all.at[r, c], local_sems.at[len(locals_)])
    own_weights.start()

    @pl.when(z == 0)
    def _():
        eb[0, 0:rim] = jnp.zeros((rim, tile, width), eb.dtype)
        eb[1, 0:rim] = jnp.zeros((rim, tile, width), eb.dtype)

    @pl.when(z == planes - 1)
    def _():
        eb[0, rim + 2 * tile:] = jnp.zeros((rim, tile, width), eb.dtype)
        eb[1, rim + 2 * tile:] = jnp.zeros((rim, tile, width), eb.dtype)

    @pl.when(r == 0)
    def _():
        vb[0] = jnp.zeros((1, 1, tok), vb.dtype)
        vb[3] = jnp.zeros((1, 1, tok), vb.dtype)

    @pl.when(r == rows - 1)
    def _():
        vb[2] = jnp.zeros((1, 1, tok), vb.dtype)
        vb[5] = jnp.zeros((1, 1, tok), vb.dtype)

    @pl.when(jnp.logical_not(outside))
    def _():
        rims_in[...] = jnp.zeros(rims_in.shape, rims_in.dtype)

    for item in locals_[1:5]:
        item.wait()
    gain, bias = gain_ref[...].reshape(1, width), bias_ref[...].reshape(1, width)
    per = rim

    def roll_block(block, carry):
        pos = pos_ref[pl.ds(pl.multiple_of(block * per * win, per * win), per * win)]
        pos = pos.astype(jnp.float32).reshape(per, win, width)
        posr[pl.ds(block * per, per)] = pltpu.roll(pos, win - rim, 1)
        return carry

    lax.fori_loop(0, win // per, roll_block, 0)
    place = lax.broadcasted_iota(jnp.int32, (per, tile, 1), 1)

    def norm_block(which, block, side):
        which = which + x * (1 - 2 * which)
        block = block + x * (win // per - 1 - 2 * block)
        at = pl.ds(which * tile + block * per, per)
        rim_ok = jnp.where(side == 0, place, tile - 1 - place) < rim
        left = eb[side, at].astype(jnp.float32)
        right = jnp.where(rim_ok, eb[1 - side, at].astype(jnp.float32), 0.0)
        v = (jnp.concatenate([left, right], axis=1) + posr[pl.ds(block * per, per)]).reshape(per * win, width)
        v = v - jnp.mean(v, axis=-1, keepdims=True)
        variance = jnp.mean(v * v, axis=-1, keepdims=True)
        v = v * lax.rsqrt(variance + EPSILON) * gain + bias
        there = pl.ds(pl.multiple_of(block * per * win, per * win), per * win)
        nrm[2 * which + side, there] = v.astype(jnp.bfloat16)

    def norm_own(n, carry):
        m = n // 2
        norm_block(m // 2, (m + 1) % 3, n % 2)
        return carry

    def norm_mate(n, carry):
        m = n // 2
        norm_block((m + 1) // 2, (m + 2) % 3 + 1, n % 2)
        return carry

    def norm_rims(n, carry):
        norm_block(n // 2, n // 2 * 3, n % 2)
        return carry

    def from_z(phase, k):
        row = 2 * away[k] + (x if phase == "A" else 1 - x)
        for a in (0, 1):
            here = wq_at(row, core[a], mine)
            arrived(f"{phase}{k}{a}", here)
            start(f"y{phase}{k}{a}", here, here, to_y)
            if k == 2:
                start(f"f{phase}{a}", here, here, (g, 2 * away[1] + x, c), inner,
                      names.setdefault(f"{phase}3{a}", len(names) + 2 * team))

    def from_y(phase, k):
        row = 2 * away[k] + (x if phase == "A" else 1 - x)
        for a in (0, 1):
            arrived(f"y{phase}{k}{a}", wq_at(row, core[a], theirs))

    arrived("ec", eb.at[other, own_rows])
    lax.fori_loop(0, 6, norm_own, 0)

    for a in (0, 1):
        here = wq_at(rx, core[a], mine)
        arrived(f"xm{a}", here)
        for k in (1, 2, 3):
            start(f"B{k}{a}", here, here, (g, 2 * away[k] + x, c), reach(k))

    for a in (0, 1):
        start(f"xt{a}", pack.at[2 * (1 - x) + core[a], :, theirs], wq_at(r, c, theirs), (g, rx, core[a]))
    start("ox", wo_ref, wo_all.at[r, c], (g, rx, c))
    start("oc", wo_ref, wo_all.at[r, c], to_core)
    units = hd // LANES
    side_w = units // 2 * LANES
    ring_w = hd - side_w
    ring = pl.ds(pl.multiple_of(g * side_w, LANES), ring_w)
    y_out = pl.ds(pl.multiple_of(g * ring_w, LANES), side_w)
    y_in = pl.ds(pl.multiple_of((1 - g) * ring_w, LANES), side_w)

    def wo_at(row, cols):
        return wo_all.at[row, c, :, cols]


    from_z("A", 1)
    arrived("ex", eb.at[c, mate_rows])
    start("exf", eb.at[c, mate_rows], eb.at[c, mate_rows], to_core)
    from_z("A", 2)

    arrived("v4", vb.at[4])

    @pl.when(has_above)
    def _():
        for item in count_down:
            item.wait_recv()

    @pl.when(has_below)
    def _():
        for item in count_up:
            item.wait_recv()

    for item in locals_[5:]:
        item.wait()
    near_v = [vb[k, 0] for k in range(3)]
    far_v = [vb[k + 3, 0] for k in range(3)]
    mate_near, mate_far = jnp.where(x == 0, near_v[2], near_v[0]), jnp.where(x == 0, far_v[2], far_v[0])
    counts = near_v + far_v
    for i in (0, 1):
        for side in (0, 1):
            same = jnp.where(c == side, near_v[1], far_v[1])
            mate = jnp.where(c == side, mate_near, mate_far)
            counts.append(jnp.where(x == i, same, mate))
    counts = jnp.concatenate(
        [v.astype(jnp.float32) for v in counts] + [jnp.zeros((6, tok), jnp.float32)], axis=0
    ).astype(jnp.bfloat16)
    t_row = lax.broadcasted_iota(jnp.int32, (tok, tok), 0)
    t_col = lax.broadcasted_iota(jnp.int32, (tok, tok), 1)
    base_row = t_row // win * win
    pick = (t_col == base_row + (t_row - base_row + rim) % win).astype(jnp.float32).astype(jnp.bfloat16)
    counts = lax.dot_general(pick, counts, (((1,), (1,)), ((), ())), preferred_element_type=jnp.float32)
    t = lax.broadcasted_iota(jnp.int32, (tok, 1), 0)
    oi = (t // win).astype(jnp.float32) - (win - 1) / 2.0
    oj = ((t % win + rim) % win).astype(jnp.float32) - (win - 1) / 2.0
    gauss = jnp.exp(-(oi * oi + oj * oj) / (2.0 * SPREAD * SPREAD))
    weights = gauss * counts / 196.0
    at_col = lax.broadcasted_iota(jnp.int32, weights.shape, 1) % 2
    at_place = lax.broadcasted_iota(jnp.int32, weights.shape, 0) % win - tile
    kept = jnp.where(at_col == 0, at_place, tile - 1 - at_place) < rim
    wcol[...] = jnp.where(jnp.logical_or(at_place < 0, kept), weights, 0.0)
    grid = weights.reshape(win, win, weights.shape[1])
    near = grid[:, :tile].reshape(win * tile, weights.shape[1])
    far = grid[:, tile:].reshape(win * tile, weights.shape[1])
    u = lax.broadcasted_iota(jnp.int32, (win * tile, 1), 0) % tile
    fold_ok = jnp.where(c == 1, u, tile - 1 - u) < rim
    far = jnp.where(fold_ok, far, 0.0)
    low, high = rim * tile, (rim + tile) * tile
    near0, far0 = near[low:high, 1:2], far[low:high, 4:5]
    near_a = jnp.where(has_above, near[high:, 0:1], 0.0)
    far_a = jnp.where(has_above, far[high:, 3:4], 0.0)
    near_b = jnp.where(has_below, near[:low, 2:3], 0.0)
    far_b = jnp.where(has_below, far[:low, 5:6], 0.0)
    denom = near0 + far0 + jnp.concatenate([near_a + far_a, near_b + far_b], axis=0)

    def flat(lo, hi, a, b):
        return posr[lo:hi, a:b].reshape((hi - lo) * (b - a), width)

    total = denom * (
        eb[c, own_rows].astype(jnp.float32).reshape(tile * tile, width)
        + bo_ref[...].reshape(1, width)
    )
    total += near0 * flat(rim, rim + tile, 0, tile) + far0 * flat(rim, rim + tile, tile, win)
    base[...] = total
    base[0:low] += near_a * flat(rim + tile, win, 0, tile) + far_a * flat(rim + tile, win, tile, win)
    base[low:] += near_b * flat(0, rim, 0, tile) + far_b * flat(0, rim, tile, win)

    arrived("exf", eb.at[other, mate_rows])
    from_z("A", 3)
    lax.fori_loop(0, 6, norm_mate, 0)
    for name, place_at, when in (("ht", top_rows, has_up), ("hb", low_rows, has_down)):
        arrived(name, eb.at[c, place_at], when)
        start(f"{name}f", eb.at[c, place_at], eb.at[c, place_at], to_core, when)
    from_z("B", 1)
    for k in (1, 2, 3):
        start(f"o{k}", wo_ref.at[:, ring], wo_at(r, ring), (g, 2 * away[k] + x, c), reach(k))
    from_z("B", 2)
    for name, place_at, when in (("ht", top_rows, has_up), ("hb", low_rows, has_down)):
        arrived(f"{name}f", eb.at[other, place_at], when)
    lax.fori_loop(0, 4, norm_rims, 0)
    from_z("B", 3)
    arrived("ox", wo_at(rx, pl.ds(0, hd)))
    start("oxf", wo_all.at[rx, c], wo_all.at[rx, c], to_core)

    def out_from_z(k):
        here, side = wo_at(2 * away[k] + x, ring), wo_at(2 * away[k] + x, y_out)
        arrived(f"o{k}", here)
        start(f"ox{k}", here, here, (g, rx, c))
        start(f"oy{k}", side, side, to_y)
        start(f"od{k}", side, side, (1 - g, rx, c))
        if k == 2:
            start("of", here, here, (g, 2 * away[1] + x, c), inner, names.setdefault("o3", len(names) + 2 * team))

    def out_to_core(k):
        row, mate = 2 * away[k] + x, 2 * away[k] + 1 - x
        arrived(f"oy{k}", wo_at(row, y_in))
        start(f"oc{k}", wo_all.at[row, c], wo_all.at[row, c], to_core)
        arrived(f"ox{k}", wo_at(mate, ring))
        arrived(f"od{k}", wo_at(mate, y_in))
        start(f"om{k}", wo_all.at[mate, c], wo_all.at[mate, c], to_core)

    for k in (1, 2):
        out_from_z(k)
    own_weights.wait()
    arrived("wc", wq_all.at[r, other])
    for a in (0, 1):
        arrived(f"xt{a}", wq_at(rx, core[a], theirs))
    for phase in ("A", "B"):
        for k in (1, 2, 3):
            from_y(phase, k)

    b_own = bq_ref[...].reshape(1, qkv)
    b_parts = []
    for k in range(team):
        cut = [b_own[:, t * hd + k * part:t * hd + (k + 1) * part] for t in range(3)]
        rest = part - LANES
        b_parts.append(jnp.concatenate(
            [item[:, :LANES] for item in cut] + [item[:, LANES:] for item in cut]
            + [jnp.zeros((1, LANES - 3 * rest), jnp.float32)], axis=1))
    b_mine = jnp.where(x == 0, jnp.where(c == 0, b_parts[0], b_parts[1]), jnp.where(c == 0, b_parts[2], b_parts[3]))
    lane = lax.broadcasted_iota(jnp.int32, (1, 2 * LANES), 1)
    rest = part - LANES

    def attend(w):
        proj = jnp.dot(nrm[w], wq_all[...].reshape(width, packed), preferred_element_type=jnp.float32) + b_mine
        tail = proj[:, 3 * LANES:]
        queries = jnp.concatenate([proj[:, :LANES], tail], axis=1)
        keys = jnp.concatenate([proj[:, LANES:2 * LANES], pltpu.roll(tail, LANES - rest, 1)], axis=1)
        values = jnp.concatenate([proj[:, 2 * LANES:3 * LANES], pltpu.roll(tail, LANES - 2 * rest, 1)], axis=1)
        keys, values = keys.astype(jnp.bfloat16), values.astype(jnp.bfloat16)
        outs = []
        for h in range(HEADS // team):
            inside = jnp.logical_and(lane >= h * head, lane < (h + 1) * head)
            used = -(-(h + 1) * head // LANES) * LANES
            chosen = jnp.where(inside, queries, 0.0).astype(jnp.bfloat16)
            scores = lax.dot_general(
                chosen[:, :used], keys[:, :used], (((1,), (1,)), ((), ())), preferred_element_type=jnp.float32
            ) * head ** (-0.5)
            expon = jnp.exp(scores - jnp.max(scores, axis=-1, keepdims=True))
            probs = (expon / jnp.sum(expon, axis=-1, keepdims=True)).astype(jnp.bfloat16)
            outs.append(jnp.dot(probs, values, preferred_element_type=jnp.float32))
        mixed = jnp.where(lane < head, outs[0], jnp.where(lane < part, outs[1], 0.0))
        mixed = mixed.astype(jnp.bfloat16).astype(jnp.float32) * wcol[:, 6 + w:7 + w]
        return mixed.reshape(win, win, 2 * LANES)

    def flatten(value):
        return value.reshape(value.shape[0] * tile, 2 * LANES)

    def both(i):
        left, right = attend(2 * i), attend(2 * i + 1)
        return [left[:, :tile] + right[:, tile:], right[:, :tile] + left[:, tile:]]

    upper = both(0)
    for side in (0, 1):
        rims_out[0, side] = flatten(upper[side][:rim]).astype(jnp.bfloat16)
    for side in (0, 1):
        start(f"rt{side}", rims_out.at[0, side], rims_in.at[q], (g, lax.rem(2 * z + rows - 1, rows), side), has_up,
              rim_base + q)
    out_from_z(3)
    lower = both(1)
    for side in (0, 1):
        rims_out[1, side] = flatten(lower[side][rim + tile:]).astype(jnp.bfloat16)
    for side in (0, 1):
        start(f"rb{side}", rims_out.at[1, side], rims_in.at[q], (g, lax.rem(2 * z + 2, rows), side), has_down,
              rim_base + q)
    for side in (0, 1):
        first = jnp.concatenate([upper[side][rim:tile], upper[side][tile:rim + tile] + lower[side][:rim]], axis=0)
        second = jnp.concatenate([lower[side][rim:tile] + upper[side][rim + tile:], lower[side][tile:rim + tile]], axis=0)
        tiles_out[0, side] = flatten(first).astype(jnp.bfloat16)
        tiles_out[1, side] = flatten(second).astype(jnp.bfloat16)
    start("fx", tiles_out.at[1 - x, c], tiles_in.at[q], (g, rx, c), None, fold_base + q)
    start("fd", tiles_out.at[1 - x, other], tiles_in.at[q], (g, rx, other), None, fold_base + q)
    start("fc", tiles_out.at[x, other], tiles_in.at[q], to_core, None, fold_base + q)
    tiles_in[q] = tiles_out[x, c]

    for k in (1, 2, 3):
        out_to_core(k)
    arrived("oc", wo_all.at[r, other])
    arrived("oxf", wo_all.at[rx, other])
    for k in (1, 2, 3):
        arrived(f"oc{k}", wo_all.at[2 * away[k] + x, other])
        arrived(f"om{k}", wo_all.at[2 * away[k] + 1 - x, other])

    for at in (2 * x + other, 2 * (1 - x) + c, 2 * (1 - x) + other):
        arrived("fc", tiles_in.at[at], None, fold_base + at)
    for at in range(team):
        arrived("fc", rims_in.at[at], outside, rim_base + at)

    sums = []
    for at in range(team):
        edge = rims_in[at].astype(jnp.float32)
        edge = jnp.concatenate([jnp.where(x == 0, edge, 0.0), jnp.where(x == 1, edge, 0.0)], axis=0)
        sums.append((tiles_in[at].astype(jnp.float32) + edge)[:, :part])
    merged = jnp.concatenate(sums, axis=1).astype(jnp.bfloat16)
    result = base[...] + lax.dot_general(
        merged, wo_all[...].reshape(width, hd), (((1,), (1,)), ((), ())), preferred_element_type=jnp.float32,
    )
    result = result / jnp.maximum(denom, FLOOR)
    out_ref[...] = result.reshape(tile, tile, width).astype(out_ref.dtype)

    for when, item in pending:
        if when is None:
            item.wait_send()
        else:
            pl.when(when)(item.wait_send)

    @pl.when(has_above)
    def _():
        for item in count_up:
            item.wait_send()

    @pl.when(has_below)
    def _():
        for item in count_down:
            item.wait_send()


def fused(rows, embeddings, pos_embed, ln_gain, ln_bias, w_qkv, b_qkv, w_out, b_out, valid):
    tile, _, width = embeddings.shape
    win, rim = 2 * tile, tile // 2
    tok = win * win
    shard, qkv = w_qkv.shape
    hd = w_out.shape[1]
    team = 4
    packed = 4 * LANES
    bf16, f32 = jnp.bfloat16, jnp.float32
    vmem = pl.BlockSpec(memory_space=pltpu.VMEM)
    return pl.pallas_call(
        functools.partial(kernel, rows),
        out_shape=jax.ShapeDtypeStruct(embeddings.shape, bf16),
        in_specs=[pl.BlockSpec(memory_space=pltpu.HBM)] * 9,
        out_specs=vmem,
        scratch_shapes=[
            pltpu.VMEM((tok, width), bf16),
            pltpu.VMEM((width,), f32),
            pltpu.VMEM((width,), f32),
            pltpu.VMEM((qkv,), f32),
            pltpu.VMEM((width,), f32),
            pltpu.VMEM((shard, qkv), bf16),
            pltpu.VMEM((2, 2 * tile + 2 * rim, tile, width), bf16),
            pltpu.VMEM((6, 1, 1, tok), jnp.int32),
            pltpu.VMEM((team, shard, packed), bf16),
            pltpu.VMEM((rows, 2, shard, packed), bf16),
            pltpu.VMEM((rows, 2, shard, hd), bf16),
            pltpu.VMEM((team, tok, width), bf16),
            pltpu.VMEM((win, win, width), f32),
            pltpu.VMEM((tile * tile, width), f32),
            pltpu.VMEM((tok, 16), f32),
            pltpu.VMEM((2, 2, tile * tile, 2 * LANES), bf16),
            pltpu.VMEM((team, tile * tile, 2 * LANES), bf16),
            pltpu.VMEM((2, 2, rim * tile, 2 * LANES), bf16),
            pltpu.VMEM((team, rim * tile, 2 * LANES), bf16),
            pltpu.SemaphoreType.DMA((128,)),
            pltpu.SemaphoreType.DMA((128,)),
            pltpu.SemaphoreType.DMA((10,)),
        ],
        compiler_params=pltpu.CompilerParams(
            collective_id=0, has_side_effects=True, vmem_limit_bytes=60000000
        ),
    )(
        embeddings, pos_embed, ln_gain, ln_bias, w_qkv, b_qkv, w_out, b_out, valid
    )


def shifted(value, axis, steps):
    count = lax.axis_size(axis)
    initial, last = (max(0, -steps), min(count, count - steps))
    return lax.ppermute(value, axis, [(source, source + steps) for source in range(initial, last)])


def extended(block, sides, width):
    for axis, dim in sides:
        count = lax.axis_size(axis)
        forward = [(i, i + 1) for i in range(count - 1)]
        backward = [(target, source) for source, target in forward]
        low = lax.ppermute(
            lax.slice_in_dim(block, block.shape[dim] - width, None, axis=dim), axis, forward
        )
        high = lax.ppermute(lax.slice_in_dim(block, 0, width, axis=dim), axis, backward)
        block = jnp.concatenate([low, block, high], axis=dim)
    return block


def layer_norm(inputs, ln_gain, ln_bias):
    centred = inputs - jnp.mean(inputs, axis=-1, keepdims=True)
    variance = jnp.mean(centred * centred, axis=-1, keepdims=True)
    return centred * lax.rsqrt(variance + EPSILON) * ln_gain + ln_bias


def gauss_table(win):
    offsets = jnp.arange(win, dtype=jnp.float32) - (win - 1) / 2.0
    squared = offsets[:, None] * offsets[:, None] + offsets[None, :] * offsets[None, :]
    return jnp.exp(-squared / (2.0 * SPREAD * SPREAD))


def attend(projected):
    rows_count = projected.shape[0]
    width = projected.shape[1] // 3
    head_size = width // HEADS
    queries = projected[:, :width].reshape(rows_count, HEADS, head_size)
    keys = projected[:, width : 2 * width].reshape(rows_count, HEADS, head_size)
    values = projected[:, 2 * width :].reshape(rows_count, HEADS, head_size)
    scores = jnp.einsum(
        "qhd,khd->hqk", queries, keys, preferred_element_type=jnp.float32
    ) * head_size ** (-0.5)
    highest = jnp.max(scores, axis=-1, keepdims=True)
    expon = jnp.exp(scores - highest)
    probs = (expon / jnp.sum(expon, axis=-1, keepdims=True)).astype(jnp.bfloat16)
    mixed = jnp.einsum("hqk,khd->qhd", probs, values, preferred_element_type=jnp.float32)
    return mixed.astype(jnp.bfloat16).reshape(rows_count, width)


def fold_rows(numerator, denominator, rim):
    from_next = (
        shifted(numerator[:rim].astype(jnp.bfloat16), "row", -1).astype(jnp.float32),
        shifted(denominator[:rim].astype(jnp.bfloat16), "row", -1).astype(jnp.float32),
    )
    from_prev = (
        shifted(numerator[-rim:].astype(jnp.bfloat16), "row", 1).astype(jnp.float32),
        shifted(denominator[-rim:].astype(jnp.bfloat16), "row", 1).astype(jnp.float32),
    )
    middle_num = numerator[rim:-rim]
    middle_den = denominator[rim:-rim]
    middle_num = middle_num.at[:rim].add(from_prev[0]).at[-rim:].add(from_next[0])
    middle_den = middle_den.at[:rim].add(from_prev[1]).at[-rim:].add(from_next[1])
    return (middle_num, middle_den)


def fold_cols(numerator, denominator, rim):
    from_next = (
        shifted(numerator[:, :rim].astype(jnp.bfloat16), "col", -1).astype(jnp.float32),
        shifted(denominator[:, :rim].astype(jnp.bfloat16), "col", -1).astype(jnp.float32),
    )
    from_prev = (
        shifted(numerator[:, -rim:].astype(jnp.bfloat16), "col", 1).astype(jnp.float32),
        shifted(denominator[:, -rim:].astype(jnp.bfloat16), "col", 1).astype(jnp.float32),
    )
    middle_num = numerator[:, rim:-rim] + jnp.concatenate([from_prev[0], from_next[0]], axis=1)
    middle_den = denominator[:, rim:-rim] + jnp.concatenate([from_prev[1], from_next[1]], axis=1)
    return (middle_num, middle_den)


def body(embeddings, pos_embed, ln_gain, ln_bias, w_qkv, b_qkv, w_out, b_out, valid):
    tile = embeddings.shape[1]
    tile_rows = embeddings.shape[0] // tile
    rim = tile // 2
    win = tile + 2 * rim
    rows_count = win * win
    width_model = embeddings.shape[2]
    window = extended(embeddings, (("row", 0), ("col", 1)), rim)
    stacked = jnp.stack([window], axis=0)
    inputs = stacked.reshape(tile_rows, rows_count, width_model).astype(
        jnp.float32
    ) + pos_embed.astype(jnp.float32)
    inputs = inputs.reshape(tile_rows * rows_count, width_model)
    normed = layer_norm(inputs, ln_gain, ln_bias).astype(jnp.bfloat16)
    projected = jnp.dot(
        normed,
        lax.all_gather(w_qkv, ("row", "col"), axis=0, tiled=True),
        preferred_element_type=jnp.float32,
    )
    projected = (
        (projected + b_qkv).astype(jnp.bfloat16).reshape(tile_rows, rows_count, w_qkv.shape[1])
    )
    attended = jax.vmap(attend)(projected).reshape(tile_rows * rows_count, -1)
    projected_out = lax.dot_general(
        attended,
        lax.all_gather(w_out, ("row", "col"), axis=0, tiled=True),
        (((1,), (1,)), ((), ())),
        preferred_element_type=jnp.float32,
    )
    hidden = inputs + projected_out + b_out
    gauss = gauss_table(win).reshape(1, rows_count)
    weight = gauss * valid.reshape(tile_rows, rows_count).astype(jnp.float32) / 196.0
    contrib = (weight.reshape(tile_rows * rows_count, 1) * hidden).reshape(
        tile_rows, win, win, width_model
    )
    weight_grid = weight.reshape(tile_rows, win, win)
    numerator = jnp.zeros((tile_rows * tile + 2 * rim, win, width_model), jnp.float32)
    denominator = jnp.zeros((tile_rows * tile + 2 * rim, win), jnp.float32)
    numerator = numerator.at[0:win].add(contrib[0])
    denominator = denominator.at[0:win].add(weight_grid[0])
    numerator, denominator = fold_rows(numerator, denominator, rim)
    numerator, denominator = fold_cols(numerator, denominator, rim)
    return (numerator / jnp.maximum(denominator, FLOOR)[:, :, None]).astype(jnp.bfloat16)


def solution(mesh):
    placed = (
        P(("groups", "row"), "col", None),
        P(),
        P(),
        P(),
        P(("row", "col"), None),
        P(),
        P(("row", "col"), None),
        P(),
        P(("groups", "row"), "col", None),
    )
    rows = mesh.shape["row"]

    def run(*arrays):
        embeddings, w_qkv = arrays[0], arrays[4]
        tile = embeddings.shape[1]
        whole_tiles = w_qkv.shape[0] % 16 == 0 and embeddings.shape[0] == tile == 8
        pairs = mesh.shape["groups"] == 2 and mesh.shape["col"] == 2
        if whole_tiles and pairs and rows == 8:
            return fused(rows, *arrays)
        return body(*arrays)

    return jax.shard_map(
        run,
        mesh=mesh,
        in_specs=placed,
        out_specs=P(("groups", "row"), "col", None),
        check_vma=False,
    )
```

```python
import functools

import jax
import jax.numpy as jnp
from jax import lax
from jax.experimental import pallas as pl
from jax.experimental.pallas import tpu as pltpu
from jax.sharding import PartitionSpec as P

HEADS = 8
EPSILON = 1e-06
SPREAD = 4.0
FLOOR = 0.25
LANES = 128
LOG2E = 1.4426950408889634
MESH = pl.DeviceIdType.MESH


def kernel(
    rows,
    emb_ref, pos_hbm, gain_hbm, bias_hbm, wq_ref, bq_hbm, wo_ref, bo_hbm, valid_ref,
    out_ref, pos_ref, gain_ref, bias_ref, bq_ref, bo_ref, wq_own,
    eb, vb, pack, wq_all, wo_all, nrm, posr, base, wcol, tiles_out, tiles_in,
    rims_out, rims_in, send_sems, recv_sems, local_sems,
):
    g, r, c = lax.axis_index("groups"), lax.axis_index("row"), lax.axis_index("col")
    tile, _, width = emb_ref.shape
    rim = tile // 2
    win = 2 * tile
    tok = win * win
    shard, qkv = wq_ref.shape
    hd = wo_ref.shape[1]
    head = hd // HEADS
    team = 4
    part = hd // team
    packed = pack.shape[2]
    x, z = r % 2, r // 2
    planes = rows // 2
    away = {1: z + 1 - 2 * (z % 2), 2: (z + 2) % planes, 3: planes - 1 - z}
    inner = jnp.logical_and(z > 0, z < planes - 1)
    rx, other = r + 1 - 2 * x, 1 - c
    q = 2 * x + c
    above, below = lax.rem(r + rows - 1, rows), lax.rem(r + 1, rows)
    has_above, has_below = r > 0, r < rows - 1
    has_up, has_down = z > 0, z < planes - 1
    outside = jnp.logical_and(has_above, has_below)
    facing = jnp.where(x == 0, above, below)
    to_core, to_y = (g, r, other), (1 - g, r, c)
    core = {0: c, 1: other}

    names = {}
    pending = []
    fold_base, rim_base = 0, team

    def copy(name, src, dst, device, recv=None):
        at = names.setdefault(name, len(names) + 2 * team)
        return pltpu.make_async_remote_copy(
            src_ref=src, dst_ref=dst, send_sem=send_sems.at[at],
            recv_sem=recv_sems.at[at if recv is None else recv],
            device_id=device, device_id_type=MESH,
        )

    def start(name, src, dst, device, when=None, recv=None):
        item = copy(name, src, dst, device, recv)
        pending.append((when, item))
        if when is None:
            item.start()
        else:
            pl.when(when)(item.start)

    def flush(count):
        for when, item in pending[:count]:
            if when is None:
                item.wait_send()
            else:
                pl.when(when)(item.wait_send)
        del pending[:count]

    def arrived(name, dst, when=None, recv=None):
        item = copy(name, dst, dst, to_core, recv)
        if when is None:
            item.wait_recv()
        else:
            pl.when(when)(item.wait_recv)

    own_rows, mate_rows = pl.ds(rim + tile * x, tile), pl.ds(rim + tile * (1 - x), tile)
    top_rows, low_rows = pl.ds(0, rim), pl.ds(rim + 2 * tile, rim)
    locals_ = []
    for src, dst in (
        (wq_ref, wq_own), (pos_hbm, pos_ref), (gain_hbm, gain_ref), (bias_hbm, bias_ref),
        (emb_ref, eb.at[c, own_rows]), (valid_ref, vb.at[1]), (bo_hbm, bo_ref), (bq_hbm, bq_ref),
        (wo_ref, wo_all.at[r, c]),
    ):
        item = pltpu.make_async_copy(src, dst, local_sems.at[len(locals_)])
        item.start()
        locals_.append(item)

    barrier = pltpu.get_barrier_semaphore()

    def greet(*device):
        pl.semaphore_signal(barrier, inc=1, device_id=device, device_id_type=MESH)

    for k in (2, 1):
        greet(g, 2 * away[k] + x, c)
        greet(g, 2 * away[k] + x, other)

    @pl.when(inner)
    def _():
        greet(g, 2 * away[3] + x, c)
        greet(g, 2 * away[3] + x, other)

    @pl.when(outside)
    def _():
        greet(g, facing, c)
        greet(g, facing, other)

    greet(1 - g, rx, c)
    greet(1 - g, r, c)
    greet(g, rx, c)
    greet(g, rx, other)
    greet(g, r, other)

    locals_[0].wait()
    own = wq_own[...].astype(jnp.float32)
    for k in range(team):
        cut = [own[:, t * hd + k * part:t * hd + (k + 1) * part] for t in range(3)]
        for t in range(3):
            pack[k, :, t * LANES:(t + 1) * LANES] = cut[t][:, :LANES].astype(jnp.bfloat16)
        rest = part - LANES
        pieces = [item[:, LANES:] for item in cut] + [jnp.zeros((shard, LANES - 3 * rest), jnp.float32)]
        pack[k, :, 3 * LANES:] = jnp.concatenate(pieces, axis=1).astype(jnp.bfloat16)

    pl.semaphore_wait(
        barrier, 9 + 2 * inner.astype(jnp.int32) + 2 * outside.astype(jnp.int32)
    )

    half_w = packed // 2
    mine = pl.ds(pl.multiple_of(g * half_w, LANES), half_w)
    theirs = pl.ds(pl.multiple_of((1 - g) * half_w, LANES), half_w)

    def wq_at(row, core_at, cols):
        return wq_all.at[row, core_at, :, cols]

    def reach(k):
        return None if k < 3 else inner

    for a in (0, 1):
        start(f"xm{a}", pack.at[2 * (1 - x) + core[a], :, mine], wq_at(r, c, mine), (g, rx, core[a]))
    for k in (1, 2, 3):
        for a in (0, 1):
            start(f"A{k}{a}", pack.at[2 * x + core[a], :, mine], wq_at(r, c, mine),
                  (g, 2 * away[k] + x, core[a]), reach(k))
    start("ec", emb_ref, eb.at[c, own_rows], to_core)
    start("ex", emb_ref, eb.at[c, own_rows], (g, rx, c))

    count_down = [copy("v0", valid_ref, vb.at[0], (g, below, c)), copy("v3", valid_ref, vb.at[3], (g, below, other))]
    count_up = [copy("v2", valid_ref, vb.at[2], (g, above, c)), copy("v5", valid_ref, vb.at[5], (g, above, other))]

    @pl.when(has_below)
    def _():
        for item in count_down:
            item.start()

    @pl.when(has_above)
    def _():
        for item in count_up:
            item.start()

    start("v4", valid_ref, vb.at[4], to_core)
    own_weights = pltpu.make_async_copy(pack.at[q], wq_all.at[r, c], local_sems.at[len(locals_)])
    own_weights.start()

    @pl.when(z == 0)
    def _():
        eb[0, 0:rim] = jnp.zeros((rim, tile, width), eb.dtype)
        eb[1, 0:rim] = jnp.zeros((rim, tile, width), eb.dtype)

    @pl.when(z == planes - 1)
    def _():
        eb[0, rim + 2 * tile:] = jnp.zeros((rim, tile, width), eb.dtype)
        eb[1, rim + 2 * tile:] = jnp.zeros((rim, tile, width), eb.dtype)

    @pl.when(r == 0)
    def _():
        vb[0] = jnp.zeros((1, 1, tok), vb.dtype)
        vb[3] = jnp.zeros((1, 1, tok), vb.dtype)

    @pl.when(r == rows - 1)
    def _():
        vb[2] = jnp.zeros((1, 1, tok), vb.dtype)
        vb[5] = jnp.zeros((1, 1, tok), vb.dtype)

    @pl.when(jnp.logical_not(outside))
    def _():
        rims_in[...] = jnp.zeros(rims_in.shape, rims_in.dtype)

    for item in locals_[1:5]:
        item.wait()
    gain, bias = gain_ref[...].reshape(1, width), bias_ref[...].reshape(1, width)
    per = rim

    def roll_block(block, carry):
        pos = pos_ref[pl.ds(pl.multiple_of(block * per * win, per * win), per * win)]
        pos = pos.astype(jnp.float32).reshape(per, win, width)
        posr[pl.ds(block * per, per)] = pltpu.roll(pos, win - rim, 1)
        return carry

    lax.fori_loop(0, win // per, roll_block, 0)
    place = lax.broadcasted_iota(jnp.int32, (per, tile, 1), 1)

    def norm_block(which, block, side):
        which = which + x * (1 - 2 * which)
        block = block + x * (win // per - 1 - 2 * block)
        at = pl.ds(which * tile + block * per, per)
        rim_ok = jnp.where(side == 0, place, tile - 1 - place) < rim
        left = eb[side, at].astype(jnp.float32)
        right = jnp.where(rim_ok, eb[1 - side, at].astype(jnp.float32), 0.0)
        v = (jnp.concatenate([left, right], axis=1) + posr[pl.ds(block * per, per)]).reshape(per * win, width)
        v = v - jnp.mean(v, axis=-1, keepdims=True)
        variance = jnp.mean(v * v, axis=-1, keepdims=True)
        v = v * lax.rsqrt(variance + EPSILON) * gain + bias
        there = pl.ds(pl.multiple_of(block * per * win, per * win), per * win)
        nrm[2 * which + side, there] = v.astype(jnp.bfloat16)

    def norm_own(n, carry):
        m = n // 2
        norm_block(m // 2, (m + 1) % 3, n % 2)
        return carry

    def norm_mate(n, carry):
        m = n // 2
        norm_block((m + 1) // 2, (m + 2) % 3 + 1, n % 2)
        return carry

    def norm_rims(n, carry):
        norm_block(n // 2, n // 2 * 3, n % 2)
        return carry

    def pair_at(row, cols):
        return wq_all.at[row, :, :, cols]

    def slot(name):
        return names.setdefault(name, len(names) + 2 * team)

    outer_only = jnp.logical_not(inner)

    def from_z(phase, k):
        row = 2 * away[k] + (x if phase == "A" else 1 - x)
        here = pair_at(row, mine)
        if phase == "A" and k == 1:
            for a in (0, 1):
                one = wq_at(row, core[a], mine)
                arrived(f"A1{a}", one)
                start(f"yA1{a}", one, one, to_y)
            return
        if phase == "A" and k == 2:
            for a in (0, 1):
                one = wq_at(row, core[a], mine)
                arrived(f"A2{a}", one)
        else:
            arrived(f"{phase}{k}", here, outer_only if phase == "A" else None)
            if phase == "A":
                for a in (0, 1):
                    arrived(f"A3{a}", wq_at(row, core[a], mine), inner)
        start(f"y{phase}{k}", here, here, to_y)
        if k == 2:
            start(f"f{phase}", here, here, (g, 2 * away[1] + x, c), inner, slot(f"{phase}3"))

    def from_y(phase, k):
        row = 2 * away[k] + (x if phase == "A" else 1 - x)
        if phase == "A" and k == 1:
            for a in (0, 1):
                arrived(f"yA1{a}", wq_at(row, core[a], theirs))
        else:
            arrived(f"y{phase}{k}", pair_at(row, theirs))

    arrived("ec", eb.at[other, own_rows])
    lax.fori_loop(0, 6, norm_own, 0)

    for a in (0, 1):
        arrived(f"xm{a}", wq_at(rx, core[a], mine))
    given = pair_at(rx, mine)
    gives_down = jnp.logical_and(x == 1, has_down)
    gives_up = jnp.logical_and(x == 0, has_up)
    start("B2", given, given, (g, 2 * away[2] + x, c))
    start("ht", emb_ref.at[pl.ds(tile - rim, rim)], eb.at[c, top_rows], (g, lax.rem(r + 2, rows), c), gives_down,
          slot("ht"))
    start("hb", emb_ref.at[pl.ds(0, rim)], eb.at[c, low_rows], (g, lax.rem(r + rows - 2, rows), c), gives_up,
          slot("hb"))
    start("B1", given, given, (g, 2 * away[1] + x, c))
    start("B3", given, given, (g, 2 * away[3] + x, c), inner)
    for a in (0, 1):
        start(f"xt{a}", pack.at[2 * (1 - x) + core[a], :, theirs], wq_at(r, c, theirs), (g, rx, core[a]))
    start("wc", pack.at[2 * x + other], wq_all.at[r, c], to_core)
    start("ox", wo_ref, wo_all.at[r, c], (g, rx, c))
    start("oc", wo_ref, wo_all.at[r, c], to_core)

    units = hd // LANES
    side_w = units // 2 * LANES
    ring_w = hd - side_w
    ring = pl.ds(pl.multiple_of(g * side_w, LANES), ring_w)
    y_out = pl.ds(pl.multiple_of(g * ring_w, LANES), side_w)
    y_in = pl.ds(pl.multiple_of((1 - g) * ring_w, LANES), side_w)

    def wo_at(row, cols):
        return wo_all.at[row, c, :, cols]


    from_z("A", 1)
    from_z("A", 2)

    arrived("ex", eb.at[c, mate_rows])
    start("exf", eb.at[c, mate_rows], eb.at[c, mate_rows], to_core)
    arrived("v4", vb.at[4])

    @pl.when(has_above)
    def _():
        for item in count_down:
            item.wait_recv()

    @pl.when(has_below)
    def _():
        for item in count_up:
            item.wait_recv()

    for item in locals_[5:]:
        item.wait()
    near_v = [vb[k, 0] for k in range(3)]
    far_v = [vb[k + 3, 0] for k in range(3)]
    mate_near, mate_far = jnp.where(x == 0, near_v[2], near_v[0]), jnp.where(x == 0, far_v[2], far_v[0])
    counts = near_v + far_v
    for i in (0, 1):
        for side in (0, 1):
            same = jnp.where(c == side, near_v[1], far_v[1])
            mate = jnp.where(c == side, mate_near, mate_far)
            counts.append(jnp.where(x == i, same, mate))
    counts = jnp.concatenate(
        [v.astype(jnp.float32) for v in counts] + [jnp.zeros((6, tok), jnp.float32)], axis=0
    ).astype(jnp.bfloat16)
    t_row = lax.broadcasted_iota(jnp.int32, (tok, tok), 0)
    t_col = lax.broadcasted_iota(jnp.int32, (tok, tok), 1)
    base_row = t_row // win * win
    pick = (t_col == base_row + (t_row - base_row + rim) % win).astype(jnp.float32).astype(jnp.bfloat16)
    counts = lax.dot_general(pick, counts, (((1,), (1,)), ((), ())), preferred_element_type=jnp.float32)
    t = lax.broadcasted_iota(jnp.int32, (tok, 1), 0)
    oi = (t // win).astype(jnp.float32) - (win - 1) / 2.0
    oj = ((t % win + rim) % win).astype(jnp.float32) - (win - 1) / 2.0
    gauss = jnp.exp(-(oi * oi + oj * oj) / (2.0 * SPREAD * SPREAD))
    weights = gauss * counts / 196.0
    at_col = lax.broadcasted_iota(jnp.int32, weights.shape, 1) % 2
    at_place = lax.broadcasted_iota(jnp.int32, weights.shape, 0) % win - tile
    kept = jnp.where(at_col == 0, at_place, tile - 1 - at_place) < rim
    wcol[...] = jnp.where(jnp.logical_or(at_place < 0, kept), weights, 0.0)
    grid = weights.reshape(win, win, weights.shape[1])
    near = grid[:, :tile].reshape(win * tile, weights.shape[1])
    far = grid[:, tile:].reshape(win * tile, weights.shape[1])
    u = lax.broadcasted_iota(jnp.int32, (win * tile, 1), 0) % tile
    fold_ok = jnp.where(c == 1, u, tile - 1 - u) < rim
    far = jnp.where(fold_ok, far, 0.0)
    low, high = rim * tile, (rim + tile) * tile
    near0, far0 = near[low:high, 1:2], far[low:high, 4:5]
    near_a = jnp.where(has_above, near[high:, 0:1], 0.0)
    far_a = jnp.where(has_above, far[high:, 3:4], 0.0)
    near_b = jnp.where(has_below, near[:low, 2:3], 0.0)
    far_b = jnp.where(has_below, far[:low, 5:6], 0.0)
    denom = near0 + far0 + jnp.concatenate([near_a + far_a, near_b + far_b], axis=0)

    def flat(lo, hi, a, b):
        return posr[lo:hi, a:b].reshape((hi - lo) * (b - a), width)

    total = denom * (
        eb[c, own_rows].astype(jnp.float32).reshape(tile * tile, width)
        + bo_ref[...].reshape(1, width)
    )
    total += near0 * flat(rim, rim + tile, 0, tile) + far0 * flat(rim, rim + tile, tile, win)
    base[...] = total
    base[0:low] += near_a * flat(rim + tile, win, 0, tile) + far_a * flat(rim + tile, win, tile, win)
    base[low:] += near_b * flat(0, rim, 0, tile) + far_b * flat(0, rim, tile, win)

    early = len(pending)
    from_z("B", 2)
    for k in (2, 1, 3):
        start(f"o{k}", wo_ref.at[:, ring], wo_at(r, ring), (g, 2 * away[k] + x, c), reach(k))
    from_z("B", 1)
    arrived("exf", eb.at[other, mate_rows])
    lax.fori_loop(0, 6, norm_mate, 0)
    from_z("A", 3)
    for name, place_at, exists, direct in (("ht", top_rows, has_up, x == 1), ("hb", low_rows, has_down, x == 0)):
        here = eb.at[c, place_at]
        first = jnp.logical_and(exists, direct)
        arrived(name, here, first)
        start(f"{name}x", here, here, (g, rx, c), first)
        start(f"{name}f", here, here, to_core, first)
    from_z("B", 3)
    later = len(pending)
    arrived("ox", wo_at(rx, pl.ds(0, hd)))
    start("oxf", wo_all.at[rx, c], wo_all.at[rx, c], to_core)

    def out_from_z(k):
        here, side = wo_at(2 * away[k] + x, ring), wo_at(2 * away[k] + x, y_out)
        arrived(f"o{k}", here)
        start(f"ox{k}", here, here, (g, rx, c))
        start(f"oy{k}", side, side, to_y)
        start(f"od{k}", side, side, (1 - g, rx, c))
        if k == 2:
            start("of", here, here, (g, 2 * away[1] + x, c), inner, names.setdefault("o3", len(names) + 2 * team))

    def out_to_core(k):
        row, mate = 2 * away[k] + x, 2 * away[k] + 1 - x
        arrived(f"oy{k}", wo_at(row, y_in))
        start(f"oc{k}", wo_all.at[row, c], wo_all.at[row, c], to_core)
        arrived(f"ox{k}", wo_at(mate, ring))
        arrived(f"od{k}", wo_at(mate, y_in))
        start(f"om{k}", wo_all.at[mate, c], wo_all.at[mate, c], to_core)

    out_from_z(2)
    for name, place_at, exists, direct in (("ht", top_rows, has_up, x == 1), ("hb", low_rows, has_down, x == 0)):
        here = eb.at[c, place_at]
        second = jnp.logical_and(exists, jnp.logical_not(direct))
        arrived(f"{name}x", here, second)
        start(f"{name}g", here, here, to_core, second, slot(f"{name}f"))
    for name, place_at, when in (("ht", top_rows, has_up), ("hb", low_rows, has_down)):
        arrived(f"{name}f", eb.at[other, place_at], when)
    lax.fori_loop(0, 4, norm_rims, 0)
    out_from_z(1)
    flush(early)
    own_weights.wait()
    arrived("wc", wq_all.at[r, other])
    for a in (0, 1):
        arrived(f"xt{a}", wq_at(rx, core[a], theirs))
    for phase in ("A", "B"):
        for k in (1, 2, 3):
            from_y(phase, k)

    b_own = bq_ref[...].reshape(1, qkv)
    b_parts = []
    for k in range(team):
        cut = [b_own[:, t * hd + k * part:t * hd + (k + 1) * part] for t in range(3)]
        rest = part - LANES
        b_parts.append(jnp.concatenate(
            [item[:, :LANES] for item in cut] + [item[:, LANES:] for item in cut]
            + [jnp.zeros((1, LANES - 3 * rest), jnp.float32)], axis=1))
    b_mine = jnp.where(x == 0, jnp.where(c == 0, b_parts[0], b_parts[1]), jnp.where(c == 0, b_parts[2], b_parts[3]))
    lane = lax.broadcasted_iota(jnp.int32, (1, 2 * LANES), 1)
    rest = part - LANES

    def attend(w):
        proj = jnp.dot(nrm[w], wq_all[...].reshape(width, packed), preferred_element_type=jnp.float32) + b_mine
        tail = proj[:, 3 * LANES:]
        queries = jnp.concatenate([proj[:, :LANES], tail], axis=1)
        keys = jnp.concatenate([proj[:, LANES:2 * LANES], pltpu.roll(tail, LANES - rest, 1)], axis=1)
        values = jnp.concatenate([proj[:, 2 * LANES:3 * LANES], pltpu.roll(tail, LANES - 2 * rest, 1)], axis=1)
        keys, values = keys.astype(jnp.bfloat16), values.astype(jnp.bfloat16)
        outs = []
        for h in range(HEADS // team):
            inside = jnp.logical_and(lane >= h * head, lane < (h + 1) * head)
            used = -(-(h + 1) * head // LANES) * LANES
            chosen = jnp.where(inside, queries, 0.0).astype(jnp.bfloat16)
            scores = lax.dot_general(
                chosen[:, :used], keys[:, :used], (((1,), (1,)), ((), ())), preferred_element_type=jnp.float32
            )
            expon = jnp.exp2((scores - jnp.max(scores, axis=-1, keepdims=True)) * (head ** (-0.5) * LOG2E))
            inverse = 1.0 / jnp.sum(expon, axis=-1, keepdims=True)
            outs.append(jnp.dot(expon.astype(jnp.bfloat16), values, preferred_element_type=jnp.float32) * inverse)
        mixed = jnp.where(lane < head, outs[0], jnp.where(lane < part, outs[1], 0.0))
        mixed = mixed.astype(jnp.bfloat16).astype(jnp.float32) * wcol[:, 6 + w:7 + w]
        return mixed.reshape(win, win, 2 * LANES)

    def flatten(value):
        return value.reshape(value.shape[0] * tile, 2 * LANES)

    def both(i):
        left, right = attend(2 * i), attend(2 * i + 1)
        return [left[:, :tile] + right[:, tile:], right[:, :tile] + left[:, tile:]]

    upper = both(0)
    for side in (0, 1):
        rims_out[0, side] = flatten(upper[side][:rim]).astype(jnp.bfloat16)
    for side in (0, 1):
        start(f"rt{side}", rims_out.at[0, side], rims_in.at[q], (g, lax.rem(2 * z + rows - 1, rows), side), has_up,
              rim_base + q)
    out_from_z(3)
    lower = both(1)
    for side in (0, 1):
        rims_out[1, side] = flatten(lower[side][rim + tile:]).astype(jnp.bfloat16)
    for side in (0, 1):
        start(f"rb{side}", rims_out.at[1, side], rims_in.at[q], (g, lax.rem(2 * z + 2, rows), side), has_down,
              rim_base + q)
    for side in (0, 1):
        first = jnp.concatenate([upper[side][rim:tile], upper[side][tile:rim + tile] + lower[side][:rim]], axis=0)
        second = jnp.concatenate([lower[side][rim:tile] + upper[side][rim + tile:], lower[side][tile:rim + tile]], axis=0)
        tiles_out[0, side] = flatten(first).astype(jnp.bfloat16)
        tiles_out[1, side] = flatten(second).astype(jnp.bfloat16)
    start("fx", tiles_out.at[1 - x, c], tiles_in.at[q], (g, rx, c), None, fold_base + q)
    start("fd", tiles_out.at[1 - x, other], tiles_in.at[q], (g, rx, other), None, fold_base + q)
    start("fc", tiles_out.at[x, other], tiles_in.at[q], to_core, None, fold_base + q)
    tiles_in[q] = tiles_out[x, c]

    flush(later - early)
    for k in (1, 2, 3):
        out_to_core(k)
    arrived("oc", wo_all.at[r, other])
    arrived("oxf", wo_all.at[rx, other])
    for k in (1, 2, 3):
        arrived(f"oc{k}", wo_all.at[2 * away[k] + x, other])
        arrived(f"om{k}", wo_all.at[2 * away[k] + 1 - x, other])

    for at in (2 * x + other, 2 * (1 - x) + c, 2 * (1 - x) + other):
        arrived("fc", tiles_in.at[at], None, fold_base + at)
    for at in range(team):
        arrived("fc", rims_in.at[at], outside, rim_base + at)

    sums = []
    for at in range(team):
        edge = rims_in[at].astype(jnp.float32)
        edge = jnp.concatenate([jnp.where(x == 0, edge, 0.0), jnp.where(x == 1, edge, 0.0)], axis=0)
        sums.append((tiles_in[at].astype(jnp.float32) + edge)[:, :part])
    merged = jnp.concatenate(sums, axis=1).astype(jnp.bfloat16)
    result = base[...] + lax.dot_general(
        merged, wo_all[...].reshape(width, hd), (((1,), (1,)), ((), ())), preferred_element_type=jnp.float32,
    )
    result = result / jnp.maximum(denom, FLOOR)
    out_ref[...] = result.reshape(tile, tile, width).astype(out_ref.dtype)

    flush(len(pending))

    @pl.when(has_above)
    def _():
        for item in count_up:
            item.wait_send()

    @pl.when(has_below)
    def _():
        for item in count_down:
            item.wait_send()


def fused(rows, embeddings, pos_embed, ln_gain, ln_bias, w_qkv, b_qkv, w_out, b_out, valid):
    tile, _, width = embeddings.shape
    win, rim = 2 * tile, tile // 2
    tok = win * win
    shard, qkv = w_qkv.shape
    hd = w_out.shape[1]
    team = 4
    packed = 4 * LANES
    bf16, f32 = jnp.bfloat16, jnp.float32
    vmem = pl.BlockSpec(memory_space=pltpu.VMEM)
    return pl.pallas_call(
        functools.partial(kernel, rows),
        out_shape=jax.ShapeDtypeStruct(embeddings.shape, bf16),
        in_specs=[pl.BlockSpec(memory_space=pltpu.HBM)] * 9,
        out_specs=vmem,
        scratch_shapes=[
            pltpu.VMEM((tok, width), bf16),
            pltpu.VMEM((width,), f32),
            pltpu.VMEM((width,), f32),
            pltpu.VMEM((qkv,), f32),
            pltpu.VMEM((width,), f32),
            pltpu.VMEM((shard, qkv), bf16),
            pltpu.VMEM((2, 2 * tile + 2 * rim, tile, width), bf16),
            pltpu.VMEM((6, 1, 1, tok), jnp.int32),
            pltpu.VMEM((team, shard, packed), bf16),
            pltpu.VMEM((rows, 2, shard, packed), bf16),
            pltpu.VMEM((rows, 2, shard, hd), bf16),
            pltpu.VMEM((team, tok, width), bf16),
            pltpu.VMEM((win, win, width), f32),
            pltpu.VMEM((tile * tile, width), f32),
            pltpu.VMEM((tok, 16), f32),
            pltpu.VMEM((2, 2, tile * tile, 2 * LANES), bf16),
            pltpu.VMEM((team, tile * tile, 2 * LANES), bf16),
            pltpu.VMEM((2, 2, rim * tile, 2 * LANES), bf16),
            pltpu.VMEM((team, rim * tile, 2 * LANES), bf16),
            pltpu.SemaphoreType.DMA((128,)),
            pltpu.SemaphoreType.DMA((128,)),
            pltpu.SemaphoreType.DMA((10,)),
        ],
        compiler_params=pltpu.CompilerParams(
            collective_id=0, has_side_effects=True, vmem_limit_bytes=60000000
        ),
    )(
        embeddings, pos_embed, ln_gain, ln_bias, w_qkv, b_qkv, w_out, b_out, valid
    )


def shifted(value, axis, steps):
    count = lax.axis_size(axis)
    initial, last = (max(0, -steps), min(count, count - steps))
    return lax.ppermute(value, axis, [(source, source + steps) for source in range(initial, last)])


def extended(block, sides, width):
    for axis, dim in sides:
        count = lax.axis_size(axis)
        forward = [(i, i + 1) for i in range(count - 1)]
        backward = [(target, source) for source, target in forward]
        low = lax.ppermute(
            lax.slice_in_dim(block, block.shape[dim] - width, None, axis=dim), axis, forward
        )
        high = lax.ppermute(lax.slice_in_dim(block, 0, width, axis=dim), axis, backward)
        block = jnp.concatenate([low, block, high], axis=dim)
    return block


def layer_norm(inputs, ln_gain, ln_bias):
    centred = inputs - jnp.mean(inputs, axis=-1, keepdims=True)
    variance = jnp.mean(centred * centred, axis=-1, keepdims=True)
    return centred * lax.rsqrt(variance + EPSILON) * ln_gain + ln_bias


def gauss_table(win):
    offsets = jnp.arange(win, dtype=jnp.float32) - (win - 1) / 2.0
    squared = offsets[:, None] * offsets[:, None] + offsets[None, :] * offsets[None, :]
    return jnp.exp(-squared / (2.0 * SPREAD * SPREAD))


def attend(projected):
    rows_count = projected.shape[0]
    width = projected.shape[1] // 3
    head_size = width // HEADS
    queries = projected[:, :width].reshape(rows_count, HEADS, head_size)
    keys = projected[:, width : 2 * width].reshape(rows_count, HEADS, head_size)
    values = projected[:, 2 * width :].reshape(rows_count, HEADS, head_size)
    scores = jnp.einsum(
        "qhd,khd->hqk", queries, keys, preferred_element_type=jnp.float32
    ) * head_size ** (-0.5)
    highest = jnp.max(scores, axis=-1, keepdims=True)
    expon = jnp.exp(scores - highest)
    probs = (expon / jnp.sum(expon, axis=-1, keepdims=True)).astype(jnp.bfloat16)
    mixed = jnp.einsum("hqk,khd->qhd", probs, values, preferred_element_type=jnp.float32)
    return mixed.astype(jnp.bfloat16).reshape(rows_count, width)


def fold_rows(numerator, denominator, rim):
    from_next = (
        shifted(numerator[:rim].astype(jnp.bfloat16), "row", -1).astype(jnp.float32),
        shifted(denominator[:rim].astype(jnp.bfloat16), "row", -1).astype(jnp.float32),
    )
    from_prev = (
        shifted(numerator[-rim:].astype(jnp.bfloat16), "row", 1).astype(jnp.float32),
        shifted(denominator[-rim:].astype(jnp.bfloat16), "row", 1).astype(jnp.float32),
    )
    middle_num = numerator[rim:-rim]
    middle_den = denominator[rim:-rim]
    middle_num = middle_num.at[:rim].add(from_prev[0]).at[-rim:].add(from_next[0])
    middle_den = middle_den.at[:rim].add(from_prev[1]).at[-rim:].add(from_next[1])
    return (middle_num, middle_den)


def fold_cols(numerator, denominator, rim):
    from_next = (
        shifted(numerator[:, :rim].astype(jnp.bfloat16), "col", -1).astype(jnp.float32),
        shifted(denominator[:, :rim].astype(jnp.bfloat16), "col", -1).astype(jnp.float32),
    )
    from_prev = (
        shifted(numerator[:, -rim:].astype(jnp.bfloat16), "col", 1).astype(jnp.float32),
        shifted(denominator[:, -rim:].astype(jnp.bfloat16), "col", 1).astype(jnp.float32),
    )
    middle_num = numerator[:, rim:-rim] + jnp.concatenate([from_prev[0], from_next[0]], axis=1)
    middle_den = denominator[:, rim:-rim] + jnp.concatenate([from_prev[1], from_next[1]], axis=1)
    return (middle_num, middle_den)


def body(embeddings, pos_embed, ln_gain, ln_bias, w_qkv, b_qkv, w_out, b_out, valid):
    tile = embeddings.shape[1]
    tile_rows = embeddings.shape[0] // tile
    rim = tile // 2
    win = tile + 2 * rim
    rows_count = win * win
    width_model = embeddings.shape[2]
    window = extended(embeddings, (("row", 0), ("col", 1)), rim)
    stacked = jnp.stack([window], axis=0)
    inputs = stacked.reshape(tile_rows, rows_count, width_model).astype(
        jnp.float32
    ) + pos_embed.astype(jnp.float32)
    inputs = inputs.reshape(tile_rows * rows_count, width_model)
    normed = layer_norm(inputs, ln_gain, ln_bias).astype(jnp.bfloat16)
    projected = jnp.dot(
        normed,
        lax.all_gather(w_qkv, ("row", "col"), axis=0, tiled=True),
        preferred_element_type=jnp.float32,
    )
    projected = (
        (projected + b_qkv).astype(jnp.bfloat16).reshape(tile_rows, rows_count, w_qkv.shape[1])
    )
    attended = jax.vmap(attend)(projected).reshape(tile_rows * rows_count, -1)
    projected_out = lax.dot_general(
        attended,
        lax.all_gather(w_out, ("row", "col"), axis=0, tiled=True),
        (((1,), (1,)), ((), ())),
        preferred_element_type=jnp.float32,
    )
    hidden = inputs + projected_out + b_out
    gauss = gauss_table(win).reshape(1, rows_count)
    weight = gauss * valid.reshape(tile_rows, rows_count).astype(jnp.float32) / 196.0
    contrib = (weight.reshape(tile_rows * rows_count, 1) * hidden).reshape(
        tile_rows, win, win, width_model
    )
    weight_grid = weight.reshape(tile_rows, win, win)
    numerator = jnp.zeros((tile_rows * tile + 2 * rim, win, width_model), jnp.float32)
    denominator = jnp.zeros((tile_rows * tile + 2 * rim, win), jnp.float32)
    numerator = numerator.at[0:win].add(contrib[0])
    denominator = denominator.at[0:win].add(weight_grid[0])
    numerator, denominator = fold_rows(numerator, denominator, rim)
    numerator, denominator = fold_cols(numerator, denominator, rim)
    return (numerator / jnp.maximum(denominator, FLOOR)[:, :, None]).astype(jnp.bfloat16)


def solution(mesh):
    placed = (
        P(("groups", "row"), "col", None),
        P(),
        P(),
        P(),
        P(("row", "col"), None),
        P(),
        P(("row", "col"), None),
        P(),
        P(("groups", "row"), "col", None),
    )
    rows = mesh.shape["row"]

    def run(*arrays):
        embeddings, w_qkv = arrays[0], arrays[4]
        tile = embeddings.shape[1]
        whole_tiles = w_qkv.shape[0] % 16 == 0 and embeddings.shape[0] == tile == 8
        pairs = mesh.shape["groups"] == 2 and mesh.shape["col"] == 2
        if whole_tiles and pairs and rows == 8:
            return fused(rows, *arrays)
        return body(*arrays)

    return jax.shard_map(
        run,
        mesh=mesh,
        in_specs=placed,
        out_specs=P(("groups", "row"), "col", None),
        check_vma=False,
    )
```

```python
import functools

import jax
import jax.numpy as jnp
from jax import lax
from jax.experimental import pallas as pl
from jax.experimental.pallas import tpu as pltpu
from jax.sharding import PartitionSpec as P

HEADS = 8
EPSILON = 1e-06
SPREAD = 4.0
FLOOR = 0.25
LANES = 128
LOG2E = 1.4426950408889634
MESH = pl.DeviceIdType.MESH


def kernel(
    rows,
    emb_ref, pos_hbm, gain_hbm, bias_hbm, wq_ref, bq_hbm, wo_ref, bo_hbm, valid_ref,
    out_ref, pos_ref, gain_ref, bias_ref, bq_ref, bo_ref, wq_own,
    eb, vb, pack, wq_all, wo_all, nrm, posr, base, wcol, tiles_out, tiles_in,
    rims_out, rims_in, send_sems, recv_sems, local_sems, early_qkv,
):
    g, r, c = lax.axis_index("groups"), lax.axis_index("row"), lax.axis_index("col")
    tile, _, width = emb_ref.shape
    rim = tile // 2
    win = 2 * tile
    tok = win * win
    shard, qkv = wq_ref.shape
    hd = wo_ref.shape[1]
    head = hd // HEADS
    team = 4
    part = hd // team
    packed = pack.shape[2]
    x, z = r % 2, r // 2
    planes = rows // 2
    away = {1: z + 1 - 2 * (z % 2), 2: (z + 2) % planes, 3: planes - 1 - z}
    inner = jnp.logical_and(z > 0, z < planes - 1)
    rx, other = r + 1 - 2 * x, 1 - c
    q = 2 * x + c
    above, below = lax.rem(r + rows - 1, rows), lax.rem(r + 1, rows)
    has_above, has_below = r > 0, r < rows - 1
    has_up, has_down = z > 0, z < planes - 1
    outside = jnp.logical_and(has_above, has_below)
    facing = jnp.where(x == 0, above, below)
    to_core, to_y = (g, r, other), (1 - g, r, c)
    core = {0: c, 1: other}

    names = {}
    pending = []
    fold_base, rim_base = 0, team

    def copy(name, src, dst, device, recv=None):
        at = names.setdefault(name, len(names) + 2 * team)
        return pltpu.make_async_remote_copy(
            src_ref=src, dst_ref=dst, send_sem=send_sems.at[at],
            recv_sem=recv_sems.at[at if recv is None else recv],
            device_id=device, device_id_type=MESH,
        )

    def start(name, src, dst, device, when=None, recv=None):
        item = copy(name, src, dst, device, recv)
        pending.append((when, item))
        if when is None:
            item.start()
        else:
            pl.when(when)(item.start)

    def flush(count):
        for when, item in pending[:count]:
            if when is None:
                item.wait_send()
            else:
                pl.when(when)(item.wait_send)
        del pending[:count]

    def arrived(name, dst, when=None, recv=None):
        item = copy(name, dst, dst, to_core, recv)
        if when is None:
            item.wait_recv()
        else:
            pl.when(when)(item.wait_recv)

    own_rows, mate_rows = pl.ds(rim + tile * x, tile), pl.ds(rim + tile * (1 - x), tile)
    top_rows, low_rows = pl.ds(0, rim), pl.ds(rim + 2 * tile, rim)
    locals_ = []
    for src, dst in (
        (wq_ref, wq_own), (pos_hbm, pos_ref), (gain_hbm, gain_ref), (bias_hbm, bias_ref),
        (emb_ref, eb.at[c, own_rows]), (valid_ref, vb.at[1]), (bo_hbm, bo_ref), (bq_hbm, bq_ref),
        (wo_ref, wo_all.at[r, c]),
    ):
        item = pltpu.make_async_copy(src, dst, local_sems.at[len(locals_)])
        item.start()
        locals_.append(item)

    barrier = pltpu.get_barrier_semaphore()

    def greet(*device):
        pl.semaphore_signal(barrier, inc=1, device_id=device, device_id_type=MESH)

    for k in (2, 1):
        greet(g, 2 * away[k] + x, c)
        greet(g, 2 * away[k] + x, other)

    @pl.when(inner)
    def _():
        greet(g, 2 * away[3] + x, c)
        greet(g, 2 * away[3] + x, other)

    @pl.when(outside)
    def _():
        greet(g, facing, c)
        greet(g, facing, other)

    greet(1 - g, rx, c)
    greet(1 - g, r, c)
    greet(g, rx, c)
    greet(g, rx, other)
    greet(g, r, other)

    locals_[0].wait()
    own = wq_own[...].astype(jnp.float32)
    for k in range(team):
        cut = [own[:, t * hd + k * part:t * hd + (k + 1) * part] for t in range(3)]
        for t in range(3):
            pack[k, :, t * LANES:(t + 1) * LANES] = cut[t][:, :LANES].astype(jnp.bfloat16)
        rest = part - LANES
        pieces = [item[:, LANES:] for item in cut] + [jnp.zeros((shard, LANES - 3 * rest), jnp.float32)]
        pack[k, :, 3 * LANES:] = jnp.concatenate(pieces, axis=1).astype(jnp.bfloat16)

    pl.semaphore_wait(
        barrier, 9 + 2 * inner.astype(jnp.int32) + 2 * outside.astype(jnp.int32)
    )

    half_w = packed // 2
    mine = pl.ds(pl.multiple_of(g * half_w, LANES), half_w)
    theirs = pl.ds(pl.multiple_of((1 - g) * half_w, LANES), half_w)

    def wq_at(row, core_at, cols):
        return wq_all.at[row, core_at, :, cols]

    def reach(k):
        return None if k < 3 else inner

    for a in (0, 1):
        start(f"xm{a}", pack.at[2 * (1 - x) + core[a], :, mine], wq_at(r, c, mine), (g, rx, core[a]))
    for k in (1, 2, 3):
        for a in (0, 1):
            start(f"A{k}{a}", pack.at[2 * x + core[a], :, mine], wq_at(r, c, mine),
                  (g, 2 * away[k] + x, core[a]), reach(k))
    start("ec", emb_ref, eb.at[c, own_rows], to_core)
    start("ex", emb_ref, eb.at[c, own_rows], (g, rx, c))

    count_down = [copy("v0", valid_ref, vb.at[0], (g, below, c)), copy("v3", valid_ref, vb.at[3], (g, below, other))]
    count_up = [copy("v2", valid_ref, vb.at[2], (g, above, c)), copy("v5", valid_ref, vb.at[5], (g, above, other))]

    @pl.when(has_below)
    def _():
        for item in count_down:
            item.start()

    @pl.when(has_above)
    def _():
        for item in count_up:
            item.start()

    start("v4", valid_ref, vb.at[4], to_core)
    own_weights = pltpu.make_async_copy(pack.at[q], wq_all.at[r, c], local_sems.at[len(locals_)])
    own_weights.start()

    @pl.when(z == 0)
    def _():
        eb[0, 0:rim] = jnp.zeros((rim, tile, width), eb.dtype)
        eb[1, 0:rim] = jnp.zeros((rim, tile, width), eb.dtype)

    @pl.when(z == planes - 1)
    def _():
        eb[0, rim + 2 * tile:] = jnp.zeros((rim, tile, width), eb.dtype)
        eb[1, rim + 2 * tile:] = jnp.zeros((rim, tile, width), eb.dtype)

    @pl.when(r == 0)
    def _():
        vb[0] = jnp.zeros((1, 1, tok), vb.dtype)
        vb[3] = jnp.zeros((1, 1, tok), vb.dtype)

    @pl.when(r == rows - 1)
    def _():
        vb[2] = jnp.zeros((1, 1, tok), vb.dtype)
        vb[5] = jnp.zeros((1, 1, tok), vb.dtype)

    @pl.when(jnp.logical_not(outside))
    def _():
        rims_in[...] = jnp.zeros(rims_in.shape, rims_in.dtype)

    for item in locals_[1:5]:
        item.wait()
    gain, bias = gain_ref[...].reshape(1, width), bias_ref[...].reshape(1, width)
    per = rim

    def roll_block(block, carry):
        pos = pos_ref[pl.ds(pl.multiple_of(block * per * win, per * win), per * win)]
        pos = pos.astype(jnp.float32).reshape(per, win, width)
        posr[pl.ds(block * per, per)] = pltpu.roll(pos, win - rim, 1)
        return carry

    lax.fori_loop(0, win // per, roll_block, 0)
    place = lax.broadcasted_iota(jnp.int32, (per, tile, 1), 1)

    def norm_block(which, block, side):
        which = which + x * (1 - 2 * which)
        block = block + x * (win // per - 1 - 2 * block)
        at = pl.ds(which * tile + block * per, per)
        rim_ok = jnp.where(side == 0, place, tile - 1 - place) < rim
        left = eb[side, at].astype(jnp.float32)
        right = jnp.where(rim_ok, eb[1 - side, at].astype(jnp.float32), 0.0)
        v = (jnp.concatenate([left, right], axis=1) + posr[pl.ds(block * per, per)]).reshape(per * win, width)
        v = v - jnp.mean(v, axis=-1, keepdims=True)
        variance = jnp.mean(v * v, axis=-1, keepdims=True)
        v = v * lax.rsqrt(variance + EPSILON) * gain + bias
        there = pl.ds(pl.multiple_of(block * per * win, per * win), per * win)
        nrm[2 * which + side, there] = v.astype(jnp.bfloat16)

    def norm_own(n, carry):
        m = n // 2
        norm_block(m // 2, (m + 1) % 3, n % 2)
        return carry

    def norm_mate(n, carry):
        m = n // 2
        norm_block((m + 1) // 2, (m + 2) % 3 + 1, n % 2)
        return carry

    def norm_rims(n, carry):
        norm_block(n // 2, n // 2 * 3, n % 2)
        return carry

    def pair_at(row, cols):
        return wq_all.at[row, :, :, cols]

    def slot(name):
        return names.setdefault(name, len(names) + 2 * team)

    outer_only = jnp.logical_not(inner)

    def from_z(phase, k):
        row = 2 * away[k] + (x if phase == "A" else 1 - x)
        here = pair_at(row, mine)
        if phase == "A" and k == 1:
            for a in (0, 1):
                one = wq_at(row, core[a], mine)
                arrived(f"A1{a}", one)
                start(f"yA1{a}", one, one, to_y)
            return
        if phase == "B" and k > 1:
            for a in (0, 1):
                one = wq_at(row, core[a], mine)
                arrived(f"B{k}{a}", one)
                if k == 2:
                    start(f"fB{a}", one, one, (g, 2 * away[1] + x, c), inner, slot(f"B3{a}"))
                start(f"yB{k}{a}", one, one, to_y)
            return
        if phase == "A" and k == 2:
            for a in (0, 1):
                one = wq_at(row, core[a], mine)
                arrived(f"A2{a}", one)
        else:
            arrived(f"{phase}{k}", here, outer_only if phase == "A" else None)
            if phase == "A":
                for a in (0, 1):
                    arrived(f"A3{a}", wq_at(row, core[a], mine), inner)
        start(f"y{phase}{k}", here, here, to_y)
        if k == 2:
            start(f"f{phase}", here, here, (g, 2 * away[1] + x, c), inner, slot(f"{phase}3"))

    def from_y(phase, k):
        row = 2 * away[k] + (x if phase == "A" else 1 - x)
        if (phase, k) in (("A", 1), ("B", 2), ("B", 3)):
            for a in (0, 1):
                arrived(f"y{phase}{k}{a}", wq_at(row, core[a], theirs))
        else:
            arrived(f"y{phase}{k}", pair_at(row, theirs))

    arrived("ec", eb.at[other, own_rows])
    lax.fori_loop(0, 6, norm_own, 0)

    for a in (0, 1):
        arrived(f"xm{a}", wq_at(rx, core[a], mine))
    given = pair_at(rx, mine)
    gives_down = jnp.logical_and(x == 1, has_down)
    gives_up = jnp.logical_and(x == 0, has_up)
    halves = [wq_at(rx, core[a], mine) for a in (0, 1)]
    for a in (0, 1):
        start(f"B2{a}", halves[a], halves[a], (g, 2 * away[2] + x, c))
    start("ht", emb_ref.at[pl.ds(tile - rim, rim)], eb.at[c, top_rows], (g, lax.rem(r + 2, rows), c), gives_down,
          slot("ht"))
    start("hb", emb_ref.at[pl.ds(0, rim)], eb.at[c, low_rows], (g, lax.rem(r + rows - 2, rows), c), gives_up,
          slot("hb"))
    start("B1", given, given, (g, 2 * away[1] + x, c))
    for a in (0, 1):
        start(f"B3{a}", halves[a], halves[a], (g, 2 * away[3] + x, c), inner)
    for a in (0, 1):
        start(f"xt{a}", pack.at[2 * (1 - x) + core[a], :, theirs], wq_at(r, c, theirs), (g, rx, core[a]))
    start("wc", pack.at[2 * x + other], wq_all.at[r, c], to_core)
    start("ox", wo_ref, wo_all.at[r, c], (g, rx, c))
    start("oc", wo_ref, wo_all.at[r, c], to_core)

    units = hd // LANES
    side_w = units // 2 * LANES
    ring_w = hd - side_w
    ring = pl.ds(pl.multiple_of(g * side_w, LANES), ring_w)
    y_out = pl.ds(pl.multiple_of(g * ring_w, LANES), side_w)
    y_in = pl.ds(pl.multiple_of((1 - g) * ring_w, LANES), side_w)

    def wo_at(row, cols):
        return wo_all.at[row, c, :, cols]


    from_z("A", 1)
    from_z("A", 2)

    arrived("ex", eb.at[c, mate_rows])
    start("exf", eb.at[c, mate_rows], eb.at[c, mate_rows], to_core)
    arrived("v4", vb.at[4])

    @pl.when(has_above)
    def _():
        for item in count_down:
            item.wait_recv()

    @pl.when(has_below)
    def _():
        for item in count_up:
            item.wait_recv()

    for item in locals_[5:]:
        item.wait()
    near_v = [vb[k, 0] for k in range(3)]
    far_v = [vb[k + 3, 0] for k in range(3)]
    mate_near, mate_far = jnp.where(x == 0, near_v[2], near_v[0]), jnp.where(x == 0, far_v[2], far_v[0])
    counts = near_v + far_v
    for i in (0, 1):
        for side in (0, 1):
            same = jnp.where(c == side, near_v[1], far_v[1])
            mate = jnp.where(c == side, mate_near, mate_far)
            counts.append(jnp.where(x == i, same, mate))
    counts = jnp.concatenate(
        [v.astype(jnp.float32) for v in counts] + [jnp.zeros((6, tok), jnp.float32)], axis=0
    ).astype(jnp.bfloat16)
    t_row = lax.broadcasted_iota(jnp.int32, (tok, tok), 0)
    t_col = lax.broadcasted_iota(jnp.int32, (tok, tok), 1)
    base_row = t_row // win * win
    pick = (t_col == base_row + (t_row - base_row + rim) % win).astype(jnp.float32).astype(jnp.bfloat16)
    counts = lax.dot_general(pick, counts, (((1,), (1,)), ((), ())), preferred_element_type=jnp.float32)
    t = lax.broadcasted_iota(jnp.int32, (tok, 1), 0)
    oi = (t // win).astype(jnp.float32) - (win - 1) / 2.0
    oj = ((t % win + rim) % win).astype(jnp.float32) - (win - 1) / 2.0
    gauss = jnp.exp(-(oi * oi + oj * oj) / (2.0 * SPREAD * SPREAD))
    weights = gauss * counts / 196.0
    at_col = lax.broadcasted_iota(jnp.int32, weights.shape, 1) % 2
    at_place = lax.broadcasted_iota(jnp.int32, weights.shape, 0) % win - tile
    kept = jnp.where(at_col == 0, at_place, tile - 1 - at_place) < rim
    wcol[...] = jnp.where(jnp.logical_or(at_place < 0, kept), weights, 0.0)
    grid = weights.reshape(win, win, weights.shape[1])
    near = grid[:, :tile].reshape(win * tile, weights.shape[1])
    far = grid[:, tile:].reshape(win * tile, weights.shape[1])
    u = lax.broadcasted_iota(jnp.int32, (win * tile, 1), 0) % tile
    fold_ok = jnp.where(c == 1, u, tile - 1 - u) < rim
    far = jnp.where(fold_ok, far, 0.0)
    low, high = rim * tile, (rim + tile) * tile
    near0, far0 = near[low:high, 1:2], far[low:high, 4:5]
    near_a = jnp.where(has_above, near[high:, 0:1], 0.0)
    far_a = jnp.where(has_above, far[high:, 3:4], 0.0)
    near_b = jnp.where(has_below, near[:low, 2:3], 0.0)
    far_b = jnp.where(has_below, far[:low, 5:6], 0.0)
    denom = near0 + far0 + jnp.concatenate([near_a + far_a, near_b + far_b], axis=0)

    def flat(lo, hi, a, b):
        return posr[lo:hi, a:b].reshape((hi - lo) * (b - a), width)

    total = denom * (
        eb[c, own_rows].astype(jnp.float32).reshape(tile * tile, width)
        + bo_ref[...].reshape(1, width)
    )
    total += near0 * flat(rim, rim + tile, 0, tile) + far0 * flat(rim, rim + tile, tile, win)
    base[...] = total
    base[0:low] += near_a * flat(rim + tile, win, 0, tile) + far_a * flat(rim + tile, win, tile, win)
    base[low:] += near_b * flat(0, rim, 0, tile) + far_b * flat(0, rim, tile, win)

    for k in (2, 1,):
        start(f"o{k}", wo_ref.at[:, ring], wo_at(r, ring), (g, 2 * away[k] + x, c), outer_only)

    early = len(pending)
    from_z("B", 2)
    for k in (2, 1, 3):
        start(f"o{k}", wo_ref.at[:, ring], wo_at(r, ring), (g, 2 * away[k] + x, c), inner)
    from_z("B", 1)
    arrived("exf", eb.at[other, mate_rows])
    lax.fori_loop(0, 6, norm_mate, 0)
    from_z("A", 3)
    for name, place_at, exists, direct in (("ht", top_rows, has_up, x == 1), ("hb", low_rows, has_down, x == 0)):
        here = eb.at[c, place_at]
        first = jnp.logical_and(exists, direct)
        arrived(name, here, first)
        start(f"{name}x", here, here, (g, rx, c), first)
        start(f"{name}f", here, here, to_core, first)
    from_z("B", 3)
    later = len(pending)
    arrived("ox", wo_at(rx, pl.ds(0, hd)))
    start("oxf", wo_all.at[rx, c], wo_all.at[rx, c], to_core)

    def out_from_z(k):
        here, side = wo_at(2 * away[k] + x, ring), wo_at(2 * away[k] + x, y_out)
        arrived(f"o{k}", here)
        start(f"ox{k}", here, here, (g, rx, c))
        start(f"oy{k}", side, side, to_y)
        start(f"od{k}", side, side, (1 - g, rx, c))
        if k == 2:
            start("of", here, here, (g, 2 * away[1] + x, c), inner, names.setdefault("o3", len(names) + 2 * team))

    def out_to_core(k):
        row, mate = 2 * away[k] + x, 2 * away[k] + 1 - x
        arrived(f"oy{k}", wo_at(row, y_in))
        start(f"oc{k}", wo_all.at[row, c], wo_all.at[row, c], to_core)
        arrived(f"ox{k}", wo_at(mate, ring))
        arrived(f"od{k}", wo_at(mate, y_in))
        start(f"om{k}", wo_all.at[mate, c], wo_all.at[mate, c], to_core)

    out_from_z(2)
    out_from_z(1)
    for name, place_at, exists, direct in (("ht", top_rows, has_up, x == 1), ("hb", low_rows, has_down, x == 0)):
        here = eb.at[c, place_at]
        second = jnp.logical_and(exists, jnp.logical_not(direct))
        arrived(f"{name}x", here, second)
        start(f"{name}g", here, here, to_core, second, slot(f"{name}f"))
    for name, place_at, when in (("ht", top_rows, has_up), ("hb", low_rows, has_down)):
        arrived(f"{name}f", eb.at[other, place_at], when)
    lax.fori_loop(0, 4, norm_rims, 0)
    flush(early)
    own_weights.wait()
    arrived("wc", wq_all.at[r, other])
    for a in (0, 1):
        arrived(f"xt{a}", wq_at(rx, core[a], theirs))
    for phase in ("A", "B"):
        from_y(phase, 1)

    b_own = bq_ref[...].reshape(1, qkv)
    b_parts = []
    for k in range(team):
        cut = [b_own[:, t * hd + k * part:t * hd + (k + 1) * part] for t in range(3)]
        rest = part - LANES
        b_parts.append(jnp.concatenate(
            [item[:, :LANES] for item in cut] + [item[:, LANES:] for item in cut]
            + [jnp.zeros((1, LANES - 3 * rest), jnp.float32)], axis=1))
    b_mine = jnp.where(x == 0, jnp.where(c == 0, b_parts[0], b_parts[1]), jnp.where(c == 0, b_parts[2], b_parts[3]))

    deep = width // 2

    def part_dot(w, which):
        at = pl.ds(pl.multiple_of(which * deep, LANES), deep)
        rows_at = pl.ds(which * (rows // 2), rows // 2)
        return jnp.dot(nrm[w, :, at], wq_all[rows_at].reshape(deep, packed), preferred_element_type=jnp.float32)

    def near_part(w, carry):
        early_qkv[w] = part_dot(w, z // 2) + b_mine
        return carry

    lax.fori_loop(0, team, near_part, 0)
    for phase in ("A", "B"):
        for k in (2, 3):
            from_y(phase, k)


    lane = lax.broadcasted_iota(jnp.int32, (1, 2 * LANES), 1)
    rest = part - LANES

    def attend(w):
        proj = part_dot(w, 1 - z // 2) + early_qkv[w]
        tail = proj[:, 3 * LANES:]
        queries = jnp.concatenate([proj[:, :LANES], tail], axis=1)
        keys = jnp.concatenate([proj[:, LANES:2 * LANES], pltpu.roll(tail, LANES - rest, 1)], axis=1)
        values = jnp.concatenate([proj[:, 2 * LANES:3 * LANES], pltpu.roll(tail, LANES - 2 * rest, 1)], axis=1)
        keys, values = keys.astype(jnp.bfloat16), values.astype(jnp.bfloat16)
        outs = []
        for h in range(HEADS // team):
            inside = jnp.logical_and(lane >= h * head, lane < (h + 1) * head)
            used = -(-(h + 1) * head // LANES) * LANES
            chosen = jnp.where(inside, queries, 0.0).astype(jnp.bfloat16)
            scores = lax.dot_general(
                chosen[:, :used], keys[:, :used], (((1,), (1,)), ((), ())), preferred_element_type=jnp.float32
            )
            expon = jnp.exp2((scores - jnp.max(scores, axis=-1, keepdims=True)) * (head ** (-0.5) * LOG2E))
            inverse = 1.0 / jnp.sum(expon, axis=-1, keepdims=True)
            outs.append(jnp.dot(expon.astype(jnp.bfloat16), values, preferred_element_type=jnp.float32) * inverse)
        mixed = jnp.where(lane < head, outs[0], jnp.where(lane < part, outs[1], 0.0))
        mixed = mixed.astype(jnp.bfloat16).astype(jnp.float32) * wcol[:, 6 + w:7 + w]
        return mixed.reshape(win, win, 2 * LANES)

    def flatten(value):
        return value.reshape(value.shape[0] * tile, 2 * LANES)

    def both(i):
        left, right = attend(2 * i), attend(2 * i + 1)
        return [left[:, :tile] + right[:, tile:], right[:, :tile] + left[:, tile:]]

    out_from_z(3)
    upper = both(0)
    for side in (0, 1):
        rims_out[0, side] = flatten(upper[side][:rim]).astype(jnp.bfloat16)
    for side in (0, 1):
        start(f"rt{side}", rims_out.at[0, side], rims_in.at[q], (g, lax.rem(2 * z + rows - 1, rows), side), has_up,
              rim_base + q)
    lower = both(1)
    for side in (0, 1):
        rims_out[1, side] = flatten(lower[side][rim + tile:]).astype(jnp.bfloat16)
    for side in (0, 1):
        start(f"rb{side}", rims_out.at[1, side], rims_in.at[q], (g, lax.rem(2 * z + 2, rows), side), has_down,
              rim_base + q)
    for side in (0, 1):
        first = jnp.concatenate([upper[side][rim:tile], upper[side][tile:rim + tile] + lower[side][:rim]], axis=0)
        second = jnp.concatenate([lower[side][rim:tile] + upper[side][rim + tile:], lower[side][tile:rim + tile]], axis=0)
        tiles_out[0, side] = flatten(first).astype(jnp.bfloat16)
        tiles_out[1, side] = flatten(second).astype(jnp.bfloat16)
    start("fx", tiles_out.at[1 - x, c], tiles_in.at[q], (g, rx, c), None, fold_base + q)
    start("fd", tiles_out.at[1 - x, other], tiles_in.at[q], (g, rx, other), None, fold_base + q)
    start("fc", tiles_out.at[x, other], tiles_in.at[q], to_core, None, fold_base + q)
    tiles_in[q] = tiles_out[x, c]

    flush(later - early)
    for k in (1, 2, 3):
        out_to_core(k)
    arrived("oc", wo_all.at[r, other])
    arrived("oxf", wo_all.at[rx, other])
    for k in (1, 2, 3):
        arrived(f"oc{k}", wo_all.at[2 * away[k] + x, other])
        arrived(f"om{k}", wo_all.at[2 * away[k] + 1 - x, other])

    for at in (2 * x + other, 2 * (1 - x) + c, 2 * (1 - x) + other):
        arrived("fc", tiles_in.at[at], None, fold_base + at)
    for at in range(team):
        arrived("fc", rims_in.at[at], outside, rim_base + at)

    sums = []
    for at in range(team):
        edge = rims_in[at].astype(jnp.float32)
        edge = jnp.concatenate([jnp.where(x == 0, edge, 0.0), jnp.where(x == 1, edge, 0.0)], axis=0)
        sums.append((tiles_in[at].astype(jnp.float32) + edge)[:, :part])
    merged = jnp.concatenate(sums, axis=1).astype(jnp.bfloat16)
    result = base[...] + lax.dot_general(
        merged, wo_all[...].reshape(width, hd), (((1,), (1,)), ((), ())), preferred_element_type=jnp.float32,
    )
    result = result / jnp.maximum(denom, FLOOR)
    out_ref[...] = result.reshape(tile, tile, width).astype(out_ref.dtype)

    flush(len(pending))

    @pl.when(has_above)
    def _():
        for item in count_up:
            item.wait_send()

    @pl.when(has_below)
    def _():
        for item in count_down:
            item.wait_send()


def fused(rows, embeddings, pos_embed, ln_gain, ln_bias, w_qkv, b_qkv, w_out, b_out, valid):
    tile, _, width = embeddings.shape
    win, rim = 2 * tile, tile // 2
    tok = win * win
    shard, qkv = w_qkv.shape
    hd = w_out.shape[1]
    team = 4
    packed = 4 * LANES
    bf16, f32 = jnp.bfloat16, jnp.float32
    vmem = pl.BlockSpec(memory_space=pltpu.VMEM)
    return pl.pallas_call(
        functools.partial(kernel, rows),
        out_shape=jax.ShapeDtypeStruct(embeddings.shape, bf16),
        in_specs=[pl.BlockSpec(memory_space=pltpu.HBM)] * 9,
        out_specs=vmem,
        scratch_shapes=[
            pltpu.VMEM((tok, width), bf16),
            pltpu.VMEM((width,), f32),
            pltpu.VMEM((width,), f32),
            pltpu.VMEM((qkv,), f32),
            pltpu.VMEM((width,), f32),
            pltpu.VMEM((shard, qkv), bf16),
            pltpu.VMEM((2, 2 * tile + 2 * rim, tile, width), bf16),
            pltpu.VMEM((6, 1, 1, tok), jnp.int32),
            pltpu.VMEM((team, shard, packed), bf16),
            pltpu.VMEM((rows, 2, shard, packed), bf16),
            pltpu.VMEM((rows, 2, shard, hd), bf16),
            pltpu.VMEM((team, tok, width), bf16),
            pltpu.VMEM((win, win, width), f32),
            pltpu.VMEM((tile * tile, width), f32),
            pltpu.VMEM((tok, 16), f32),
            pltpu.VMEM((2, 2, tile * tile, 2 * LANES), bf16),
            pltpu.VMEM((team, tile * tile, 2 * LANES), bf16),
            pltpu.VMEM((2, 2, rim * tile, 2 * LANES), bf16),
            pltpu.VMEM((team, rim * tile, 2 * LANES), bf16),
            pltpu.SemaphoreType.DMA((128,)),
            pltpu.SemaphoreType.DMA((128,)),
            pltpu.SemaphoreType.DMA((10,)),
            pltpu.VMEM((team, tok, packed), f32),
        ],
        compiler_params=pltpu.CompilerParams(
            collective_id=0, has_side_effects=True, vmem_limit_bytes=60000000
        ),
    )(
        embeddings, pos_embed, ln_gain, ln_bias, w_qkv, b_qkv, w_out, b_out, valid
    )


def shifted(value, axis, steps):
    count = lax.axis_size(axis)
    initial, last = (max(0, -steps), min(count, count - steps))
    return lax.ppermute(value, axis, [(source, source + steps) for source in range(initial, last)])


def extended(block, sides, width):
    for axis, dim in sides:
        count = lax.axis_size(axis)
        forward = [(i, i + 1) for i in range(count - 1)]
        backward = [(target, source) for source, target in forward]
        low = lax.ppermute(
            lax.slice_in_dim(block, block.shape[dim] - width, None, axis=dim), axis, forward
        )
        high = lax.ppermute(lax.slice_in_dim(block, 0, width, axis=dim), axis, backward)
        block = jnp.concatenate([low, block, high], axis=dim)
    return block


def layer_norm(inputs, ln_gain, ln_bias):
    centred = inputs - jnp.mean(inputs, axis=-1, keepdims=True)
    variance = jnp.mean(centred * centred, axis=-1, keepdims=True)
    return centred * lax.rsqrt(variance + EPSILON) * ln_gain + ln_bias


def gauss_table(win):
    offsets = jnp.arange(win, dtype=jnp.float32) - (win - 1) / 2.0
    squared = offsets[:, None] * offsets[:, None] + offsets[None, :] * offsets[None, :]
    return jnp.exp(-squared / (2.0 * SPREAD * SPREAD))


def attend(projected):
    rows_count = projected.shape[0]
    width = projected.shape[1] // 3
    head_size = width // HEADS
    queries = projected[:, :width].reshape(rows_count, HEADS, head_size)
    keys = projected[:, width : 2 * width].reshape(rows_count, HEADS, head_size)
    values = projected[:, 2 * width :].reshape(rows_count, HEADS, head_size)
    scores = jnp.einsum(
        "qhd,khd->hqk", queries, keys, preferred_element_type=jnp.float32
    ) * head_size ** (-0.5)
    highest = jnp.max(scores, axis=-1, keepdims=True)
    expon = jnp.exp(scores - highest)
    probs = (expon / jnp.sum(expon, axis=-1, keepdims=True)).astype(jnp.bfloat16)
    mixed = jnp.einsum("hqk,khd->qhd", probs, values, preferred_element_type=jnp.float32)
    return mixed.astype(jnp.bfloat16).reshape(rows_count, width)


def fold_rows(numerator, denominator, rim):
    from_next = (
        shifted(numerator[:rim].astype(jnp.bfloat16), "row", -1).astype(jnp.float32),
        shifted(denominator[:rim].astype(jnp.bfloat16), "row", -1).astype(jnp.float32),
    )
    from_prev = (
        shifted(numerator[-rim:].astype(jnp.bfloat16), "row", 1).astype(jnp.float32),
        shifted(denominator[-rim:].astype(jnp.bfloat16), "row", 1).astype(jnp.float32),
    )
    middle_num = numerator[rim:-rim]
    middle_den = denominator[rim:-rim]
    middle_num = middle_num.at[:rim].add(from_prev[0]).at[-rim:].add(from_next[0])
    middle_den = middle_den.at[:rim].add(from_prev[1]).at[-rim:].add(from_next[1])
    return (middle_num, middle_den)


def fold_cols(numerator, denominator, rim):
    from_next = (
        shifted(numerator[:, :rim].astype(jnp.bfloat16), "col", -1).astype(jnp.float32),
        shifted(denominator[:, :rim].astype(jnp.bfloat16), "col", -1).astype(jnp.float32),
    )
    from_prev = (
        shifted(numerator[:, -rim:].astype(jnp.bfloat16), "col", 1).astype(jnp.float32),
        shifted(denominator[:, -rim:].astype(jnp.bfloat16), "col", 1).astype(jnp.float32),
    )
    middle_num = numerator[:, rim:-rim] + jnp.concatenate([from_prev[0], from_next[0]], axis=1)
    middle_den = denominator[:, rim:-rim] + jnp.concatenate([from_prev[1], from_next[1]], axis=1)
    return (middle_num, middle_den)


def body(embeddings, pos_embed, ln_gain, ln_bias, w_qkv, b_qkv, w_out, b_out, valid):
    tile = embeddings.shape[1]
    tile_rows = embeddings.shape[0] // tile
    rim = tile // 2
    win = tile + 2 * rim
    rows_count = win * win
    width_model = embeddings.shape[2]
    window = extended(embeddings, (("row", 0), ("col", 1)), rim)
    stacked = jnp.stack([window], axis=0)
    inputs = stacked.reshape(tile_rows, rows_count, width_model).astype(
        jnp.float32
    ) + pos_embed.astype(jnp.float32)
    inputs = inputs.reshape(tile_rows * rows_count, width_model)
    normed = layer_norm(inputs, ln_gain, ln_bias).astype(jnp.bfloat16)
    projected = jnp.dot(
        normed,
        lax.all_gather(w_qkv, ("row", "col"), axis=0, tiled=True),
        preferred_element_type=jnp.float32,
    )
    projected = (
        (projected + b_qkv).astype(jnp.bfloat16).reshape(tile_rows, rows_count, w_qkv.shape[1])
    )
    attended = jax.vmap(attend)(projected).reshape(tile_rows * rows_count, -1)
    projected_out = lax.dot_general(
        attended,
        lax.all_gather(w_out, ("row", "col"), axis=0, tiled=True),
        (((1,), (1,)), ((), ())),
        preferred_element_type=jnp.float32,
    )
    hidden = inputs + projected_out + b_out
    gauss = gauss_table(win).reshape(1, rows_count)
    weight = gauss * valid.reshape(tile_rows, rows_count).astype(jnp.float32) / 196.0
    contrib = (weight.reshape(tile_rows * rows_count, 1) * hidden).reshape(
        tile_rows, win, win, width_model
    )
    weight_grid = weight.reshape(tile_rows, win, win)
    numerator = jnp.zeros((tile_rows * tile + 2 * rim, win, width_model), jnp.float32)
    denominator = jnp.zeros((tile_rows * tile + 2 * rim, win), jnp.float32)
    numerator = numerator.at[0:win].add(contrib[0])
    denominator = denominator.at[0:win].add(weight_grid[0])
    numerator, denominator = fold_rows(numerator, denominator, rim)
    numerator, denominator = fold_cols(numerator, denominator, rim)
    return (numerator / jnp.maximum(denominator, FLOOR)[:, :, None]).astype(jnp.bfloat16)


def solution(mesh):
    placed = (
        P(("groups", "row"), "col", None),
        P(),
        P(),
        P(),
        P(("row", "col"), None),
        P(),
        P(("row", "col"), None),
        P(),
        P(("groups", "row"), "col", None),
    )
    rows = mesh.shape["row"]

    def run(*arrays):
        embeddings, w_qkv = arrays[0], arrays[4]
        tile = embeddings.shape[1]
        whole_tiles = w_qkv.shape[0] % 16 == 0 and embeddings.shape[0] == tile == 8
        pairs = mesh.shape["groups"] == 2 and mesh.shape["col"] == 2
        if whole_tiles and pairs and rows == 8:
            return fused(rows, *arrays)
        return body(*arrays)

    return jax.shard_map(
        run,
        mesh=mesh,
        in_specs=placed,
        out_specs=P(("groups", "row"), "col", None),
        check_vma=False,
    )
```

```python
import functools

import jax
import jax.numpy as jnp
from jax import lax
from jax.experimental import pallas as pl
from jax.experimental.pallas import tpu as pltpu
from jax.sharding import PartitionSpec as P

HEADS = 8
EPSILON = 1e-06
SPREAD = 4.0
FLOOR = 0.25
LANES = 128
LOG2E = 1.4426950408889634
MESH = pl.DeviceIdType.MESH


def kernel(
    rows,
    emb_ref, pos_hbm, gain_hbm, bias_hbm, wq_ref, bq_hbm, wo_ref, bo_hbm, valid_ref,
    out_ref, pos_ref, gain_ref, bias_ref, bq_ref, bo_ref, wq_own,
    eb, vb, pack, wq_all, wo_all, nrm, posr, base, wcol, tiles_out, tiles_in,
    rims_out, rims_in, send_sems, recv_sems, local_sems, early_qkv,
):
    g, r, c = lax.axis_index("groups"), lax.axis_index("row"), lax.axis_index("col")
    tile, _, width = emb_ref.shape
    rim = tile // 2
    win = 2 * tile
    tok = win * win
    shard, qkv = wq_ref.shape
    hd = wo_ref.shape[1]
    head = hd // HEADS
    team = 4
    part = hd // team
    packed = pack.shape[2]
    x, z = r % 2, r // 2
    planes = rows // 2
    away = {1: z + 1 - 2 * (z % 2), 2: (z + 2) % planes, 3: planes - 1 - z}
    inner = jnp.logical_and(z > 0, z < planes - 1)
    rx, other = r + 1 - 2 * x, 1 - c
    q = 2 * x + c
    above, below = lax.rem(r + rows - 1, rows), lax.rem(r + 1, rows)
    has_above, has_below = r > 0, r < rows - 1
    has_up, has_down = z > 0, z < planes - 1
    outside = jnp.logical_and(has_above, has_below)
    facing = jnp.where(x == 0, above, below)
    to_core, to_y = (g, r, other), (1 - g, r, c)
    core = {0: c, 1: other}

    names = {}
    pending = []
    fold_base, rim_base = 0, team

    def copy(name, src, dst, device, recv=None):
        at = names.setdefault(name, len(names) + 2 * team)
        return pltpu.make_async_remote_copy(
            src_ref=src, dst_ref=dst, send_sem=send_sems.at[at],
            recv_sem=recv_sems.at[at if recv is None else recv],
            device_id=device, device_id_type=MESH,
        )

    def start(name, src, dst, device, when=None, recv=None):
        item = copy(name, src, dst, device, recv)
        pending.append((when, item))
        if when is None:
            item.start()
        else:
            pl.when(when)(item.start)

    def flush(count):
        for when, item in pending[:count]:
            if when is None:
                item.wait_send()
            else:
                pl.when(when)(item.wait_send)
        del pending[:count]

    def arrived(name, dst, when=None, recv=None):
        item = copy(name, dst, dst, to_core, recv)
        if when is None:
            item.wait_recv()
        else:
            pl.when(when)(item.wait_recv)

    own_rows, mate_rows = pl.ds(rim + tile * x, tile), pl.ds(rim + tile * (1 - x), tile)
    top_rows, low_rows = pl.ds(0, rim), pl.ds(rim + 2 * tile, rim)
    locals_ = []
    for src, dst in (
        (wq_ref, wq_own), (pos_hbm, pos_ref), (gain_hbm, gain_ref), (bias_hbm, bias_ref),
        (emb_ref, eb.at[c, own_rows]), (valid_ref, vb.at[1]), (bo_hbm, bo_ref), (bq_hbm, bq_ref),
        (wo_ref, wo_all.at[r, c]),
    ):
        item = pltpu.make_async_copy(src, dst, local_sems.at[len(locals_)])
        item.start()
        locals_.append(item)

    barrier = pltpu.get_barrier_semaphore()

    def greet(*device):
        pl.semaphore_signal(barrier, inc=1, device_id=device, device_id_type=MESH)

    for k in (2, 1):
        greet(g, 2 * away[k] + x, c)
        greet(g, 2 * away[k] + x, other)

    @pl.when(inner)
    def _():
        greet(g, 2 * away[3] + x, c)
        greet(g, 2 * away[3] + x, other)

    @pl.when(outside)
    def _():
        greet(g, facing, c)
        greet(g, facing, other)

    greet(1 - g, rx, c)
    greet(1 - g, r, c)
    greet(g, rx, c)
    greet(g, rx, other)
    greet(g, r, other)

    locals_[0].wait()
    own = wq_own[...].astype(jnp.float32)
    for k in range(team):
        cut = [own[:, t * hd + k * part:t * hd + (k + 1) * part] for t in range(3)]
        for t in range(3):
            pack[k, :, t * LANES:(t + 1) * LANES] = cut[t][:, :LANES].astype(jnp.bfloat16)
        rest = part - LANES
        pieces = [item[:, LANES:] for item in cut] + [jnp.zeros((shard, LANES - 3 * rest), jnp.float32)]
        pack[k, :, 3 * LANES:] = jnp.concatenate(pieces, axis=1).astype(jnp.bfloat16)

    pl.semaphore_wait(
        barrier, 9 + 2 * inner.astype(jnp.int32) + 2 * outside.astype(jnp.int32)
    )

    half_w = packed // 2
    mine = pl.ds(pl.multiple_of(g * half_w, LANES), half_w)
    theirs = pl.ds(pl.multiple_of((1 - g) * half_w, LANES), half_w)

    def wq_at(row, core_at, cols):
        return wq_all.at[row, core_at, :, cols]

    def reach(k):
        return None if k < 3 else inner

    for a in (0, 1):
        start(f"xm{a}", pack.at[2 * (1 - x) + core[a], :, mine], wq_at(r, c, mine), (g, rx, core[a]))
    for k in (1, 2, 3):
        for a in (0, 1):
            start(f"A{k}{a}", pack.at[2 * x + core[a], :, mine], wq_at(r, c, mine),
                  (g, 2 * away[k] + x, core[a]), reach(k))
    start("ec", emb_ref, eb.at[c, own_rows], to_core)
    start("ex", emb_ref, eb.at[c, own_rows], (g, rx, c))

    count_down = [copy("v0", valid_ref, vb.at[0], (g, below, c)), copy("v3", valid_ref, vb.at[3], (g, below, other))]
    count_up = [copy("v2", valid_ref, vb.at[2], (g, above, c)), copy("v5", valid_ref, vb.at[5], (g, above, other))]

    @pl.when(has_below)
    def _():
        for item in count_down:
            item.start()

    @pl.when(has_above)
    def _():
        for item in count_up:
            item.start()

    start("v4", valid_ref, vb.at[4], to_core)
    own_weights = pltpu.make_async_copy(pack.at[q], wq_all.at[r, c], local_sems.at[len(locals_)])
    own_weights.start()

    @pl.when(z == 0)
    def _():
        eb[0, 0:rim] = jnp.zeros((rim, tile, width), eb.dtype)
        eb[1, 0:rim] = jnp.zeros((rim, tile, width), eb.dtype)

    @pl.when(z == planes - 1)
    def _():
        eb[0, rim + 2 * tile:] = jnp.zeros((rim, tile, width), eb.dtype)
        eb[1, rim + 2 * tile:] = jnp.zeros((rim, tile, width), eb.dtype)

    @pl.when(r == 0)
    def _():
        vb[0] = jnp.zeros((1, 1, tok), vb.dtype)
        vb[3] = jnp.zeros((1, 1, tok), vb.dtype)

    @pl.when(r == rows - 1)
    def _():
        vb[2] = jnp.zeros((1, 1, tok), vb.dtype)
        vb[5] = jnp.zeros((1, 1, tok), vb.dtype)

    @pl.when(jnp.logical_not(outside))
    def _():
        rims_in[...] = jnp.zeros(rims_in.shape, rims_in.dtype)

    for item in locals_[1:5]:
        item.wait()
    gain, bias = gain_ref[...].reshape(1, width), bias_ref[...].reshape(1, width)
    per = rim

    def roll_block(block, carry):
        pos = pos_ref[pl.ds(pl.multiple_of(block * per * win, per * win), per * win)]
        pos = pos.astype(jnp.float32).reshape(per, win, width)
        posr[pl.ds(block * per, per)] = pltpu.roll(pos, win - rim, 1)
        return carry

    lax.fori_loop(0, win // per, roll_block, 0)
    place = lax.broadcasted_iota(jnp.int32, (per, tile, 1), 1)

    def norm_block(which, block, side):
        which = which + x * (1 - 2 * which)
        block = block + x * (win // per - 1 - 2 * block)
        at = pl.ds(which * tile + block * per, per)
        rim_ok = jnp.where(side == 0, place, tile - 1 - place) < rim
        left = eb[side, at].astype(jnp.float32)
        right = jnp.where(rim_ok, eb[1 - side, at].astype(jnp.float32), 0.0)
        v = (jnp.concatenate([left, right], axis=1) + posr[pl.ds(block * per, per)]).reshape(per * win, width)
        v = v - jnp.mean(v, axis=-1, keepdims=True)
        variance = jnp.mean(v * v, axis=-1, keepdims=True)
        v = v * lax.rsqrt(variance + EPSILON) * gain + bias
        there = pl.ds(pl.multiple_of(block * per * win, per * win), per * win)
        nrm[2 * which + side, there] = v.astype(jnp.bfloat16)

    def norm_own(n, carry):
        m = n // 2
        norm_block(m // 2, (m + 1) % 3, n % 2)
        return carry

    def norm_mate(n, carry):
        m = n // 2
        norm_block((m + 1) // 2, (m + 2) % 3 + 1, n % 2)
        return carry

    def norm_rims(n, carry):
        norm_block(n // 2, n // 2 * 3, n % 2)
        return carry

    def pair_at(row, cols):
        return wq_all.at[row, :, :, cols]

    def slot(name):
        return names.setdefault(name, len(names) + 2 * team)

    outer_only = jnp.logical_not(inner)

    def from_z(phase, k):
        row = 2 * away[k] + (x if phase == "A" else 1 - x)
        here = pair_at(row, mine)
        if phase == "A" and k == 1:
            for a in (0, 1):
                one = wq_at(row, core[a], mine)
                arrived(f"A1{a}", one)
                start(f"yA1{a}", one, one, to_y)
            return
        if phase == "B" and k > 1:
            for a in (0, 1):
                one = wq_at(row, core[a], mine)
                arrived(f"B{k}{a}", one)
                if k == 2:
                    start(f"fB{a}", one, one, (g, 2 * away[1] + x, c), inner, slot(f"B3{a}"))
                start(f"yB{k}{a}", one, one, to_y)
            return
        if phase == "A" and k == 2:
            for a in (0, 1):
                one = wq_at(row, core[a], mine)
                arrived(f"A2{a}", one)
        else:
            arrived(f"{phase}{k}", here, outer_only if phase == "A" else None)
            if phase == "A":
                for a in (0, 1):
                    arrived(f"A3{a}", wq_at(row, core[a], mine), inner)
        start(f"y{phase}{k}", here, here, to_y)
        if k == 2:
            start(f"f{phase}", here, here, (g, 2 * away[1] + x, c), inner, slot(f"{phase}3"))

    def from_y(phase, k):
        row = 2 * away[k] + (x if phase == "A" else 1 - x)
        if (phase, k) in (("A", 1), ("B", 2), ("B", 3)):
            for a in (0, 1):
                arrived(f"y{phase}{k}{a}", wq_at(row, core[a], theirs))
        else:
            arrived(f"y{phase}{k}", pair_at(row, theirs))

    arrived("ec", eb.at[other, own_rows])
    lax.fori_loop(0, 6, norm_own, 0)

    for a in (0, 1):
        arrived(f"xm{a}", wq_at(rx, core[a], mine))
    given = pair_at(rx, mine)
    gives_down = jnp.logical_and(x == 1, has_down)
    gives_up = jnp.logical_and(x == 0, has_up)
    halves = [wq_at(rx, core[a], mine) for a in (0, 1)]
    for a in (0, 1):
        start(f"B2{a}", halves[a], halves[a], (g, 2 * away[2] + x, c))
    start("B1", given, given, (g, 2 * away[1] + x, c))
    start("ht", emb_ref.at[pl.ds(tile - rim, rim)], eb.at[c, top_rows], (g, lax.rem(r + 2, rows), c), gives_down,
          slot("ht"))
    start("hb", emb_ref.at[pl.ds(0, rim)], eb.at[c, low_rows], (g, lax.rem(r + rows - 2, rows), c), gives_up,
          slot("hb"))
    for a in (0, 1):
        start(f"B3{a}", halves[a], halves[a], (g, 2 * away[3] + x, c), inner)
    for a in (0, 1):
        start(f"xt{a}", pack.at[2 * (1 - x) + core[a], :, theirs], wq_at(r, c, theirs), (g, rx, core[a]))
    start("wc", pack.at[2 * x + other], wq_all.at[r, c], to_core)
    start("ox", wo_ref, wo_all.at[r, c], (g, rx, c))
    start("oc", wo_ref, wo_all.at[r, c], to_core)

    units = hd // LANES
    side_w = units // 2 * LANES
    ring_w = hd - side_w
    ring = pl.ds(pl.multiple_of(g * side_w, LANES), ring_w)
    y_out = pl.ds(pl.multiple_of(g * ring_w, LANES), side_w)
    y_in = pl.ds(pl.multiple_of((1 - g) * ring_w, LANES), side_w)

    def wo_at(row, cols):
        return wo_all.at[row, c, :, cols]


    from_z("A", 1)
    from_z("A", 2)

    arrived("ex", eb.at[c, mate_rows])
    start("exf", eb.at[c, mate_rows], eb.at[c, mate_rows], to_core)
    arrived("v4", vb.at[4])

    @pl.when(has_above)
    def _():
        for item in count_down:
            item.wait_recv()

    @pl.when(has_below)
    def _():
        for item in count_up:
            item.wait_recv()

    for item in locals_[5:]:
        item.wait()
    near_v = [vb[k, 0] for k in range(3)]
    far_v = [vb[k + 3, 0] for k in range(3)]
    mate_near, mate_far = jnp.where(x == 0, near_v[2], near_v[0]), jnp.where(x == 0, far_v[2], far_v[0])
    counts = near_v + far_v
    for i in (0, 1):
        for side in (0, 1):
            same = jnp.where(c == side, near_v[1], far_v[1])
            mate = jnp.where(c == side, mate_near, mate_far)
            counts.append(jnp.where(x == i, same, mate))
    counts = jnp.concatenate(
        [v.astype(jnp.float32) for v in counts] + [jnp.zeros((6, tok), jnp.float32)], axis=0
    ).astype(jnp.bfloat16)
    t_row = lax.broadcasted_iota(jnp.int32, (tok, tok), 0)
    t_col = lax.broadcasted_iota(jnp.int32, (tok, tok), 1)
    base_row = t_row // win * win
    pick = (t_col == base_row + (t_row - base_row + rim) % win).astype(jnp.float32).astype(jnp.bfloat16)
    counts = lax.dot_general(pick, counts, (((1,), (1,)), ((), ())), preferred_element_type=jnp.float32)
    t = lax.broadcasted_iota(jnp.int32, (tok, 1), 0)
    oi = (t // win).astype(jnp.float32) - (win - 1) / 2.0
    oj = ((t % win + rim) % win).astype(jnp.float32) - (win - 1) / 2.0
    gauss = jnp.exp(-(oi * oi + oj * oj) / (2.0 * SPREAD * SPREAD))
    weights = gauss * counts / 196.0
    at_col = lax.broadcasted_iota(jnp.int32, weights.shape, 1) % 2
    at_place = lax.broadcasted_iota(jnp.int32, weights.shape, 0) % win - tile
    kept = jnp.where(at_col == 0, at_place, tile - 1 - at_place) < rim
    wcol[...] = jnp.where(jnp.logical_or(at_place < 0, kept), weights, 0.0)
    grid = weights.reshape(win, win, weights.shape[1])
    near = grid[:, :tile].reshape(win * tile, weights.shape[1])
    far = grid[:, tile:].reshape(win * tile, weights.shape[1])
    u = lax.broadcasted_iota(jnp.int32, (win * tile, 1), 0) % tile
    fold_ok = jnp.where(c == 1, u, tile - 1 - u) < rim
    far = jnp.where(fold_ok, far, 0.0)
    low, high = rim * tile, (rim + tile) * tile
    near0, far0 = near[low:high, 1:2], far[low:high, 4:5]
    near_a = jnp.where(has_above, near[high:, 0:1], 0.0)
    far_a = jnp.where(has_above, far[high:, 3:4], 0.0)
    near_b = jnp.where(has_below, near[:low, 2:3], 0.0)
    far_b = jnp.where(has_below, far[:low, 5:6], 0.0)
    denom = near0 + far0 + jnp.concatenate([near_a + far_a, near_b + far_b], axis=0)

    def flat(lo, hi, a, b):
        return posr[lo:hi, a:b].reshape((hi - lo) * (b - a), width)

    total = denom * (
        eb[c, own_rows].astype(jnp.float32).reshape(tile * tile, width)
        + bo_ref[...].reshape(1, width)
    )
    total += near0 * flat(rim, rim + tile, 0, tile) + far0 * flat(rim, rim + tile, tile, win)
    base[...] = total
    base[0:low] += near_a * flat(rim + tile, win, 0, tile) + far_a * flat(rim + tile, win, tile, win)
    base[low:] += near_b * flat(0, rim, 0, tile) + far_b * flat(0, rim, tile, win)

    for k in (2, 1,):
        start(f"o{k}", wo_ref.at[:, ring], wo_at(r, ring), (g, 2 * away[k] + x, c), outer_only)

    early = len(pending)
    from_z("B", 2)
    for k in (2, 1, 3):
        start(f"o{k}", wo_ref.at[:, ring], wo_at(r, ring), (g, 2 * away[k] + x, c), inner)
    from_z("B", 1)
    arrived("exf", eb.at[other, mate_rows])
    lax.fori_loop(0, 6, norm_mate, 0)
    from_z("A", 3)
    for name, place_at, exists, direct in (("ht", top_rows, has_up, x == 1), ("hb", low_rows, has_down, x == 0)):
        here = eb.at[c, place_at]
        first = jnp.logical_and(exists, direct)
        arrived(name, here, first)
        start(f"{name}x", here, here, (g, rx, c), first)
        start(f"{name}f", here, here, to_core, first)
    from_z("B", 3)
    later = len(pending)
    arrived("ox", wo_at(rx, pl.ds(0, hd)))
    start("oxf", wo_all.at[rx, c], wo_all.at[rx, c], to_core)

    def out_from_z(k):
        here, side = wo_at(2 * away[k] + x, ring), wo_at(2 * away[k] + x, y_out)
        arrived(f"o{k}", here)
        if k == 2:
            start("of", here, here, (g, 2 * away[1] + x, c), inner, names.setdefault("o3", len(names) + 2 * team))
        start(f"ox{k}", here, here, (g, rx, c))
        start(f"oy{k}", side, side, to_y)
        start(f"od{k}", side, side, (1 - g, rx, c))

    def out_to_core(k):
        row, mate = 2 * away[k] + x, 2 * away[k] + 1 - x
        arrived(f"oy{k}", wo_at(row, y_in))
        start(f"oc{k}", wo_all.at[row, c], wo_all.at[row, c], to_core)
        arrived(f"ox{k}", wo_at(mate, ring))
        arrived(f"od{k}", wo_at(mate, y_in))
        start(f"om{k}", wo_all.at[mate, c], wo_all.at[mate, c], to_core)

    out_from_z(2)
    out_from_z(1)
    for name, place_at, exists, direct in (("ht", top_rows, has_up, x == 1), ("hb", low_rows, has_down, x == 0)):
        here = eb.at[c, place_at]
        second = jnp.logical_and(exists, jnp.logical_not(direct))
        arrived(f"{name}x", here, second)
        start(f"{name}g", here, here, to_core, second, slot(f"{name}f"))
    for name, place_at, when in (("ht", top_rows, has_up), ("hb", low_rows, has_down)):
        arrived(f"{name}f", eb.at[other, place_at], when)
    lax.fori_loop(0, 4, norm_rims, 0)
    flush(early)
    own_weights.wait()
    arrived("wc", wq_all.at[r, other])
    for a in (0, 1):
        arrived(f"xt{a}", wq_at(rx, core[a], theirs))
    for phase in ("A", "B"):
        from_y(phase, 1)

    b_own = bq_ref[...].reshape(1, qkv)
    b_parts = []
    for k in range(team):
        cut = [b_own[:, t * hd + k * part:t * hd + (k + 1) * part] for t in range(3)]
        rest = part - LANES
        b_parts.append(jnp.concatenate(
            [item[:, :LANES] for item in cut] + [item[:, LANES:] for item in cut]
            + [jnp.zeros((1, LANES - 3 * rest), jnp.float32)], axis=1))
    b_mine = jnp.where(x == 0, jnp.where(c == 0, b_parts[0], b_parts[1]), jnp.where(c == 0, b_parts[2], b_parts[3]))

    deep = width // 2

    def part_dot(w, which):
        at = pl.ds(pl.multiple_of(which * deep, LANES), deep)
        rows_at = pl.ds(which * (rows // 2), rows // 2)
        return jnp.dot(nrm[w, :, at], wq_all[rows_at].reshape(deep, packed), preferred_element_type=jnp.float32)

    def near_part(w, carry):
        early_qkv[w] = part_dot(w, z // 2) + b_mine
        return carry

    lax.fori_loop(0, team, near_part, 0)
    for phase in ("A", "B"):
        for k in (2, 3):
            from_y(phase, k)


    lane = lax.broadcasted_iota(jnp.int32, (1, 2 * LANES), 1)
    rest = part - LANES

    def attend(w):
        proj = part_dot(w, 1 - z // 2) + early_qkv[w]
        tail = proj[:, 3 * LANES:]
        queries = jnp.concatenate([proj[:, :LANES], tail], axis=1)
        keys = jnp.concatenate([proj[:, LANES:2 * LANES], pltpu.roll(tail, LANES - rest, 1)], axis=1)
        values = jnp.concatenate([proj[:, 2 * LANES:3 * LANES], pltpu.roll(tail, LANES - 2 * rest, 1)], axis=1)
        keys, values = keys.astype(jnp.bfloat16), values.astype(jnp.bfloat16)
        outs = []
        for h in range(HEADS // team):
            inside = jnp.logical_and(lane >= h * head, lane < (h + 1) * head)
            used = -(-(h + 1) * head // LANES) * LANES
            chosen = jnp.where(inside, queries, 0.0).astype(jnp.bfloat16)
            scores = lax.dot_general(
                chosen[:, :used], keys[:, :used], (((1,), (1,)), ((), ())), preferred_element_type=jnp.float32
            )
            expon = jnp.exp2((scores - jnp.max(scores, axis=-1, keepdims=True)) * (head ** (-0.5) * LOG2E))
            inverse = 1.0 / jnp.sum(expon, axis=-1, keepdims=True)
            outs.append(jnp.dot(expon.astype(jnp.bfloat16), values, preferred_element_type=jnp.float32) * inverse)
        mixed = jnp.where(lane < head, outs[0], jnp.where(lane < part, outs[1], 0.0))
        mixed = mixed.astype(jnp.bfloat16).astype(jnp.float32) * wcol[:, 6 + w:7 + w]
        return mixed.reshape(win, win, 2 * LANES)

    def flatten(value):
        return value.reshape(value.shape[0] * tile, 2 * LANES)

    def both(i):
        left, right = attend(2 * i), attend(2 * i + 1)
        return [left[:, :tile] + right[:, tile:], right[:, :tile] + left[:, tile:]]

    out_from_z(3)
    upper = both(0)
    for side in (0, 1):
        rims_out[0, side] = flatten(upper[side][:rim]).astype(jnp.bfloat16)
    for side in (0, 1):
        start(f"rt{side}", rims_out.at[0, side], rims_in.at[q], (g, lax.rem(2 * z + rows - 1, rows), side), has_up,
              rim_base + q)
    lower = both(1)
    for side in (0, 1):
        rims_out[1, side] = flatten(lower[side][rim + tile:]).astype(jnp.bfloat16)
    for side in (0, 1):
        start(f"rb{side}", rims_out.at[1, side], rims_in.at[q], (g, lax.rem(2 * z + 2, rows), side), has_down,
              rim_base + q)
    for side in (0, 1):
        first = jnp.concatenate([upper[side][rim:tile], upper[side][tile:rim + tile] + lower[side][:rim]], axis=0)
        second = jnp.concatenate([lower[side][rim:tile] + upper[side][rim + tile:], lower[side][tile:rim + tile]], axis=0)
        tiles_out[0, side] = flatten(first).astype(jnp.bfloat16)
        tiles_out[1, side] = flatten(second).astype(jnp.bfloat16)
    start("fx", tiles_out.at[1 - x, c], tiles_in.at[q], (g, rx, c), None, fold_base + q)
    start("fd", tiles_out.at[1 - x, other], tiles_in.at[q], (g, rx, other), None, fold_base + q)
    start("fc", tiles_out.at[x, other], tiles_in.at[q], to_core, None, fold_base + q)
    tiles_in[q] = tiles_out[x, c]

    flush(later - early)
    for k in (1, 2, 3):
        out_to_core(k)
    arrived("oc", wo_all.at[r, other])
    arrived("oxf", wo_all.at[rx, other])
    for k in (1, 2, 3):
        arrived(f"oc{k}", wo_all.at[2 * away[k] + x, other])
        arrived(f"om{k}", wo_all.at[2 * away[k] + 1 - x, other])

    for at in (2 * x + other, 2 * (1 - x) + c, 2 * (1 - x) + other):
        arrived("fc", tiles_in.at[at], None, fold_base + at)
    for at in range(team):
        arrived("fc", rims_in.at[at], outside, rim_base + at)

    sums = []
    for at in range(team):
        edge = rims_in[at].astype(jnp.float32)
        edge = jnp.concatenate([jnp.where(x == 0, edge, 0.0), jnp.where(x == 1, edge, 0.0)], axis=0)
        sums.append((tiles_in[at].astype(jnp.float32) + edge)[:, :part])
    merged = jnp.concatenate(sums, axis=1).astype(jnp.bfloat16)
    result = base[...] + lax.dot_general(
        merged, wo_all[...].reshape(width, hd), (((1,), (1,)), ((), ())), preferred_element_type=jnp.float32,
    )
    result = result / jnp.maximum(denom, FLOOR)
    out_ref[...] = result.reshape(tile, tile, width).astype(out_ref.dtype)

    flush(len(pending))

    @pl.when(has_above)
    def _():
        for item in count_up:
            item.wait_send()

    @pl.when(has_below)
    def _():
        for item in count_down:
            item.wait_send()


def fused(rows, embeddings, pos_embed, ln_gain, ln_bias, w_qkv, b_qkv, w_out, b_out, valid):
    tile, _, width = embeddings.shape
    win, rim = 2 * tile, tile // 2
    tok = win * win
    shard, qkv = w_qkv.shape
    hd = w_out.shape[1]
    team = 4
    packed = 4 * LANES
    bf16, f32 = jnp.bfloat16, jnp.float32
    vmem = pl.BlockSpec(memory_space=pltpu.VMEM)
    return pl.pallas_call(
        functools.partial(kernel, rows),
        out_shape=jax.ShapeDtypeStruct(embeddings.shape, bf16),
        in_specs=[pl.BlockSpec(memory_space=pltpu.HBM)] * 9,
        out_specs=vmem,
        scratch_shapes=[
            pltpu.VMEM((tok, width), bf16),
            pltpu.VMEM((width,), f32),
            pltpu.VMEM((width,), f32),
            pltpu.VMEM((qkv,), f32),
            pltpu.VMEM((width,), f32),
            pltpu.VMEM((shard, qkv), bf16),
            pltpu.VMEM((2, 2 * tile + 2 * rim, tile, width), bf16),
            pltpu.VMEM((6, 1, 1, tok), jnp.int32),
            pltpu.VMEM((team, shard, packed), bf16),
            pltpu.VMEM((rows, 2, shard, packed), bf16),
            pltpu.VMEM((rows, 2, shard, hd), bf16),
            pltpu.VMEM((team, tok, width), bf16),
            pltpu.VMEM((win, win, width), f32),
            pltpu.VMEM((tile * tile, width), f32),
            pltpu.VMEM((tok, 16), f32),
            pltpu.VMEM((2, 2, tile * tile, 2 * LANES), bf16),
            pltpu.VMEM((team, tile * tile, 2 * LANES), bf16),
            pltpu.VMEM((2, 2, rim * tile, 2 * LANES), bf16),
            pltpu.VMEM((team, rim * tile, 2 * LANES), bf16),
            pltpu.SemaphoreType.DMA((128,)),
            pltpu.SemaphoreType.DMA((128,)),
            pltpu.SemaphoreType.DMA((10,)),
            pltpu.VMEM((team, tok, packed), f32),
        ],
        compiler_params=pltpu.CompilerParams(
            collective_id=0, has_side_effects=True, vmem_limit_bytes=60000000
        ),
    )(
        embeddings, pos_embed, ln_gain, ln_bias, w_qkv, b_qkv, w_out, b_out, valid
    )


def shifted(value, axis, steps):
    count = lax.axis_size(axis)
    initial, last = (max(0, -steps), min(count, count - steps))
    return lax.ppermute(value, axis, [(source, source + steps) for source in range(initial, last)])


def extended(block, sides, width):
    for axis, dim in sides:
        count = lax.axis_size(axis)
        forward = [(i, i + 1) for i in range(count - 1)]
        backward = [(target, source) for source, target in forward]
        low = lax.ppermute(
            lax.slice_in_dim(block, block.shape[dim] - width, None, axis=dim), axis, forward
        )
        high = lax.ppermute(lax.slice_in_dim(block, 0, width, axis=dim), axis, backward)
        block = jnp.concatenate([low, block, high], axis=dim)
    return block


def layer_norm(inputs, ln_gain, ln_bias):
    centred = inputs - jnp.mean(inputs, axis=-1, keepdims=True)
    variance = jnp.mean(centred * centred, axis=-1, keepdims=True)
    return centred * lax.rsqrt(variance + EPSILON) * ln_gain + ln_bias


def gauss_table(win):
    offsets = jnp.arange(win, dtype=jnp.float32) - (win - 1) / 2.0
    squared = offsets[:, None] * offsets[:, None] + offsets[None, :] * offsets[None, :]
    return jnp.exp(-squared / (2.0 * SPREAD * SPREAD))


def attend(projected):
    rows_count = projected.shape[0]
    width = projected.shape[1] // 3
    head_size = width // HEADS
    queries = projected[:, :width].reshape(rows_count, HEADS, head_size)
    keys = projected[:, width : 2 * width].reshape(rows_count, HEADS, head_size)
    values = projected[:, 2 * width :].reshape(rows_count, HEADS, head_size)
    scores = jnp.einsum(
        "qhd,khd->hqk", queries, keys, preferred_element_type=jnp.float32
    ) * head_size ** (-0.5)
    highest = jnp.max(scores, axis=-1, keepdims=True)
    expon = jnp.exp(scores - highest)
    probs = (expon / jnp.sum(expon, axis=-1, keepdims=True)).astype(jnp.bfloat16)
    mixed = jnp.einsum("hqk,khd->qhd", probs, values, preferred_element_type=jnp.float32)
    return mixed.astype(jnp.bfloat16).reshape(rows_count, width)


def fold_rows(numerator, denominator, rim):
    from_next = (
        shifted(numerator[:rim].astype(jnp.bfloat16), "row", -1).astype(jnp.float32),
        shifted(denominator[:rim].astype(jnp.bfloat16), "row", -1).astype(jnp.float32),
    )
    from_prev = (
        shifted(numerator[-rim:].astype(jnp.bfloat16), "row", 1).astype(jnp.float32),
        shifted(denominator[-rim:].astype(jnp.bfloat16), "row", 1).astype(jnp.float32),
    )
    middle_num = numerator[rim:-rim]
    middle_den = denominator[rim:-rim]
    middle_num = middle_num.at[:rim].add(from_prev[0]).at[-rim:].add(from_next[0])
    middle_den = middle_den.at[:rim].add(from_prev[1]).at[-rim:].add(from_next[1])
    return (middle_num, middle_den)


def fold_cols(numerator, denominator, rim):
    from_next = (
        shifted(numerator[:, :rim].astype(jnp.bfloat16), "col", -1).astype(jnp.float32),
        shifted(denominator[:, :rim].astype(jnp.bfloat16), "col", -1).astype(jnp.float32),
    )
    from_prev = (
        shifted(numerator[:, -rim:].astype(jnp.bfloat16), "col", 1).astype(jnp.float32),
        shifted(denominator[:, -rim:].astype(jnp.bfloat16), "col", 1).astype(jnp.float32),
    )
    middle_num = numerator[:, rim:-rim] + jnp.concatenate([from_prev[0], from_next[0]], axis=1)
    middle_den = denominator[:, rim:-rim] + jnp.concatenate([from_prev[1], from_next[1]], axis=1)
    return (middle_num, middle_den)


def body(embeddings, pos_embed, ln_gain, ln_bias, w_qkv, b_qkv, w_out, b_out, valid):
    tile = embeddings.shape[1]
    tile_rows = embeddings.shape[0] // tile
    rim = tile // 2
    win = tile + 2 * rim
    rows_count = win * win
    width_model = embeddings.shape[2]
    window = extended(embeddings, (("row", 0), ("col", 1)), rim)
    stacked = jnp.stack([window], axis=0)
    inputs = stacked.reshape(tile_rows, rows_count, width_model).astype(
        jnp.float32
    ) + pos_embed.astype(jnp.float32)
    inputs = inputs.reshape(tile_rows * rows_count, width_model)
    normed = layer_norm(inputs, ln_gain, ln_bias).astype(jnp.bfloat16)
    projected = jnp.dot(
        normed,
        lax.all_gather(w_qkv, ("row", "col"), axis=0, tiled=True),
        preferred_element_type=jnp.float32,
    )
    projected = (
        (projected + b_qkv).astype(jnp.bfloat16).reshape(tile_rows, rows_count, w_qkv.shape[1])
    )
    attended = jax.vmap(attend)(projected).reshape(tile_rows * rows_count, -1)
    projected_out = lax.dot_general(
        attended,
        lax.all_gather(w_out, ("row", "col"), axis=0, tiled=True),
        (((1,), (1,)), ((), ())),
        preferred_element_type=jnp.float32,
    )
    hidden = inputs + projected_out + b_out
    gauss = gauss_table(win).reshape(1, rows_count)
    weight = gauss * valid.reshape(tile_rows, rows_count).astype(jnp.float32) / 196.0
    contrib = (weight.reshape(tile_rows * rows_count, 1) * hidden).reshape(
        tile_rows, win, win, width_model
    )
    weight_grid = weight.reshape(tile_rows, win, win)
    numerator = jnp.zeros((tile_rows * tile + 2 * rim, win, width_model), jnp.float32)
    denominator = jnp.zeros((tile_rows * tile + 2 * rim, win), jnp.float32)
    numerator = numerator.at[0:win].add(contrib[0])
    denominator = denominator.at[0:win].add(weight_grid[0])
    numerator, denominator = fold_rows(numerator, denominator, rim)
    numerator, denominator = fold_cols(numerator, denominator, rim)
    return (numerator / jnp.maximum(denominator, FLOOR)[:, :, None]).astype(jnp.bfloat16)


def solution(mesh):
    placed = (
        P(("groups", "row"), "col", None),
        P(),
        P(),
        P(),
        P(("row", "col"), None),
        P(),
        P(("row", "col"), None),
        P(),
        P(("groups", "row"), "col", None),
    )
    rows = mesh.shape["row"]

    def run(*arrays):
        embeddings, w_qkv = arrays[0], arrays[4]
        tile = embeddings.shape[1]
        whole_tiles = w_qkv.shape[0] % 16 == 0 and embeddings.shape[0] == tile == 8
        pairs = mesh.shape["groups"] == 2 and mesh.shape["col"] == 2
        if whole_tiles and pairs and rows == 8:
            return fused(rows, *arrays)
        return body(*arrays)

    return jax.shard_map(
        run,
        mesh=mesh,
        in_specs=placed,
        out_specs=P(("groups", "row"), "col", None),
        check_vma=False,
    )
```

```python
import functools

import jax
import jax.numpy as jnp
from jax import lax
from jax.experimental import pallas as pl
from jax.experimental.pallas import tpu as pltpu
from jax.sharding import PartitionSpec as P

HEADS = 8
EPSILON = 1e-06
SPREAD = 4.0
FLOOR = 0.25
LANES = 128
LOG2E = 1.4426950408889634
MESH = pl.DeviceIdType.MESH


def kernel(
    rows,
    emb_ref, pos_hbm, gain_hbm, bias_hbm, wq_ref, bq_hbm, wo_ref, bo_hbm, valid_ref,
    out_ref, pos_ref, gain_ref, bias_ref, bq_ref, bo_ref, wq_own,
    eb, vb, pack, wq_all, wo_all, nrm, posr, base, wcol, tiles_out, tiles_in,
    rims_out, rims_in, send_sems, recv_sems, local_sems, early_qkv,
):
    g, r, c = lax.axis_index("groups"), lax.axis_index("row"), lax.axis_index("col")
    tile, _, width = emb_ref.shape
    rim = tile // 2
    win = 2 * tile
    tok = win * win
    shard, qkv = wq_ref.shape
    hd = wo_ref.shape[1]
    head = hd // HEADS
    team = 4
    part = hd // team
    packed = pack.shape[2]
    x, z = r % 2, r // 2
    planes = rows // 2
    away = {1: z + 1 - 2 * (z % 2), 2: (z + 2) % planes, 3: planes - 1 - z}
    inner = jnp.logical_and(z > 0, z < planes - 1)
    rx, other = r + 1 - 2 * x, 1 - c
    q = 2 * x + c
    above, below = lax.rem(r + rows - 1, rows), lax.rem(r + 1, rows)
    has_above, has_below = r > 0, r < rows - 1
    has_up, has_down = z > 0, z < planes - 1
    outside = jnp.logical_and(has_above, has_below)
    facing = jnp.where(x == 0, above, below)
    to_core, to_y = (g, r, other), (1 - g, r, c)
    core = {0: c, 1: other}

    names = {}
    pending = []
    fold_base, rim_base = 0, team

    def copy(name, src, dst, device, recv=None):
        at = names.setdefault(name, len(names) + 2 * team)
        return pltpu.make_async_remote_copy(
            src_ref=src, dst_ref=dst, send_sem=send_sems.at[at],
            recv_sem=recv_sems.at[at if recv is None else recv],
            device_id=device, device_id_type=MESH,
        )

    def start(name, src, dst, device, when=None, recv=None):
        item = copy(name, src, dst, device, recv)
        pending.append((when, item))
        if when is None:
            item.start()
        else:
            pl.when(when)(item.start)

    def flush(count):
        for when, item in pending[:count]:
            if when is None:
                item.wait_send()
            else:
                pl.when(when)(item.wait_send)
        del pending[:count]

    def arrived(name, dst, when=None, recv=None):
        item = copy(name, dst, dst, to_core, recv)
        if when is None:
            item.wait_recv()
        else:
            pl.when(when)(item.wait_recv)

    own_rows, mate_rows = pl.ds(rim + tile * x, tile), pl.ds(rim + tile * (1 - x), tile)
    top_rows, low_rows = pl.ds(0, rim), pl.ds(rim + 2 * tile, rim)
    locals_ = []
    for src, dst in (
        (wq_ref, wq_own), (pos_hbm, pos_ref), (gain_hbm, gain_ref), (bias_hbm, bias_ref),
        (emb_ref, eb.at[c, own_rows]), (valid_ref, vb.at[1]), (bo_hbm, bo_ref), (bq_hbm, bq_ref),
        (wo_ref, wo_all.at[r, c]),
    ):
        item = pltpu.make_async_copy(src, dst, local_sems.at[len(locals_)])
        item.start()
        locals_.append(item)

    barrier = pltpu.get_barrier_semaphore()

    def greet(*device):
        pl.semaphore_signal(barrier, inc=1, device_id=device, device_id_type=MESH)

    for k in (2, 1):
        greet(g, 2 * away[k] + x, c)
        greet(g, 2 * away[k] + x, other)

    @pl.when(inner)
    def _():
        greet(g, 2 * away[3] + x, c)
        greet(g, 2 * away[3] + x, other)

    @pl.when(outside)
    def _():
        greet(g, facing, c)
        greet(g, facing, other)

    greet(1 - g, rx, c)
    greet(1 - g, r, c)
    greet(g, rx, c)
    greet(g, rx, other)
    greet(g, r, other)

    locals_[0].wait()
    own = wq_own[...].astype(jnp.float32)
    for k in range(team):
        cut = [own[:, t * hd + k * part:t * hd + (k + 1) * part] for t in range(3)]
        for t in range(3):
            pack[k, :, t * LANES:(t + 1) * LANES] = cut[t][:, :LANES].astype(jnp.bfloat16)
        rest = part - LANES
        pieces = [item[:, LANES:] for item in cut] + [jnp.zeros((shard, LANES - 3 * rest), jnp.float32)]
        pack[k, :, 3 * LANES:] = jnp.concatenate(pieces, axis=1).astype(jnp.bfloat16)

    pl.semaphore_wait(
        barrier, 9 + 2 * inner.astype(jnp.int32) + 2 * outside.astype(jnp.int32)
    )

    half_w = packed // 2
    mine = pl.ds(pl.multiple_of(g * half_w, LANES), half_w)
    theirs = pl.ds(pl.multiple_of((1 - g) * half_w, LANES), half_w)

    def wq_at(row, core_at, cols):
        return wq_all.at[row, core_at, :, cols]

    def reach(k):
        return None if k < 3 else inner

    for a in (0, 1):
        start(f"xm{a}", pack.at[2 * (1 - x) + core[a], :, mine], wq_at(r, c, mine), (g, rx, core[a]))
    for k in (1, 2, 3):
        for a in (0, 1):
            start(f"A{k}{a}", pack.at[2 * x + core[a], :, mine], wq_at(r, c, mine),
                  (g, 2 * away[k] + x, core[a]), reach(k))
    start("ec", emb_ref, eb.at[c, own_rows], to_core)
    start("ex", emb_ref, eb.at[c, own_rows], (g, rx, c))

    count_down = [copy("v0", valid_ref, vb.at[0], (g, below, c)), copy("v3", valid_ref, vb.at[3], (g, below, other))]
    count_up = [copy("v2", valid_ref, vb.at[2], (g, above, c)), copy("v5", valid_ref, vb.at[5], (g, above, other))]

    @pl.when(has_below)
    def _():
        for item in count_down:
            item.start()

    @pl.when(has_above)
    def _():
        for item in count_up:
            item.start()

    start("v4", valid_ref, vb.at[4], to_core)
    own_weights = pltpu.make_async_copy(pack.at[q], wq_all.at[r, c], local_sems.at[len(locals_)])
    own_weights.start()

    @pl.when(z == 0)
    def _():
        eb[0, 0:rim] = jnp.zeros((rim, tile, width), eb.dtype)
        eb[1, 0:rim] = jnp.zeros((rim, tile, width), eb.dtype)

    @pl.when(z == planes - 1)
    def _():
        eb[0, rim + 2 * tile:] = jnp.zeros((rim, tile, width), eb.dtype)
        eb[1, rim + 2 * tile:] = jnp.zeros((rim, tile, width), eb.dtype)

    @pl.when(r == 0)
    def _():
        vb[0] = jnp.zeros((1, 1, tok), vb.dtype)
        vb[3] = jnp.zeros((1, 1, tok), vb.dtype)

    @pl.when(r == rows - 1)
    def _():
        vb[2] = jnp.zeros((1, 1, tok), vb.dtype)
        vb[5] = jnp.zeros((1, 1, tok), vb.dtype)

    @pl.when(jnp.logical_not(outside))
    def _():
        rims_in[...] = jnp.zeros(rims_in.shape, rims_in.dtype)

    for item in locals_[1:5]:
        item.wait()
    gain, bias = gain_ref[...].reshape(1, width), bias_ref[...].reshape(1, width)
    per = rim

    def roll_block(block, carry):
        pos = pos_ref[pl.ds(pl.multiple_of(block * per * win, per * win), per * win)]
        pos = pos.astype(jnp.float32).reshape(per, win, width)
        posr[pl.ds(block * per, per)] = pltpu.roll(pos, win - rim, 1)
        return carry

    lax.fori_loop(0, win // per, roll_block, 0)
    place = lax.broadcasted_iota(jnp.int32, (per, tile, 1), 1)

    def norm_block(which, block, side):
        which = which + x * (1 - 2 * which)
        block = block + x * (win // per - 1 - 2 * block)
        at = pl.ds(which * tile + block * per, per)
        rim_ok = jnp.where(side == 0, place, tile - 1 - place) < rim
        left = eb[side, at].astype(jnp.float32)
        right = jnp.where(rim_ok, eb[1 - side, at].astype(jnp.float32), 0.0)
        v = (jnp.concatenate([left, right], axis=1) + posr[pl.ds(block * per, per)]).reshape(per * win, width)
        v = v - jnp.mean(v, axis=-1, keepdims=True)
        variance = jnp.mean(v * v, axis=-1, keepdims=True)
        v = v * lax.rsqrt(variance + EPSILON) * gain + bias
        there = pl.ds(pl.multiple_of(block * per * win, per * win), per * win)
        nrm[2 * which + side, there] = v.astype(jnp.bfloat16)

    def norm_own(n, carry):
        m = n // 2
        norm_block(m // 2, (m + 1) % 3, n % 2)
        return carry

    def norm_mate(n, carry):
        m = n // 2
        norm_block((m + 1) // 2, (m + 2) % 3 + 1, n % 2)
        return carry

    def norm_rims(n, carry):
        norm_block(n // 2, n // 2 * 3, n % 2)
        return carry

    def pair_at(row, cols):
        return wq_all.at[row, :, :, cols]

    def slot(name):
        return names.setdefault(name, len(names) + 2 * team)

    outer_only = jnp.logical_not(inner)

    def from_z(phase, k):
        row = 2 * away[k] + (x if phase == "A" else 1 - x)
        here = pair_at(row, mine)
        if phase == "A" and k == 1:
            for a in (0, 1):
                one = wq_at(row, core[a], mine)
                arrived(f"A1{a}", one)
                start(f"yA1{a}", one, one, to_y)
            return
        if phase == "B" and k > 1:
            for a in (0, 1):
                one = wq_at(row, core[a], mine)
                arrived(f"B{k}{a}", one)
                if k == 2:
                    start(f"fB{a}", one, one, (g, 2 * away[1] + x, c), inner, slot(f"B3{a}"))
                start(f"yB{k}{a}", one, one, to_y)
            return
        if phase == "A" and k == 2:
            for a in (0, 1):
                one = wq_at(row, core[a], mine)
                arrived(f"A2{a}", one)
        else:
            arrived(f"{phase}{k}", here, outer_only if phase == "A" else None)
            if phase == "A":
                for a in (0, 1):
                    arrived(f"A3{a}", wq_at(row, core[a], mine), inner)
        start(f"y{phase}{k}", here, here, to_y)
        if k == 2:
            start(f"f{phase}", here, here, (g, 2 * away[1] + x, c), inner, slot(f"{phase}3"))

    def from_y(phase, k):
        row = 2 * away[k] + (x if phase == "A" else 1 - x)
        if (phase, k) in (("A", 1), ("B", 2), ("B", 3)):
            for a in (0, 1):
                arrived(f"y{phase}{k}{a}", wq_at(row, core[a], theirs))
        else:
            arrived(f"y{phase}{k}", pair_at(row, theirs))

    arrived("ec", eb.at[other, own_rows])
    lax.fori_loop(0, 3, norm_own, 0)

    for a in (0, 1):
        arrived(f"xm{a}", wq_at(rx, core[a], mine))
    given = pair_at(rx, mine)
    gives_down = jnp.logical_and(x == 1, has_down)
    gives_up = jnp.logical_and(x == 0, has_up)
    halves = [wq_at(rx, core[a], mine) for a in (0, 1)]
    for a in (0, 1):
        start(f"B2{a}", halves[a], halves[a], (g, 2 * away[2] + x, c))
    start("B1", given, given, (g, 2 * away[1] + x, c))
    start("ht", emb_ref.at[pl.ds(tile - rim, rim)], eb.at[c, top_rows], (g, lax.rem(r + 2, rows), c), gives_down,
          slot("ht"))
    start("hb", emb_ref.at[pl.ds(0, rim)], eb.at[c, low_rows], (g, lax.rem(r + rows - 2, rows), c), gives_up,
          slot("hb"))
    for a in (0, 1):
        start(f"B3{a}", halves[a], halves[a], (g, 2 * away[3] + x, c), inner)
    for a in (0, 1):
        start(f"xt{a}", pack.at[2 * (1 - x) + core[a], :, theirs], wq_at(r, c, theirs), (g, rx, core[a]))
    start("wc", pack.at[2 * x + other], wq_all.at[r, c], to_core)
    start("ox", wo_ref, wo_all.at[r, c], (g, rx, c))
    start("oc", wo_ref, wo_all.at[r, c], to_core)
    lax.fori_loop(3, 6, norm_own, 0)

    units = hd // LANES
    side_w = units // 2 * LANES
    ring_w = hd - side_w
    ring = pl.ds(pl.multiple_of(g * side_w, LANES), ring_w)
    y_out = pl.ds(pl.multiple_of(g * ring_w, LANES), side_w)
    y_in = pl.ds(pl.multiple_of((1 - g) * ring_w, LANES), side_w)

    def wo_at(row, cols):
        return wo_all.at[row, c, :, cols]


    from_z("A", 1)
    from_z("A", 2)

    arrived("ex", eb.at[c, mate_rows])
    start("exf", eb.at[c, mate_rows], eb.at[c, mate_rows], to_core)
    arrived("v4", vb.at[4])

    @pl.when(has_above)
    def _():
        for item in count_down:
            item.wait_recv()

    @pl.when(has_below)
    def _():
        for item in count_up:
            item.wait_recv()

    for item in locals_[5:]:
        item.wait()
    near_v = [vb[k, 0] for k in range(3)]
    far_v = [vb[k + 3, 0] for k in range(3)]
    mate_near, mate_far = jnp.where(x == 0, near_v[2], near_v[0]), jnp.where(x == 0, far_v[2], far_v[0])
    counts = near_v + far_v
    for i in (0, 1):
        for side in (0, 1):
            same = jnp.where(c == side, near_v[1], far_v[1])
            mate = jnp.where(c == side, mate_near, mate_far)
            counts.append(jnp.where(x == i, same, mate))
    counts = jnp.concatenate(
        [v.astype(jnp.float32) for v in counts] + [jnp.zeros((6, tok), jnp.float32)], axis=0
    ).astype(jnp.bfloat16)
    t_row = lax.broadcasted_iota(jnp.int32, (tok, tok), 0)
    t_col = lax.broadcasted_iota(jnp.int32, (tok, tok), 1)
    base_row = t_row // win * win
    pick = (t_col == base_row + (t_row - base_row + rim) % win).astype(jnp.float32).astype(jnp.bfloat16)
    counts = lax.dot_general(pick, counts, (((1,), (1,)), ((), ())), preferred_element_type=jnp.float32)
    t = lax.broadcasted_iota(jnp.int32, (tok, 1), 0)
    oi = (t // win).astype(jnp.float32) - (win - 1) / 2.0
    oj = ((t % win + rim) % win).astype(jnp.float32) - (win - 1) / 2.0
    gauss = jnp.exp(-(oi * oi + oj * oj) / (2.0 * SPREAD * SPREAD))
    weights = gauss * counts / 196.0
    at_col = lax.broadcasted_iota(jnp.int32, weights.shape, 1) % 2
    at_place = lax.broadcasted_iota(jnp.int32, weights.shape, 0) % win - tile
    kept = jnp.where(at_col == 0, at_place, tile - 1 - at_place) < rim
    wcol[...] = jnp.where(jnp.logical_or(at_place < 0, kept), weights, 0.0)
    grid = weights.reshape(win, win, weights.shape[1])
    near = grid[:, :tile].reshape(win * tile, weights.shape[1])
    far = grid[:, tile:].reshape(win * tile, weights.shape[1])
    u = lax.broadcasted_iota(jnp.int32, (win * tile, 1), 0) % tile
    fold_ok = jnp.where(c == 1, u, tile - 1 - u) < rim
    far = jnp.where(fold_ok, far, 0.0)
    low, high = rim * tile, (rim + tile) * tile
    near0, far0 = near[low:high, 1:2], far[low:high, 4:5]
    near_a = jnp.where(has_above, near[high:, 0:1], 0.0)
    far_a = jnp.where(has_above, far[high:, 3:4], 0.0)
    near_b = jnp.where(has_below, near[:low, 2:3], 0.0)
    far_b = jnp.where(has_below, far[:low, 5:6], 0.0)
    denom = near0 + far0 + jnp.concatenate([near_a + far_a, near_b + far_b], axis=0)

    def flat(lo, hi, a, b):
        return posr[lo:hi, a:b].reshape((hi - lo) * (b - a), width)

    total = denom * (
        eb[c, own_rows].astype(jnp.float32).reshape(tile * tile, width)
        + bo_ref[...].reshape(1, width)
    )
    total += near0 * flat(rim, rim + tile, 0, tile) + far0 * flat(rim, rim + tile, tile, win)
    base[...] = total
    base[0:low] += near_a * flat(rim + tile, win, 0, tile) + far_a * flat(rim + tile, win, tile, win)
    base[low:] += near_b * flat(0, rim, 0, tile) + far_b * flat(0, rim, tile, win)

    for k in (2, 1,):
        start(f"o{k}", wo_ref.at[:, ring], wo_at(r, ring), (g, 2 * away[k] + x, c), outer_only)

    early = len(pending)
    from_z("B", 2)
    for k in (2, 1, 3):
        start(f"o{k}", wo_ref.at[:, ring], wo_at(r, ring), (g, 2 * away[k] + x, c), inner)
    from_z("B", 1)
    arrived("exf", eb.at[other, mate_rows])
    lax.fori_loop(0, 6, norm_mate, 0)
    from_z("A", 3)
    for name, place_at, exists, direct in (("ht", top_rows, has_up, x == 1), ("hb", low_rows, has_down, x == 0)):
        here = eb.at[c, place_at]
        first = jnp.logical_and(exists, direct)
        arrived(name, here, first)
        start(f"{name}x", here, here, (g, rx, c), first)
        start(f"{name}f", here, here, to_core, first)
    from_z("B", 3)
    later = len(pending)
    arrived("ox", wo_at(rx, pl.ds(0, hd)))
    start("oxf", wo_all.at[rx, c], wo_all.at[rx, c], to_core)

    def out_from_z(k):
        here, side = wo_at(2 * away[k] + x, ring), wo_at(2 * away[k] + x, y_out)
        arrived(f"o{k}", here)
        if k == 2:
            start("of", here, here, (g, 2 * away[1] + x, c), inner, names.setdefault("o3", len(names) + 2 * team))
        start(f"ox{k}", here, here, (g, rx, c))
        start(f"oy{k}", side, side, to_y)
        start(f"od{k}", side, side, (1 - g, rx, c))

    def out_to_core(k):
        row, mate = 2 * away[k] + x, 2 * away[k] + 1 - x
        arrived(f"oy{k}", wo_at(row, y_in))
        start(f"oc{k}", wo_all.at[row, c], wo_all.at[row, c], to_core)
        arrived(f"ox{k}", wo_at(mate, ring))
        arrived(f"od{k}", wo_at(mate, y_in))
        start(f"om{k}", wo_all.at[mate, c], wo_all.at[mate, c], to_core)

    out_from_z(2)
    out_from_z(1)
    for name, place_at, exists, direct in (("ht", top_rows, has_up, x == 1), ("hb", low_rows, has_down, x == 0)):
        here = eb.at[c, place_at]
        second = jnp.logical_and(exists, jnp.logical_not(direct))
        arrived(f"{name}x", here, second)
        start(f"{name}g", here, here, to_core, second, slot(f"{name}f"))
    for name, place_at, when in (("ht", top_rows, has_up), ("hb", low_rows, has_down)):
        arrived(f"{name}f", eb.at[other, place_at], when)
    lax.fori_loop(0, 4, norm_rims, 0)
    flush(early)
    own_weights.wait()
    arrived("wc", wq_all.at[r, other])
    for a in (0, 1):
        arrived(f"xt{a}", wq_at(rx, core[a], theirs))
    for phase in ("A", "B"):
        from_y(phase, 1)

    b_own = bq_ref[...].reshape(1, qkv)
    b_parts = []
    for k in range(team):
        cut = [b_own[:, t * hd + k * part:t * hd + (k + 1) * part] for t in range(3)]
        rest = part - LANES
        b_parts.append(jnp.concatenate(
            [item[:, :LANES] for item in cut] + [item[:, LANES:] for item in cut]
            + [jnp.zeros((1, LANES - 3 * rest), jnp.float32)], axis=1))
    b_mine = jnp.where(x == 0, jnp.where(c == 0, b_parts[0], b_parts[1]), jnp.where(c == 0, b_parts[2], b_parts[3]))

    deep = width // 2

    def part_dot(w, which):
        at = pl.ds(pl.multiple_of(which * deep, LANES), deep)
        rows_at = pl.ds(which * (rows // 2), rows // 2)
        return jnp.dot(nrm[w, :, at], wq_all[rows_at].reshape(deep, packed), preferred_element_type=jnp.float32)

    def near_part(w, carry):
        early_qkv[w] = part_dot(w, z // 2) + b_mine
        return carry

    lax.fori_loop(0, team, near_part, 0)
    for phase in ("A", "B"):
        for k in (2, 3):
            from_y(phase, k)


    lane = lax.broadcasted_iota(jnp.int32, (1, 2 * LANES), 1)
    rest = part - LANES

    def attend(w):
        proj = part_dot(w, 1 - z // 2) + early_qkv[w]
        tail = proj[:, 3 * LANES:]
        queries = jnp.concatenate([proj[:, :LANES], tail], axis=1)
        keys = jnp.concatenate([proj[:, LANES:2 * LANES], pltpu.roll(tail, LANES - rest, 1)], axis=1)
        values = jnp.concatenate([proj[:, 2 * LANES:3 * LANES], pltpu.roll(tail, LANES - 2 * rest, 1)], axis=1)
        keys, values = keys.astype(jnp.bfloat16), values.astype(jnp.bfloat16)
        outs = []
        for h in range(HEADS // team):
            inside = jnp.logical_and(lane >= h * head, lane < (h + 1) * head)
            used = -(-(h + 1) * head // LANES) * LANES
            chosen = jnp.where(inside, queries, 0.0).astype(jnp.bfloat16)
            scores = lax.dot_general(
                chosen[:, :used], keys[:, :used], (((1,), (1,)), ((), ())), preferred_element_type=jnp.float32
            )
            expon = jnp.exp2((scores - jnp.max(scores, axis=-1, keepdims=True)) * (head ** (-0.5) * LOG2E))
            inverse = 1.0 / jnp.sum(expon, axis=-1, keepdims=True)
            outs.append(jnp.dot(expon.astype(jnp.bfloat16), values, preferred_element_type=jnp.float32) * inverse)
        mixed = jnp.where(lane < head, outs[0], jnp.where(lane < part, outs[1], 0.0))
        mixed = mixed.astype(jnp.bfloat16).astype(jnp.float32) * wcol[:, 6 + w:7 + w]
        return mixed.reshape(win, win, 2 * LANES)

    def flatten(value):
        return value.reshape(value.shape[0] * tile, 2 * LANES)

    def both(i):
        left, right = attend(2 * i), attend(2 * i + 1)
        return [left[:, :tile] + right[:, tile:], right[:, :tile] + left[:, tile:]]

    out_from_z(3)
    upper = both(0)
    for side in (0, 1):
        rims_out[0, side] = flatten(upper[side][:rim]).astype(jnp.bfloat16)
    for side in (0, 1):
        start(f"rt{side}", rims_out.at[0, side], rims_in.at[q], (g, lax.rem(2 * z + rows - 1, rows), side), has_up,
              rim_base + q)
    lower = both(1)
    for side in (0, 1):
        rims_out[1, side] = flatten(lower[side][rim + tile:]).astype(jnp.bfloat16)
    for side in (0, 1):
        start(f"rb{side}", rims_out.at[1, side], rims_in.at[q], (g, lax.rem(2 * z + 2, rows), side), has_down,
              rim_base + q)
    for side in (0, 1):
        first = jnp.concatenate([upper[side][rim:tile], upper[side][tile:rim + tile] + lower[side][:rim]], axis=0)
        second = jnp.concatenate([lower[side][rim:tile] + upper[side][rim + tile:], lower[side][tile:rim + tile]], axis=0)
        tiles_out[0, side] = flatten(first).astype(jnp.bfloat16)
        tiles_out[1, side] = flatten(second).astype(jnp.bfloat16)
    start("fx", tiles_out.at[1 - x, c], tiles_in.at[q], (g, rx, c), None, fold_base + q)
    start("fd", tiles_out.at[1 - x, other], tiles_in.at[q], (g, rx, other), None, fold_base + q)
    start("fc", tiles_out.at[x, other], tiles_in.at[q], to_core, None, fold_base + q)
    tiles_in[q] = tiles_out[x, c]

    flush(later - early)
    for k in (1, 2, 3):
        out_to_core(k)
    arrived("oc", wo_all.at[r, other])
    arrived("oxf", wo_all.at[rx, other])
    for k in (1, 2, 3):
        arrived(f"oc{k}", wo_all.at[2 * away[k] + x, other])
        arrived(f"om{k}", wo_all.at[2 * away[k] + 1 - x, other])

    for at in (2 * x + other, 2 * (1 - x) + c, 2 * (1 - x) + other):
        arrived("fc", tiles_in.at[at], None, fold_base + at)
    for at in range(team):
        arrived("fc", rims_in.at[at], outside, rim_base + at)

    sums = []
    for at in range(team):
        edge = rims_in[at].astype(jnp.float32)
        edge = jnp.concatenate([jnp.where(x == 0, edge, 0.0), jnp.where(x == 1, edge, 0.0)], axis=0)
        sums.append((tiles_in[at].astype(jnp.float32) + edge)[:, :part])
    merged = jnp.concatenate(sums, axis=1).astype(jnp.bfloat16)
    result = base[...] + lax.dot_general(
        merged, wo_all[...].reshape(width, hd), (((1,), (1,)), ((), ())), preferred_element_type=jnp.float32,
    )
    result = result / jnp.maximum(denom, FLOOR)
    out_ref[...] = result.reshape(tile, tile, width).astype(out_ref.dtype)

    flush(len(pending))

    @pl.when(has_above)
    def _():
        for item in count_up:
            item.wait_send()

    @pl.when(has_below)
    def _():
        for item in count_down:
            item.wait_send()


def fused(rows, embeddings, pos_embed, ln_gain, ln_bias, w_qkv, b_qkv, w_out, b_out, valid):
    tile, _, width = embeddings.shape
    win, rim = 2 * tile, tile // 2
    tok = win * win
    shard, qkv = w_qkv.shape
    hd = w_out.shape[1]
    team = 4
    packed = 4 * LANES
    bf16, f32 = jnp.bfloat16, jnp.float32
    vmem = pl.BlockSpec(memory_space=pltpu.VMEM)
    return pl.pallas_call(
        functools.partial(kernel, rows),
        out_shape=jax.ShapeDtypeStruct(embeddings.shape, bf16),
        in_specs=[pl.BlockSpec(memory_space=pltpu.HBM)] * 9,
        out_specs=vmem,
        scratch_shapes=[
            pltpu.VMEM((tok, width), bf16),
            pltpu.VMEM((width,), f32),
            pltpu.VMEM((width,), f32),
            pltpu.VMEM((qkv,), f32),
            pltpu.VMEM((width,), f32),
            pltpu.VMEM((shard, qkv), bf16),
            pltpu.VMEM((2, 2 * tile + 2 * rim, tile, width), bf16),
            pltpu.VMEM((6, 1, 1, tok), jnp.int32),
            pltpu.VMEM((team, shard, packed), bf16),
            pltpu.VMEM((rows, 2, shard, packed), bf16),
            pltpu.VMEM((rows, 2, shard, hd), bf16),
            pltpu.VMEM((team, tok, width), bf16),
            pltpu.VMEM((win, win, width), f32),
            pltpu.VMEM((tile * tile, width), f32),
            pltpu.VMEM((tok, 16), f32),
            pltpu.VMEM((2, 2, tile * tile, 2 * LANES), bf16),
            pltpu.VMEM((team, tile * tile, 2 * LANES), bf16),
            pltpu.VMEM((2, 2, rim * tile, 2 * LANES), bf16),
            pltpu.VMEM((team, rim * tile, 2 * LANES), bf16),
            pltpu.SemaphoreType.DMA((128,)),
            pltpu.SemaphoreType.DMA((128,)),
            pltpu.SemaphoreType.DMA((10,)),
            pltpu.VMEM((team, tok, packed), f32),
        ],
        compiler_params=pltpu.CompilerParams(
            collective_id=0, has_side_effects=True, vmem_limit_bytes=60000000
        ),
    )(
        embeddings, pos_embed, ln_gain, ln_bias, w_qkv, b_qkv, w_out, b_out, valid
    )


def shifted(value, axis, steps):
    count = lax.axis_size(axis)
    initial, last = (max(0, -steps), min(count, count - steps))
    return lax.ppermute(value, axis, [(source, source + steps) for source in range(initial, last)])


def extended(block, sides, width):
    for axis, dim in sides:
        count = lax.axis_size(axis)
        forward = [(i, i + 1) for i in range(count - 1)]
        backward = [(target, source) for source, target in forward]
        low = lax.ppermute(
            lax.slice_in_dim(block, block.shape[dim] - width, None, axis=dim), axis, forward
        )
        high = lax.ppermute(lax.slice_in_dim(block, 0, width, axis=dim), axis, backward)
        block = jnp.concatenate([low, block, high], axis=dim)
    return block


def layer_norm(inputs, ln_gain, ln_bias):
    centred = inputs - jnp.mean(inputs, axis=-1, keepdims=True)
    variance = jnp.mean(centred * centred, axis=-1, keepdims=True)
    return centred * lax.rsqrt(variance + EPSILON) * ln_gain + ln_bias


def gauss_table(win):
    offsets = jnp.arange(win, dtype=jnp.float32) - (win - 1) / 2.0
    squared = offsets[:, None] * offsets[:, None] + offsets[None, :] * offsets[None, :]
    return jnp.exp(-squared / (2.0 * SPREAD * SPREAD))


def attend(projected):
    rows_count = projected.shape[0]
    width = projected.shape[1] // 3
    head_size = width // HEADS
    queries = projected[:, :width].reshape(rows_count, HEADS, head_size)
    keys = projected[:, width : 2 * width].reshape(rows_count, HEADS, head_size)
    values = projected[:, 2 * width :].reshape(rows_count, HEADS, head_size)
    scores = jnp.einsum(
        "qhd,khd->hqk", queries, keys, preferred_element_type=jnp.float32
    ) * head_size ** (-0.5)
    highest = jnp.max(scores, axis=-1, keepdims=True)
    expon = jnp.exp(scores - highest)
    probs = (expon / jnp.sum(expon, axis=-1, keepdims=True)).astype(jnp.bfloat16)
    mixed = jnp.einsum("hqk,khd->qhd", probs, values, preferred_element_type=jnp.float32)
    return mixed.astype(jnp.bfloat16).reshape(rows_count, width)


def fold_rows(numerator, denominator, rim):
    from_next = (
        shifted(numerator[:rim].astype(jnp.bfloat16), "row", -1).astype(jnp.float32),
        shifted(denominator[:rim].astype(jnp.bfloat16), "row", -1).astype(jnp.float32),
    )
    from_prev = (
        shifted(numerator[-rim:].astype(jnp.bfloat16), "row", 1).astype(jnp.float32),
        shifted(denominator[-rim:].astype(jnp.bfloat16), "row", 1).astype(jnp.float32),
    )
    middle_num = numerator[rim:-rim]
    middle_den = denominator[rim:-rim]
    middle_num = middle_num.at[:rim].add(from_prev[0]).at[-rim:].add(from_next[0])
    middle_den = middle_den.at[:rim].add(from_prev[1]).at[-rim:].add(from_next[1])
    return (middle_num, middle_den)


def fold_cols(numerator, denominator, rim):
    from_next = (
        shifted(numerator[:, :rim].astype(jnp.bfloat16), "col", -1).astype(jnp.float32),
        shifted(denominator[:, :rim].astype(jnp.bfloat16), "col", -1).astype(jnp.float32),
    )
    from_prev = (
        shifted(numerator[:, -rim:].astype(jnp.bfloat16), "col", 1).astype(jnp.float32),
        shifted(denominator[:, -rim:].astype(jnp.bfloat16), "col", 1).astype(jnp.float32),
    )
    middle_num = numerator[:, rim:-rim] + jnp.concatenate([from_prev[0], from_next[0]], axis=1)
    middle_den = denominator[:, rim:-rim] + jnp.concatenate([from_prev[1], from_next[1]], axis=1)
    return (middle_num, middle_den)


def body(embeddings, pos_embed, ln_gain, ln_bias, w_qkv, b_qkv, w_out, b_out, valid):
    tile = embeddings.shape[1]
    tile_rows = embeddings.shape[0] // tile
    rim = tile // 2
    win = tile + 2 * rim
    rows_count = win * win
    width_model = embeddings.shape[2]
    window = extended(embeddings, (("row", 0), ("col", 1)), rim)
    stacked = jnp.stack([window], axis=0)
    inputs = stacked.reshape(tile_rows, rows_count, width_model).astype(
        jnp.float32
    ) + pos_embed.astype(jnp.float32)
    inputs = inputs.reshape(tile_rows * rows_count, width_model)
    normed = layer_norm(inputs, ln_gain, ln_bias).astype(jnp.bfloat16)
    projected = jnp.dot(
        normed,
        lax.all_gather(w_qkv, ("row", "col"), axis=0, tiled=True),
        preferred_element_type=jnp.float32,
    )
    projected = (
        (projected + b_qkv).astype(jnp.bfloat16).reshape(tile_rows, rows_count, w_qkv.shape[1])
    )
    attended = jax.vmap(attend)(projected).reshape(tile_rows * rows_count, -1)
    projected_out = lax.dot_general(
        attended,
        lax.all_gather(w_out, ("row", "col"), axis=0, tiled=True),
        (((1,), (1,)), ((), ())),
        preferred_element_type=jnp.float32,
    )
    hidden = inputs + projected_out + b_out
    gauss = gauss_table(win).reshape(1, rows_count)
    weight = gauss * valid.reshape(tile_rows, rows_count).astype(jnp.float32) / 196.0
    contrib = (weight.reshape(tile_rows * rows_count, 1) * hidden).reshape(
        tile_rows, win, win, width_model
    )
    weight_grid = weight.reshape(tile_rows, win, win)
    numerator = jnp.zeros((tile_rows * tile + 2 * rim, win, width_model), jnp.float32)
    denominator = jnp.zeros((tile_rows * tile + 2 * rim, win), jnp.float32)
    numerator = numerator.at[0:win].add(contrib[0])
    denominator = denominator.at[0:win].add(weight_grid[0])
    numerator, denominator = fold_rows(numerator, denominator, rim)
    numerator, denominator = fold_cols(numerator, denominator, rim)
    return (numerator / jnp.maximum(denominator, FLOOR)[:, :, None]).astype(jnp.bfloat16)


def solution(mesh):
    placed = (
        P(("groups", "row"), "col", None),
        P(),
        P(),
        P(),
        P(("row", "col"), None),
        P(),
        P(("row", "col"), None),
        P(),
        P(("groups", "row"), "col", None),
    )
    rows = mesh.shape["row"]

    def run(*arrays):
        embeddings, w_qkv = arrays[0], arrays[4]
        tile = embeddings.shape[1]
        whole_tiles = w_qkv.shape[0] % 16 == 0 and embeddings.shape[0] == tile == 8
        pairs = mesh.shape["groups"] == 2 and mesh.shape["col"] == 2
        if whole_tiles and pairs and rows == 8:
            return fused(rows, *arrays)
        return body(*arrays)

    return jax.shard_map(
        run,
        mesh=mesh,
        in_specs=placed,
        out_specs=P(("groups", "row"), "col", None),
        check_vma=False,
    )
```

```python
import functools

import jax
import jax.numpy as jnp
from jax import lax
from jax.experimental import pallas as pl
from jax.experimental.pallas import tpu as pltpu
from jax.sharding import PartitionSpec as P

HEADS = 8
EPSILON = 1e-06
SPREAD = 4.0
FLOOR = 0.25
LANES = 128
LOG2E = 1.4426950408889634
MESH = pl.DeviceIdType.MESH


def kernel(
    rows,
    emb_ref, pos_hbm, gain_hbm, bias_hbm, wq_ref, bq_hbm, wo_ref, bo_hbm, valid_ref,
    out_ref, pos_ref, gain_ref, bias_ref, bq_ref, bo_ref, wq_own,
    eb, vb, pack, wq_all, wo_all, nrm, posr, base, wcol, tiles_out, tiles_in,
    rims_out, rims_in, send_sems, recv_sems, local_sems, early_qkv,
):
    g, r, c = lax.axis_index("groups"), lax.axis_index("row"), lax.axis_index("col")
    tile, _, width = emb_ref.shape
    rim = tile // 2
    win = 2 * tile
    tok = win * win
    shard, qkv = wq_ref.shape
    hd = wo_ref.shape[1]
    head = hd // HEADS
    team = 4
    part = hd // team
    packed = pack.shape[2]
    x, z = r % 2, r // 2
    planes = rows // 2
    away = {1: z + 1 - 2 * (z % 2), 2: (z + 2) % planes, 3: planes - 1 - z}
    inner = jnp.logical_and(z > 0, z < planes - 1)
    rx, other = r + 1 - 2 * x, 1 - c
    q = 2 * x + c
    above, below = lax.rem(r + rows - 1, rows), lax.rem(r + 1, rows)
    has_above, has_below = r > 0, r < rows - 1
    has_up, has_down = z > 0, z < planes - 1
    outside = jnp.logical_and(has_above, has_below)
    facing = jnp.where(x == 0, above, below)
    to_core, to_y = (g, r, other), (1 - g, r, c)
    core = {0: c, 1: other}

    names = {}
    pending = []
    fold_base, rim_base = 0, team

    def copy(name, src, dst, device, recv=None):
        at = names.setdefault(name, len(names) + 2 * team)
        return pltpu.make_async_remote_copy(
            src_ref=src, dst_ref=dst, send_sem=send_sems.at[at],
            recv_sem=recv_sems.at[at if recv is None else recv],
            device_id=device, device_id_type=MESH,
        )

    def start(name, src, dst, device, when=None, recv=None):
        item = copy(name, src, dst, device, recv)
        pending.append((when, item))
        if when is None:
            item.start()
        else:
            pl.when(when)(item.start)

    def flush(count):
        for when, item in pending[:count]:
            if when is None:
                item.wait_send()
            else:
                pl.when(when)(item.wait_send)
        del pending[:count]

    def arrived(name, dst, when=None, recv=None):
        item = copy(name, dst, dst, to_core, recv)
        if when is None:
            item.wait_recv()
        else:
            pl.when(when)(item.wait_recv)

    own_rows, mate_rows = pl.ds(rim + tile * x, tile), pl.ds(rim + tile * (1 - x), tile)
    top_rows, low_rows = pl.ds(0, rim), pl.ds(rim + 2 * tile, rim)
    locals_ = []
    for src, dst in (
        (wq_ref, wq_own), (pos_hbm, pos_ref), (gain_hbm, gain_ref), (bias_hbm, bias_ref),
        (emb_ref, eb.at[c, own_rows]), (valid_ref, vb.at[1]), (bo_hbm, bo_ref), (bq_hbm, bq_ref),
        (wo_ref, wo_all.at[r, c]),
    ):
        item = pltpu.make_async_copy(src, dst, local_sems.at[len(locals_)])
        item.start()
        locals_.append(item)

    barrier = pltpu.get_barrier_semaphore()

    def greet(*device):
        pl.semaphore_signal(barrier, inc=1, device_id=device, device_id_type=MESH)

    for k in (2, 1):
        greet(g, 2 * away[k] + x, c)
        greet(g, 2 * away[k] + x, other)

    @pl.when(inner)
    def _():
        greet(g, 2 * away[3] + x, c)
        greet(g, 2 * away[3] + x, other)

    @pl.when(outside)
    def _():
        greet(g, facing, c)
        greet(g, facing, other)

    greet(1 - g, rx, c)
    greet(1 - g, r, c)
    greet(g, rx, c)
    greet(g, rx, other)
    greet(g, r, other)

    locals_[0].wait()
    own = wq_own[...].astype(jnp.float32)
    for k in range(team):
        cut = [own[:, t * hd + k * part:t * hd + (k + 1) * part] for t in range(3)]
        for t in range(3):
            pack[k, :, t * LANES:(t + 1) * LANES] = cut[t][:, :LANES].astype(jnp.bfloat16)
        rest = part - LANES
        pieces = [item[:, LANES:] for item in cut] + [jnp.zeros((shard, LANES - 3 * rest), jnp.float32)]
        pack[k, :, 3 * LANES:] = jnp.concatenate(pieces, axis=1).astype(jnp.bfloat16)

    pl.semaphore_wait(
        barrier, 9 + 2 * inner.astype(jnp.int32) + 2 * outside.astype(jnp.int32)
    )

    half_w = packed // 2
    mine = pl.ds(pl.multiple_of(g * half_w, LANES), half_w)
    theirs = pl.ds(pl.multiple_of((1 - g) * half_w, LANES), half_w)

    def wq_at(row, core_at, cols):
        return wq_all.at[row, core_at, :, cols]

    def reach(k):
        return None if k < 3 else inner

    for a in (0, 1):
        start(f"xm{a}", pack.at[2 * (1 - x) + core[a], :, mine], wq_at(r, c, mine), (g, rx, core[a]))
    for k in (1, 2, 3):
        for a in (0, 1):
            start(f"A{k}{a}", pack.at[2 * x + core[a], :, mine], wq_at(r, c, mine),
                  (g, 2 * away[k] + x, core[a]), reach(k))
    start("ec", emb_ref, eb.at[c, own_rows], to_core)
    start("ex", emb_ref, eb.at[c, own_rows], (g, rx, c))

    count_down = [copy("v0", valid_ref, vb.at[0], (g, below, c)), copy("v3", valid_ref, vb.at[3], (g, below, other))]
    count_up = [copy("v2", valid_ref, vb.at[2], (g, above, c)), copy("v5", valid_ref, vb.at[5], (g, above, other))]

    @pl.when(has_below)
    def _():
        for item in count_down:
            item.start()

    @pl.when(has_above)
    def _():
        for item in count_up:
            item.start()

    start("v4", valid_ref, vb.at[4], to_core)
    own_weights = pltpu.make_async_copy(pack.at[q], wq_all.at[r, c], local_sems.at[len(locals_)])
    own_weights.start()

    @pl.when(z == 0)
    def _():
        eb[0, 0:rim] = jnp.zeros((rim, tile, width), eb.dtype)
        eb[1, 0:rim] = jnp.zeros((rim, tile, width), eb.dtype)

    @pl.when(z == planes - 1)
    def _():
        eb[0, rim + 2 * tile:] = jnp.zeros((rim, tile, width), eb.dtype)
        eb[1, rim + 2 * tile:] = jnp.zeros((rim, tile, width), eb.dtype)

    @pl.when(r == 0)
    def _():
        vb[0] = jnp.zeros((1, 1, tok), vb.dtype)
        vb[3] = jnp.zeros((1, 1, tok), vb.dtype)

    @pl.when(r == rows - 1)
    def _():
        vb[2] = jnp.zeros((1, 1, tok), vb.dtype)
        vb[5] = jnp.zeros((1, 1, tok), vb.dtype)

    @pl.when(jnp.logical_not(outside))
    def _():
        rims_in[...] = jnp.zeros(rims_in.shape, rims_in.dtype)

    for item in locals_[1:5]:
        item.wait()
    gain, bias = gain_ref[...].reshape(1, width), bias_ref[...].reshape(1, width)
    per = rim

    def roll_block(block, carry):
        pos = pos_ref[pl.ds(pl.multiple_of(block * per * win, per * win), per * win)]
        pos = pos.astype(jnp.float32).reshape(per, win, width)
        posr[pl.ds(block * per, per)] = pltpu.roll(pos, win - rim, 1)
        return carry

    lax.fori_loop(0, win // per, roll_block, 0)
    place = lax.broadcasted_iota(jnp.int32, (per, tile, 1), 1)

    def norm_block(which, block, side):
        which = which + x * (1 - 2 * which)
        block = block + x * (win // per - 1 - 2 * block)
        at = pl.ds(which * tile + block * per, per)
        rim_ok = jnp.where(side == 0, place, tile - 1 - place) < rim
        left = eb[side, at].astype(jnp.float32)
        right = jnp.where(rim_ok, eb[1 - side, at].astype(jnp.float32), 0.0)
        v = (jnp.concatenate([left, right], axis=1) + posr[pl.ds(block * per, per)]).reshape(per * win, width)
        v = v - jnp.mean(v, axis=-1, keepdims=True)
        variance = jnp.mean(v * v, axis=-1, keepdims=True)
        v = v * lax.rsqrt(variance + EPSILON) * gain + bias
        there = pl.ds(pl.multiple_of(block * per * win, per * win), per * win)
        nrm[2 * which + side, there] = v.astype(jnp.bfloat16)

    def norm_own(n, carry):
        m = n // 2
        norm_block(m // 2, (m + 1) % 3, n % 2)
        return carry

    def norm_mate(n, carry):
        m = n // 2
        norm_block((m + 1) // 2, (m + 2) % 3 + 1, n % 2)
        return carry

    def norm_rims(n, carry):
        norm_block(n // 2, n // 2 * 3, n % 2)
        return carry

    def pair_at(row, cols):
        return wq_all.at[row, :, :, cols]

    def slot(name):
        return names.setdefault(name, len(names) + 2 * team)

    outer_only = jnp.logical_not(inner)

    def from_z(phase, k):
        row = 2 * away[k] + (x if phase == "A" else 1 - x)
        here = pair_at(row, mine)
        if phase == "A" and k == 1:
            for a in (0, 1):
                one = wq_at(row, core[a], mine)
                arrived(f"A1{a}", one)
                start(f"yA1{a}", one, one, to_y)
            return
        if phase == "B" and k > 1:
            for a in (0, 1):
                one = wq_at(row, core[a], mine)
                arrived(f"B{k}{a}", one)
                if k == 2:
                    start(f"fB{a}", one, one, (g, 2 * away[1] + x, c), inner, slot(f"B3{a}"))
                start(f"yB{k}{a}", one, one, to_y)
            return
        if phase == "A" and k == 2:
            for a in (0, 1):
                one = wq_at(row, core[a], mine)
                arrived(f"A2{a}", one)
        else:
            arrived(f"{phase}{k}", here, outer_only if phase == "A" else None)
            if phase == "A":
                for a in (0, 1):
                    arrived(f"A3{a}", wq_at(row, core[a], mine), inner)
        start(f"y{phase}{k}", here, here, to_y)
        if k == 2:
            start(f"f{phase}", here, here, (g, 2 * away[1] + x, c), inner, slot(f"{phase}3"))

    def from_y(phase, k):
        row = 2 * away[k] + (x if phase == "A" else 1 - x)
        if (phase, k) in (("A", 1), ("B", 2), ("B", 3)):
            for a in (0, 1):
                arrived(f"y{phase}{k}{a}", wq_at(row, core[a], theirs))
        else:
            arrived(f"y{phase}{k}", pair_at(row, theirs))

    arrived("ec", eb.at[other, own_rows])
    lax.fori_loop(0, 3, norm_own, 0)

    for a in (0, 1):
        arrived(f"xm{a}", wq_at(rx, core[a], mine))
    given = pair_at(rx, mine)
    gives_down = jnp.logical_and(x == 1, has_down)
    gives_up = jnp.logical_and(x == 0, has_up)
    halves = [wq_at(rx, core[a], mine) for a in (0, 1)]
    for a in (0, 1):
        start(f"B2{a}", halves[a], halves[a], (g, 2 * away[2] + x, c))
    start("B1", given, given, (g, 2 * away[1] + x, c))
    start("ht", emb_ref.at[pl.ds(tile - rim, rim)], eb.at[c, top_rows], (g, lax.rem(r + 2, rows), c), gives_down,
          slot("ht"))
    start("hb", emb_ref.at[pl.ds(0, rim)], eb.at[c, low_rows], (g, lax.rem(r + rows - 2, rows), c), gives_up,
          slot("hb"))
    for a in (0, 1):
        start(f"B3{a}", halves[a], halves[a], (g, 2 * away[3] + x, c), inner)
    for a in (0, 1):
        start(f"xt{a}", pack.at[2 * (1 - x) + core[a], :, theirs], wq_at(r, c, theirs), (g, rx, core[a]))
    start("wc", pack.at[2 * x + other], wq_all.at[r, c], to_core)
    start("ox", wo_ref, wo_all.at[r, c], (g, rx, c))
    start("oc", wo_ref, wo_all.at[r, c], to_core)
    lax.fori_loop(3, 6, norm_own, 0)

    units = hd // LANES
    side_w = units // 2 * LANES
    ring_w = hd - side_w
    ring = pl.ds(pl.multiple_of(g * side_w, LANES), ring_w)
    y_out = pl.ds(pl.multiple_of(g * ring_w, LANES), side_w)
    y_in = pl.ds(pl.multiple_of((1 - g) * ring_w, LANES), side_w)

    def wo_at(row, cols):
        return wo_all.at[row, c, :, cols]


    from_z("A", 1)
    from_z("A", 2)

    arrived("ex", eb.at[c, mate_rows])
    start("exf", eb.at[c, mate_rows], eb.at[c, mate_rows], to_core)
    arrived("v4", vb.at[4])

    @pl.when(has_above)
    def _():
        for item in count_down:
            item.wait_recv()

    @pl.when(has_below)
    def _():
        for item in count_up:
            item.wait_recv()

    for item in locals_[5:]:
        item.wait()
    near_v = [vb[k, 0] for k in range(3)]
    far_v = [vb[k + 3, 0] for k in range(3)]
    mate_near, mate_far = jnp.where(x == 0, near_v[2], near_v[0]), jnp.where(x == 0, far_v[2], far_v[0])
    counts = near_v + far_v
    for i in (0, 1):
        for side in (0, 1):
            same = jnp.where(c == side, near_v[1], far_v[1])
            mate = jnp.where(c == side, mate_near, mate_far)
            counts.append(jnp.where(x == i, same, mate))
    counts = jnp.concatenate(
        [v.astype(jnp.float32) for v in counts] + [jnp.zeros((6, tok), jnp.float32)], axis=0
    ).astype(jnp.bfloat16)
    t_row = lax.broadcasted_iota(jnp.int32, (tok, tok), 0)
    t_col = lax.broadcasted_iota(jnp.int32, (tok, tok), 1)
    base_row = t_row // win * win
    pick = (t_col == base_row + (t_row - base_row + rim) % win).astype(jnp.float32).astype(jnp.bfloat16)
    counts = lax.dot_general(pick, counts, (((1,), (1,)), ((), ())), preferred_element_type=jnp.float32)
    t = lax.broadcasted_iota(jnp.int32, (tok, 1), 0)
    oi = (t // win).astype(jnp.float32) - (win - 1) / 2.0
    oj = ((t % win + rim) % win).astype(jnp.float32) - (win - 1) / 2.0
    gauss = jnp.exp(-(oi * oi + oj * oj) / (2.0 * SPREAD * SPREAD))
    weights = gauss * counts / 196.0
    at_col = lax.broadcasted_iota(jnp.int32, weights.shape, 1) % 2
    at_place = lax.broadcasted_iota(jnp.int32, weights.shape, 0) % win - tile
    kept = jnp.where(at_col == 0, at_place, tile - 1 - at_place) < rim
    wcol[...] = jnp.where(jnp.logical_or(at_place < 0, kept), weights, 0.0)
    grid = weights.reshape(win, win, weights.shape[1])
    near = grid[:, :tile].reshape(win * tile, weights.shape[1])
    far = grid[:, tile:].reshape(win * tile, weights.shape[1])
    u = lax.broadcasted_iota(jnp.int32, (win * tile, 1), 0) % tile
    fold_ok = jnp.where(c == 1, u, tile - 1 - u) < rim
    far = jnp.where(fold_ok, far, 0.0)
    low, high = rim * tile, (rim + tile) * tile
    near0, far0 = near[low:high, 1:2], far[low:high, 4:5]
    near_a = jnp.where(has_above, near[high:, 0:1], 0.0)
    far_a = jnp.where(has_above, far[high:, 3:4], 0.0)
    near_b = jnp.where(has_below, near[:low, 2:3], 0.0)
    far_b = jnp.where(has_below, far[:low, 5:6], 0.0)
    denom = near0 + far0 + jnp.concatenate([near_a + far_a, near_b + far_b], axis=0)

    def flat(lo, hi, a, b):
        return posr[lo:hi, a:b].reshape((hi - lo) * (b - a), width)

    total = denom * (
        eb[c, own_rows].astype(jnp.float32).reshape(tile * tile, width)
        + bo_ref[...].reshape(1, width)
    )
    total += near0 * flat(rim, rim + tile, 0, tile) + far0 * flat(rim, rim + tile, tile, win)
    base[...] = total
    base[0:low] += near_a * flat(rim + tile, win, 0, tile) + far_a * flat(rim + tile, win, tile, win)
    base[low:] += near_b * flat(0, rim, 0, tile) + far_b * flat(0, rim, tile, win)

    for k in (2, 1,):
        start(f"o{k}", wo_ref.at[:, ring], wo_at(r, ring), (g, 2 * away[k] + x, c), outer_only)

    early = len(pending)
    from_z("B", 2)
    for k in (2, 1, 3):
        start(f"o{k}", wo_ref.at[:, ring], wo_at(r, ring), (g, 2 * away[k] + x, c), inner)
    from_z("B", 1)
    arrived("exf", eb.at[other, mate_rows])
    lax.fori_loop(0, 6, norm_mate, 0)
    for name, place_at, exists, direct in (("ht", top_rows, has_up, x == 1), ("hb", low_rows, has_down, x == 0)):
        here = eb.at[c, place_at]
        first = jnp.logical_and(exists, direct)
        arrived(name, here, first)
        start(f"{name}x", here, here, (g, rx, c), first)
        start(f"{name}f", here, here, to_core, first)
    from_z("A", 3)
    from_z("B", 3)
    later = len(pending)
    arrived("ox", wo_at(rx, pl.ds(0, hd)))
    start("oxf", wo_all.at[rx, c], wo_all.at[rx, c], to_core)

    def out_from_z(k):
        here, side = wo_at(2 * away[k] + x, ring), wo_at(2 * away[k] + x, y_out)
        arrived(f"o{k}", here)
        if k == 2:
            start("of", here, here, (g, 2 * away[1] + x, c), inner, names.setdefault("o3", len(names) + 2 * team))
        start(f"ox{k}", here, here, (g, rx, c))
        start(f"oy{k}", side, side, to_y)
        start(f"od{k}", side, side, (1 - g, rx, c))

    def out_to_core(k):
        row, mate = 2 * away[k] + x, 2 * away[k] + 1 - x
        arrived(f"oy{k}", wo_at(row, y_in))
        start(f"oc{k}", wo_all.at[row, c], wo_all.at[row, c], to_core)
        arrived(f"ox{k}", wo_at(mate, ring))
        arrived(f"od{k}", wo_at(mate, y_in))
        start(f"om{k}", wo_all.at[mate, c], wo_all.at[mate, c], to_core)

    out_from_z(2)
    out_from_z(1)
    for name, place_at, exists, direct in (("ht", top_rows, has_up, x == 1), ("hb", low_rows, has_down, x == 0)):
        here = eb.at[c, place_at]
        second = jnp.logical_and(exists, jnp.logical_not(direct))
        arrived(f"{name}x", here, second)
        start(f"{name}g", here, here, to_core, second, slot(f"{name}f"))
    for name, place_at, when in (("ht", top_rows, has_up), ("hb", low_rows, has_down)):
        arrived(f"{name}f", eb.at[other, place_at], when)
    lax.fori_loop(0, 4, norm_rims, 0)
    flush(early)
    own_weights.wait()
    arrived("wc", wq_all.at[r, other])
    for a in (0, 1):
        arrived(f"xt{a}", wq_at(rx, core[a], theirs))
    for phase in ("A", "B"):
        from_y(phase, 1)

    b_own = bq_ref[...].reshape(1, qkv)
    b_parts = []
    for k in range(team):
        cut = [b_own[:, t * hd + k * part:t * hd + (k + 1) * part] for t in range(3)]
        rest = part - LANES
        b_parts.append(jnp.concatenate(
            [item[:, :LANES] for item in cut] + [item[:, LANES:] for item in cut]
            + [jnp.zeros((1, LANES - 3 * rest), jnp.float32)], axis=1))
    b_mine = jnp.where(x == 0, jnp.where(c == 0, b_parts[0], b_parts[1]), jnp.where(c == 0, b_parts[2], b_parts[3]))

    deep = width // 2

    def part_dot(w, which):
        at = pl.ds(pl.multiple_of(which * deep, LANES), deep)
        rows_at = pl.ds(which * (rows // 2), rows // 2)
        return jnp.dot(nrm[w, :, at], wq_all[rows_at].reshape(deep, packed), preferred_element_type=jnp.float32)

    def near_part(w, carry):
        early_qkv[w] = part_dot(w, z // 2) + b_mine
        return carry

    lax.fori_loop(0, team, near_part, 0)
    for phase in ("A", "B"):
        for k in (2, 3):
            from_y(phase, k)


    lane = lax.broadcasted_iota(jnp.int32, (1, 2 * LANES), 1)
    rest = part - LANES

    def attend(w):
        proj = part_dot(w, 1 - z // 2) + early_qkv[w]
        tail = proj[:, 3 * LANES:]
        queries = jnp.concatenate([proj[:, :LANES], tail], axis=1)
        keys = jnp.concatenate([proj[:, LANES:2 * LANES], pltpu.roll(tail, LANES - rest, 1)], axis=1)
        values = jnp.concatenate([proj[:, 2 * LANES:3 * LANES], pltpu.roll(tail, LANES - 2 * rest, 1)], axis=1)
        keys, values = keys.astype(jnp.bfloat16), values.astype(jnp.bfloat16)
        outs = []
        for h in range(HEADS // team):
            inside = jnp.logical_and(lane >= h * head, lane < (h + 1) * head)
            used = -(-(h + 1) * head // LANES) * LANES
            chosen = jnp.where(inside, queries, 0.0).astype(jnp.bfloat16)
            scores = lax.dot_general(
                chosen[:, :used], keys[:, :used], (((1,), (1,)), ((), ())), preferred_element_type=jnp.float32
            )
            expon = jnp.exp2((scores - jnp.max(scores, axis=-1, keepdims=True)) * (head ** (-0.5) * LOG2E))
            inverse = 1.0 / jnp.sum(expon, axis=-1, keepdims=True)
            outs.append(jnp.dot(expon.astype(jnp.bfloat16), values, preferred_element_type=jnp.float32) * inverse)
        mixed = jnp.where(lane < head, outs[0], jnp.where(lane < part, outs[1], 0.0))
        mixed = mixed.astype(jnp.bfloat16).astype(jnp.float32) * wcol[:, 6 + w:7 + w]
        return mixed.reshape(win, win, 2 * LANES)

    def flatten(value):
        return value.reshape(value.shape[0] * tile, 2 * LANES)

    def both(i):
        left, right = attend(2 * i), attend(2 * i + 1)
        return [left[:, :tile] + right[:, tile:], right[:, :tile] + left[:, tile:]]

    out_from_z(3)
    upper = both(0)
    for side in (0, 1):
        rims_out[0, side] = flatten(upper[side][:rim]).astype(jnp.bfloat16)
    for side in (0, 1):
        start(f"rt{side}", rims_out.at[0, side], rims_in.at[q], (g, lax.rem(2 * z + rows - 1, rows), side), has_up,
              rim_base + q)
    lower = both(1)
    for side in (0, 1):
        rims_out[1, side] = flatten(lower[side][rim + tile:]).astype(jnp.bfloat16)
    for side in (0, 1):
        start(f"rb{side}", rims_out.at[1, side], rims_in.at[q], (g, lax.rem(2 * z + 2, rows), side), has_down,
              rim_base + q)
    for side in (0, 1):
        first = jnp.concatenate([upper[side][rim:tile], upper[side][tile:rim + tile] + lower[side][:rim]], axis=0)
        second = jnp.concatenate([lower[side][rim:tile] + upper[side][rim + tile:], lower[side][tile:rim + tile]], axis=0)
        tiles_out[0, side] = flatten(first).astype(jnp.bfloat16)
        tiles_out[1, side] = flatten(second).astype(jnp.bfloat16)
    start("fx", tiles_out.at[1 - x, c], tiles_in.at[q], (g, rx, c), None, fold_base + q)
    start("fd", tiles_out.at[1 - x, other], tiles_in.at[q], (g, rx, other), None, fold_base + q)
    start("fc", tiles_out.at[x, other], tiles_in.at[q], to_core, None, fold_base + q)
    tiles_in[q] = tiles_out[x, c]

    flush(later - early)
    for k in (1, 2, 3):
        out_to_core(k)
    arrived("oc", wo_all.at[r, other])
    arrived("oxf", wo_all.at[rx, other])
    for k in (1, 2, 3):
        arrived(f"oc{k}", wo_all.at[2 * away[k] + x, other])
        arrived(f"om{k}", wo_all.at[2 * away[k] + 1 - x, other])

    for at in (2 * x + other, 2 * (1 - x) + c, 2 * (1 - x) + other):
        arrived("fc", tiles_in.at[at], None, fold_base + at)
    for at in range(team):
        arrived("fc", rims_in.at[at], outside, rim_base + at)

    sums = []
    for at in range(team):
        edge = rims_in[at].astype(jnp.float32)
        edge = jnp.concatenate([jnp.where(x == 0, edge, 0.0), jnp.where(x == 1, edge, 0.0)], axis=0)
        sums.append((tiles_in[at].astype(jnp.float32) + edge)[:, :part])
    merged = jnp.concatenate(sums, axis=1).astype(jnp.bfloat16)
    result = base[...] + lax.dot_general(
        merged, wo_all[...].reshape(width, hd), (((1,), (1,)), ((), ())), preferred_element_type=jnp.float32,
    )
    result = result / jnp.maximum(denom, FLOOR)
    out_ref[...] = result.reshape(tile, tile, width).astype(out_ref.dtype)

    flush(len(pending))

    @pl.when(has_above)
    def _():
        for item in count_up:
            item.wait_send()

    @pl.when(has_below)
    def _():
        for item in count_down:
            item.wait_send()


def fused(rows, embeddings, pos_embed, ln_gain, ln_bias, w_qkv, b_qkv, w_out, b_out, valid):
    tile, _, width = embeddings.shape
    win, rim = 2 * tile, tile // 2
    tok = win * win
    shard, qkv = w_qkv.shape
    hd = w_out.shape[1]
    team = 4
    packed = 4 * LANES
    bf16, f32 = jnp.bfloat16, jnp.float32
    vmem = pl.BlockSpec(memory_space=pltpu.VMEM)
    return pl.pallas_call(
        functools.partial(kernel, rows),
        out_shape=jax.ShapeDtypeStruct(embeddings.shape, bf16),
        in_specs=[pl.BlockSpec(memory_space=pltpu.HBM)] * 9,
        out_specs=vmem,
        scratch_shapes=[
            pltpu.VMEM((tok, width), bf16),
            pltpu.VMEM((width,), f32),
            pltpu.VMEM((width,), f32),
            pltpu.VMEM((qkv,), f32),
            pltpu.VMEM((width,), f32),
            pltpu.VMEM((shard, qkv), bf16),
            pltpu.VMEM((2, 2 * tile + 2 * rim, tile, width), bf16),
            pltpu.VMEM((6, 1, 1, tok), jnp.int32),
            pltpu.VMEM((team, shard, packed), bf16),
            pltpu.VMEM((rows, 2, shard, packed), bf16),
            pltpu.VMEM((rows, 2, shard, hd), bf16),
            pltpu.VMEM((team, tok, width), bf16),
            pltpu.VMEM((win, win, width), f32),
            pltpu.VMEM((tile * tile, width), f32),
            pltpu.VMEM((tok, 16), f32),
            pltpu.VMEM((2, 2, tile * tile, 2 * LANES), bf16),
            pltpu.VMEM((team, tile * tile, 2 * LANES), bf16),
            pltpu.VMEM((2, 2, rim * tile, 2 * LANES), bf16),
            pltpu.VMEM((team, rim * tile, 2 * LANES), bf16),
            pltpu.SemaphoreType.DMA((128,)),
            pltpu.SemaphoreType.DMA((128,)),
            pltpu.SemaphoreType.DMA((10,)),
            pltpu.VMEM((team, tok, packed), f32),
        ],
        compiler_params=pltpu.CompilerParams(
            collective_id=0, has_side_effects=True, vmem_limit_bytes=60000000
        ),
    )(
        embeddings, pos_embed, ln_gain, ln_bias, w_qkv, b_qkv, w_out, b_out, valid
    )


def shifted(value, axis, steps):
    count = lax.axis_size(axis)
    initial, last = (max(0, -steps), min(count, count - steps))
    return lax.ppermute(value, axis, [(source, source + steps) for source in range(initial, last)])


def extended(block, sides, width):
    for axis, dim in sides:
        count = lax.axis_size(axis)
        forward = [(i, i + 1) for i in range(count - 1)]
        backward = [(target, source) for source, target in forward]
        low = lax.ppermute(
            lax.slice_in_dim(block, block.shape[dim] - width, None, axis=dim), axis, forward
        )
        high = lax.ppermute(lax.slice_in_dim(block, 0, width, axis=dim), axis, backward)
        block = jnp.concatenate([low, block, high], axis=dim)
    return block


def layer_norm(inputs, ln_gain, ln_bias):
    centred = inputs - jnp.mean(inputs, axis=-1, keepdims=True)
    variance = jnp.mean(centred * centred, axis=-1, keepdims=True)
    return centred * lax.rsqrt(variance + EPSILON) * ln_gain + ln_bias


def gauss_table(win):
    offsets = jnp.arange(win, dtype=jnp.float32) - (win - 1) / 2.0
    squared = offsets[:, None] * offsets[:, None] + offsets[None, :] * offsets[None, :]
    return jnp.exp(-squared / (2.0 * SPREAD * SPREAD))


def attend(projected):
    rows_count = projected.shape[0]
    width = projected.shape[1] // 3
    head_size = width // HEADS
    queries = projected[:, :width].reshape(rows_count, HEADS, head_size)
    keys = projected[:, width : 2 * width].reshape(rows_count, HEADS, head_size)
    values = projected[:, 2 * width :].reshape(rows_count, HEADS, head_size)
    scores = jnp.einsum(
        "qhd,khd->hqk", queries, keys, preferred_element_type=jnp.float32
    ) * head_size ** (-0.5)
    highest = jnp.max(scores, axis=-1, keepdims=True)
    expon = jnp.exp(scores - highest)
    probs = (expon / jnp.sum(expon, axis=-1, keepdims=True)).astype(jnp.bfloat16)
    mixed = jnp.einsum("hqk,khd->qhd", probs, values, preferred_element_type=jnp.float32)
    return mixed.astype(jnp.bfloat16).reshape(rows_count, width)


def fold_rows(numerator, denominator, rim):
    from_next = (
        shifted(numerator[:rim].astype(jnp.bfloat16), "row", -1).astype(jnp.float32),
        shifted(denominator[:rim].astype(jnp.bfloat16), "row", -1).astype(jnp.float32),
    )
    from_prev = (
        shifted(numerator[-rim:].astype(jnp.bfloat16), "row", 1).astype(jnp.float32),
        shifted(denominator[-rim:].astype(jnp.bfloat16), "row", 1).astype(jnp.float32),
    )
    middle_num = numerator[rim:-rim]
    middle_den = denominator[rim:-rim]
    middle_num = middle_num.at[:rim].add(from_prev[0]).at[-rim:].add(from_next[0])
    middle_den = middle_den.at[:rim].add(from_prev[1]).at[-rim:].add(from_next[1])
    return (middle_num, middle_den)


def fold_cols(numerator, denominator, rim):
    from_next = (
        shifted(numerator[:, :rim].astype(jnp.bfloat16), "col", -1).astype(jnp.float32),
        shifted(denominator[:, :rim].astype(jnp.bfloat16), "col", -1).astype(jnp.float32),
    )
    from_prev = (
        shifted(numerator[:, -rim:].astype(jnp.bfloat16), "col", 1).astype(jnp.float32),
        shifted(denominator[:, -rim:].astype(jnp.bfloat16), "col", 1).astype(jnp.float32),
    )
    middle_num = numerator[:, rim:-rim] + jnp.concatenate([from_prev[0], from_next[0]], axis=1)
    middle_den = denominator[:, rim:-rim] + jnp.concatenate([from_prev[1], from_next[1]], axis=1)
    return (middle_num, middle_den)


def body(embeddings, pos_embed, ln_gain, ln_bias, w_qkv, b_qkv, w_out, b_out, valid):
    tile = embeddings.shape[1]
    tile_rows = embeddings.shape[0] // tile
    rim = tile // 2
    win = tile + 2 * rim
    rows_count = win * win
    width_model = embeddings.shape[2]
    window = extended(embeddings, (("row", 0), ("col", 1)), rim)
    stacked = jnp.stack([window], axis=0)
    inputs = stacked.reshape(tile_rows, rows_count, width_model).astype(
        jnp.float32
    ) + pos_embed.astype(jnp.float32)
    inputs = inputs.reshape(tile_rows * rows_count, width_model)
    normed = layer_norm(inputs, ln_gain, ln_bias).astype(jnp.bfloat16)
    projected = jnp.dot(
        normed,
        lax.all_gather(w_qkv, ("row", "col"), axis=0, tiled=True),
        preferred_element_type=jnp.float32,
    )
    projected = (
        (projected + b_qkv).astype(jnp.bfloat16).reshape(tile_rows, rows_count, w_qkv.shape[1])
    )
    attended = jax.vmap(attend)(projected).reshape(tile_rows * rows_count, -1)
    projected_out = lax.dot_general(
        attended,
        lax.all_gather(w_out, ("row", "col"), axis=0, tiled=True),
        (((1,), (1,)), ((), ())),
        preferred_element_type=jnp.float32,
    )
    hidden = inputs + projected_out + b_out
    gauss = gauss_table(win).reshape(1, rows_count)
    weight = gauss * valid.reshape(tile_rows, rows_count).astype(jnp.float32) / 196.0
    contrib = (weight.reshape(tile_rows * rows_count, 1) * hidden).reshape(
        tile_rows, win, win, width_model
    )
    weight_grid = weight.reshape(tile_rows, win, win)
    numerator = jnp.zeros((tile_rows * tile + 2 * rim, win, width_model), jnp.float32)
    denominator = jnp.zeros((tile_rows * tile + 2 * rim, win), jnp.float32)
    numerator = numerator.at[0:win].add(contrib[0])
    denominator = denominator.at[0:win].add(weight_grid[0])
    numerator, denominator = fold_rows(numerator, denominator, rim)
    numerator, denominator = fold_cols(numerator, denominator, rim)
    return (numerator / jnp.maximum(denominator, FLOOR)[:, :, None]).astype(jnp.bfloat16)


def solution(mesh):
    placed = (
        P(("groups", "row"), "col", None),
        P(),
        P(),
        P(),
        P(("row", "col"), None),
        P(),
        P(("row", "col"), None),
        P(),
        P(("groups", "row"), "col", None),
    )
    rows = mesh.shape["row"]

    def run(*arrays):
        embeddings, w_qkv = arrays[0], arrays[4]
        tile = embeddings.shape[1]
        whole_tiles = w_qkv.shape[0] % 16 == 0 and embeddings.shape[0] == tile == 8
        pairs = mesh.shape["groups"] == 2 and mesh.shape["col"] == 2
        if whole_tiles and pairs and rows == 8:
            return fused(rows, *arrays)
        return body(*arrays)

    return jax.shard_map(
        run,
        mesh=mesh,
        in_specs=placed,
        out_specs=P(("groups", "row"), "col", None),
        check_vma=False,
    )
```
